32 devices in a mesh: gx: 4 (over y, x), gy: 8 (over z, core).
Axes of the slice: x: 2, y: 2, z: 4, core: 2. Of those that a mesh axis runs over, the one named last changes fastest.
Arguments:
- velocity: float32 [3, 32, 128, 256], P(None, 'gx', 'gy'), may hold values from -6 to 6
- pressure: float32 [32, 128, 256], P('gx', 'gy'), may hold values from -4 to 4
- part_cell: int32 [4, 8, 8, 512], P('gx', 'gy'), may hold values from 0 to 32767
- part_count: int32 [4, 8, 8], P('gx', 'gy'), may hold values from 1 to 512, as said below
- grain_velocities: float32 [4, 8, 8, 3, 512], P('gx', 'gy'), may hold values from -6 to 6
- part_vol: float32 [4, 8, 8, 512], P('gx', 'gy'), may hold values from 0.05 to 0.3
Outputs:
- velocity_out: float32 [3, 32, 128, 256], P(None, 'gx', 'gy')
- pressure_out: float32 [32, 128, 256], P('gx', 'gy')
- drag: float32 [4, 8, 8, 3, 512], P('gx', 'gy')
The draws below stay inside these ranges and needn't reach their ends.
Inputs may be any that keep to these rules, and one draw needn't show every extreme that they name: Every DEM owner (a, b) has at least one c with part_count[a, b, c] equal to 512.
All inputs are finite; a program needn't handle non-finite values.
Results may differ from the reference program's by a relative error of at most 0.00002.
Values sent between devices are 32-bit elements; how exact they have to be, the bound alone decides.
A program may use at most 128 MiB of HBM per device.

```python
import jax
import jax.numpy as jnp

CX = 8
CY = 16
NZ = 256
SLOT_CAPACITY = 512
STEPS = 2
SWEEPS = 4
NX = 32
NY = 128
CELLS = 32768
N_GX = 4
N_GY = 8


def draw_part_count(key, part):
    first, second = jax.random.split(key)
    base = jax.random.randint(first, (N_GX, N_GY, N_GY), 1, SLOT_CAPACITY + 1)
    chosen = jax.random.randint(second, (N_GX, N_GY, 1), 0, N_GY)
    hit = jnp.arange(N_GY, dtype=jnp.int32)[None, None, :] == chosen
    return jnp.where(hit, SLOT_CAPACITY, base).astype(jnp.int32)


def set_ends(array, stream_key, low, largest):
    place = [jax.random.randint(jax.random.fold_in(stream_key, axis), (), 0, length) for axis, length in enumerate(array.shape)]
    longest = array.shape.index(max(array.shape))
    beside = place[:longest] + [(place[longest] + 1) % array.shape[longest]] + place[longest + 1:]
    return array.at[tuple(place)].set(low).at[tuple(beside)].set(largest)


def levels(key, extent, shards, least, high):
    factor_of = 1.0
    for dim, shards_of in shards:
        steps = jax.random.uniform(jax.random.fold_in(jax.random.fold_in(key, 6), dim), (shards_of,), jnp.float32, least / len(shards), high / len(shards))
        factor_of = factor_of * jnp.repeat(jnp.exp(steps), extent[dim] // shards_of).reshape((-1,) + (1,) * (len(extent) - 1 - dim))
    return factor_of


def scatter_about(rng, extent, deviation, bound, pieces=(), kind=jnp.bfloat16):
    level = levels(rng, extent, pieces, -0.22, 0.18) if pieces else 1.0
    result = jax.random.normal(rng, extent, jnp.float32) * deviation * level
    return jnp.minimum(jnp.maximum(result, -bound), bound).astype(kind)


def setup_inputs(seed: int = 0) -> dict:
    key_of = jax.random.split(jax.random.key(seed), 7)
    velocity = scatter_about(key_of[0], (3, NX, NY, NZ), 1.0, 6.0, ((1, 4), (2, 8)), jnp.float32)
    pressure = scatter_about(key_of[1], (NX, NY, NZ), 0.5, 4.0, ((0, 4), (1, 8)), jnp.float32)
    part_cell = set_ends(jax.random.randint(key_of[2], (N_GX, N_GY, N_GY, SLOT_CAPACITY), 0, CELLS), jax.random.fold_in(key_of[2], 1), 0, CELLS - 1).astype(jnp.int32)
    part_count = draw_part_count(jax.random.fold_in(key_of[6], 71), 0)
    grain_velocities = scatter_about(key_of[4], (N_GX, N_GY, N_GY, 3, SLOT_CAPACITY), 1.0, 6.0, ((0, 4), (1, 8)), jnp.float32)
    part_vol = jnp.clip(0.05 + 0.25 * jax.random.uniform(key_of[5], (N_GX, N_GY, N_GY, SLOT_CAPACITY), jnp.float32) ** levels(key_of[5], (N_GX, N_GY, N_GY, SLOT_CAPACITY), ((0, 4), (1, 8)), -0.2, 0.2), 0.05, 0.3)
    return {"velocity": velocity, "pressure": pressure, "part_cell": part_cell, "part_count": part_count, "grain_velocities": grain_velocities, "part_vol": part_vol}


drag_coefficient = 2.0
time_step = 0.25
viscosity = 0.2
eps_floor = 0.4


def cell_faces(padded):
    return [padded[..., 2:, 1:-1, 1:-1], padded[..., :-2, 1:-1, 1:-1],
            padded[..., 1:-1, 2:, 1:-1], padded[..., 1:-1, :-2, 1:-1],
            padded[..., 1:-1, 1:-1, 2:], padded[..., 1:-1, 1:-1, :-2]]


def padded_mesh_cells(field):
    widths = [(0, 0)] * (field.ndim - 3) + [(1, 1), (1, 1), (1, 1)]
    return jnp.pad(field, widths)


def laplacian_operator(padded_velocity_field, flow_velocity, padded_voidage, porous_medium):
    near = cell_faces(padded_velocity_field)
    kernel_weights = cell_faces(padded_voidage)
    total = jnp.zeros_like(flow_velocity)
    for index in range(6):
        total = total + 0.5 * (porous_medium + kernel_weights[index]) * (near[index] - flow_velocity) / porous_medium
    return total


def divergence(flux_pad):
    near = cell_faces(flux_pad)
    return (0.5 / time_step) * (((near[0][0] - near[1][0]) + (near[2][1] - near[3][1])) + (near[4][2] - near[5][2]))


def relaxation_terms(padded_pressure_field, padded_voidage):
    central_value = padded_voidage[1:-1, 1:-1, 1:-1]
    near = cell_faces(padded_pressure_field)
    kernel_weights = cell_faces(padded_voidage)
    numerator = jnp.zeros_like(central_value)
    denominator = jnp.zeros_like(central_value)
    for index in range(6):
        weight = 0.5 * (central_value + kernel_weights[index])
        numerator = numerator + weight * near[index]
        denominator = denominator + weight
    return numerator, denominator


def gradient(padded_pressure_field):
    near = cell_faces(padded_pressure_field)
    return jnp.stack([0.5 * (near[0] - near[1]), 0.5 * (near[2] - near[3]), 0.5 * (near[4] - near[5])])


def to_grid(flat):
    return flat.reshape(N_GX, N_GY, CX, CY, NZ).transpose(0, 2, 1, 3, 4).reshape(NX, NY, NZ)


def to_grid3(flat):
    return flat.reshape(N_GX, N_GY, CX, CY, NZ, 3).transpose(5, 0, 2, 1, 3, 4).reshape(3, NX, NY, NZ)


def gather_from_mesh(grid):
    return grid.reshape(N_GX, CX, N_GY, CY, NZ).transpose(0, 2, 1, 3, 4).reshape(-1)


def from_grid3(grid):
    return grid.reshape(3, N_GX, CX, N_GY, CY, NZ).transpose(0, 1, 3, 2, 4, 5).reshape(3, -1)


def reference(velocity, pressure, part_cell, part_count, grain_velocities, part_vol):
    slots = jnp.arange(SLOT_CAPACITY, dtype=jnp.int32)
    alive = slots[None, None, None, :] < part_count[..., None]
    grain_volume = jnp.where(alive, part_vol, jnp.float32(0.0))
    owner = (jnp.arange(N_GX, dtype=jnp.int32)[:, None, None, None] * N_GY
             + jnp.arange(N_GY, dtype=jnp.int32)[None, None, :, None])
    target_field = (owner * CELLS + part_cell).astype(jnp.int32).reshape(-1)
    total = N_GX * N_GY * CELLS
    solid_flat = jax.ops.segment_sum(grain_volume.reshape(-1), target_field, num_segments=total)
    carried = jnp.moveaxis(grain_volume[..., None, :] * grain_velocities, 3, 4).reshape(-1, 3)
    flux_flat = jax.ops.segment_sum(carried, target_field, num_segments=total)
    solid = to_grid(solid_flat)
    mass_flux = to_grid3(flux_flat)
    porous_medium = jnp.maximum(1.0 - solid, eps_floor)
    padded_voidage = padded_mesh_cells(porous_medium)
    for step in range(STEPS):
        spread_to_mesh = laplacian_operator(padded_mesh_cells(velocity), velocity, padded_voidage, porous_medium)
        force = drag_coefficient * (mass_flux - solid * velocity) / porous_medium
        guess = velocity + time_step * (viscosity * spread_to_mesh + force)
        source = divergence(padded_mesh_cells(porous_medium * guess))
        for sweep in range(SWEEPS):
            numerator, denominator = relaxation_terms(padded_mesh_cells(pressure), padded_voidage)
            pressure = (numerator - source) / denominator
        velocity = guess - time_step * gradient(padded_mesh_cells(pressure))
    flat_vel = from_grid3(velocity)
    flattened_voids = gather_from_mesh(porous_medium)
    cell_flow_speed = jnp.moveaxis(flat_vel[:, target_field].reshape(3, N_GX, N_GY, N_GY, SLOT_CAPACITY), 0, 3)
    cell_void_fraction = flattened_voids[target_field].reshape(N_GX, N_GY, N_GY, SLOT_CAPACITY)
    drag = (grain_volume[..., None, :] * drag_coefficient) * (cell_flow_speed - grain_velocities) / cell_void_fraction[..., None, :]
    return velocity, pressure, drag
```

```python
import jax
import jax.numpy as jnp
from jax import lax
from jax.experimental import pallas as pl
from jax.experimental.pallas import tpu as pltpu
from jax.sharding import PartitionSpec as P

STEPS = 2
SWEEPS = 4
DRAG = 2.0
DT = 0.25
VISC = 0.2
FLOOR = 0.4

WX = SWEEPS + 1
WY = 8
ROWS = 5

MESH = pl.DeviceIdType.MESH
CORNERS = ((0, 0), (0, 1), (1, 0), (1, 1))
F32 = jnp.float32
BF16 = jnp.bfloat16


def split(value):
    high = value.astype(BF16).astype(F32)
    return high, value - high


def mate(i, k, n):
    if n & (n - 1):
        return lax.rem(i + k, n)
    bit, flip = 1, 0
    while bit < n:
        flip = flip + bit * ((i // bit + k // bit) % 2)
        bit *= 2
    return flip


def body(n_gx, n_gy, count_ref, vel_hbm, p_hbm, cell_hbm, gv_hbm, vol_hbm,
         vel_out, p_out, drag_out, cell_ref, gv_ref, vol_ref, fetch_sem,
         v1, v2, pin1, pin2, pa, pb, src1, src2, sp, solid, mf, eps, coef, rate, pull,
         guess, flux, dep, pk, rk, dk, rd, ft, corner_out, corner_in, field_send, field_recv, part_send, part_recv):
    bx, by, nz = p_hbm.shape
    ex, ey = bx + 2 * WX, by + 2 * WY
    slots = vol_hbm.shape[-1]
    columns = bx * by
    ix, iy = lax.axis_index("gx"), lax.axis_index("gy")
    has = {("x", 0): ix > 0, ("x", 1): ix < n_gx - 1, ("y", 0): iy > 0, ("y", 1): iy < n_gy - 1}
    peer = {("x", 0): (ix - 1, iy), ("x", 1): (ix + 1, iy), ("y", 0): (ix, iy - 1), ("y", 1): (ix, iy + 1)}
    own_x, own_y = pl.ds(WX, bx), pl.ds(WY, by)

    def to_mate(k):
        return mate(iy, k, n_gy)

    def from_mate(k):
        return to_mate(k) if n_gy & (n_gy - 1) == 0 else lax.rem(iy + n_gy - k, n_gy)

    def beyond(corner):
        return ix + (2 * corner[0] - 1), iy + (2 * corner[1] - 1)

    barrier = pltpu.get_barrier_semaphore()
    for k in range(1, n_gy):
        pl.semaphore_signal(barrier, inc=1, device_id=(ix, to_mate(k)), device_id_type=MESH)
    for side in (0, 1):
        @pl.when(has["x", side])
        def _():
            pl.semaphore_signal(barrier, inc=1, device_id=peer["x", side], device_id_type=MESH)
    for corner in CORNERS:
        @pl.when(has["x", corner[0]] & has["y", corner[1]])
        def _():
            pl.semaphore_signal(barrier, inc=1, device_id=beyond(corner), device_id_type=MESH)

    fetches = [(cell_hbm, cell_ref), (vol_hbm, vol_ref), (gv_hbm, gv_ref)]
    fetches += [(vel_hbm.at[d], v1.at[d, own_x, own_y]) for d in range(3)] + [(p_hbm, pin1.at[own_x, own_y])]
    fetches = [pltpu.make_async_copy(source, landing, fetch_sem.at[n]) for n, (source, landing) in enumerate(fetches)]
    for fetch in fetches:
        fetch.start()

    fields = [v1.at[d] for d in range(3)] + [v2.at[d] for d in range(3)] + [mf.at[d] for d in range(3)]
    fields += [pin1, pin2, src1, src2, solid]
    for side in (0, 1):
        @pl.when(jnp.logical_not(has["x", side]))
        def _():
            for field in fields:
                at = 0 if side == 0 else WX + bx
                field[pl.ds(at, WX)] = jnp.zeros((WX, ey, nz), F32)

        @pl.when(jnp.logical_not(has["y", side]))
        def _():
            for field in fields:
                at = 0 if side == 0 else WY + by
                field[:, pl.ds(at, WY), :] = jnp.zeros((ex, WY, nz), F32)

    for fetch in fetches[:3]:
        fetch.wait()
    slot = lax.broadcasted_iota(jnp.int32, (1, slots), 1)
    for c in range(n_gy):
        pk[c, 0:1, :] = cell_ref[pl.ds(c, 1), :].astype(F32)
        pk[c, 1:2, :] = jnp.where(slot < count_ref[c], vol_ref[pl.ds(c, 1), :], 0.0)
        for d in range(3):
            pk[c, 2 + d:3 + d, :] = gv_ref[d, pl.ds(c, 1), :]

    x_peers = jnp.where(ix > 0, 1, 0) + jnp.where(ix < n_gx - 1, 1, 0)
    y_peers = jnp.where(iy > 0, 1, 0) + jnp.where(iy < n_gy - 1, 1, 0)
    pl.semaphore_wait(barrier, n_gy - 1 + x_peers * (1 + y_peers))

    def particles(k, source, landing, bank):
        return pltpu.make_async_remote_copy(
            src_ref=source, dst_ref=landing, send_sem=part_send.at[bank, k], recv_sem=part_recv.at[bank, k],
            device_id=(ix, to_mate(k)), device_id_type=MESH)

    def outgoing(k):
        return particles(k, pk.at[to_mate(k)], rk.at[iy], 0)

    def incoming(k):
        return particles(k, pk.at[0], rk.at[from_mate(k)], 0)

    for k in range(n_gy - 1, 0, -1):
        outgoing(k).start()
    rk[iy] = pk[iy]

    class Halo:
        def __init__(self, slot, ref, width, rows=0, reach=0, axes="xy", skip=0):
            self.slot, self.ref, self.width, self.span, self.axes, self.skip = slot, ref, width, rows, axes, skip
            self.rows = [(i, j) for i in range(reach) for j in range(reach) if i + j + 2 <= reach]

        def copy(self, index, source, landing, to):
            return pltpu.make_async_remote_copy(
                src_ref=source, dst_ref=landing, send_sem=field_send.at[self.slot, index],
                recv_sem=field_recv.at[self.slot, index], device_id=to, device_id_type=MESH)

        def x_copy(self, side):
            w, skip = self.width, self.skip
            at = skip if side == 0 else bx - w - skip
            source = self.ref.at[pl.ds(WX + at, w), own_y]
            landing = self.ref.at[pl.ds(WX + bx + skip if side == 0 else WX - w - skip, w), own_y]
            return self.copy(side, source, landing, peer["x", side])

        def y_copy(self, side):
            h = self.span
            source = self.ref.at[own_x, pl.ds(WY if side == 0 else WY + by - h, h)]
            landing = self.ref.at[own_x, pl.ds(WY + by if side == 0 else WY - h, h)]
            return self.copy(2 + side, source, landing, peer["y", side])

        def c_copy(self, corner):
            n = 2 * corner[0] + corner[1]
            size = -(-len(self.rows) // 8) * 8
            return self.copy(4 + n, corner_out.at[self.slot, n, pl.ds(0, size)],
                             corner_in.at[self.slot, n, pl.ds(0, size)], beyond(corner))

        def pack(self):
            for corner in CORNERS if self.rows else ():
                for n, (i, j) in enumerate(self.rows):
                    x = WX + (i if corner[0] == 0 else bx - 1 - i)
                    y = WY + (j if corner[1] == 0 else by - 1 - j)
                    corner_out[self.slot, 2 * corner[0] + corner[1], n:n + 1, :] = self.ref[x, y:y + 1, :]

        def each(self, axis, act, flip=False):
            if axis == "c":
                for corner in CORNERS if self.rows else ():
                    near = (1 - corner[0], 1 - corner[1]) if flip else corner

                    @pl.when(has["x", near[0]] & has["y", near[1]])
                    def _():
                        act(self.c_copy(corner), corner)
            elif axis in self.axes:
                for side in (0, 1):
                    @pl.when(has[axis, 1 - side if flip else side])
                    def _():
                        act((self.x_copy if axis == "x" else self.y_copy)(side), None)

        def unpack(self, copy, corner):
            copy.wait_recv()
            for n, (i, j) in enumerate(self.rows):
                x = WX + bx + i if corner[0] == 0 else WX - 1 - i
                y = WY + by + j if corner[1] == 0 else WY - 1 - j
                self.ref[x, y:y + 1, :] = corner_in[self.slot, 2 * corner[0] + corner[1], n:n + 1, :]

    sent = []

    def start(halos):
        for h in halos:
            h.pack()
        for axis in "cxy":
            for h in halos:
                h.each(axis, lambda c, _: c.start())
        sent.extend(halos)

    def arrive(halos):
        for h in halos:
            h.each("y", lambda c, _: c.wait_recv(), flip=True)
            h.each("x", lambda c, _: c.wait_recv(), flip=True)
        for h in halos:
            h.each("c", h.unpack, flip=True)

    h_vel = [[Halo(0, v1.at[0], 2, 1, 2), Halo(1, v1.at[1], 1, 2, 2), Halo(2, v1.at[2], 1, 1)],
             [Halo(3, v2.at[0], 2, 1, 2), Halo(4, v2.at[1], 1, 2, 2), Halo(5, v2.at[2], 1, 1)]]
    h_p = [[Halo(6, pin1, WX, WX, WX)], [Halo(7, pin2, WX, WX, WX)]]
    h_src = [[Halo(8, src1, SWEEPS, SWEEPS, SWEEPS)], [Halo(9, src2, SWEEPS, SWEEPS, SWEEPS)]]
    h_solid = [Halo(10, solid, 2, WX, WX)]
    h_rest = [Halo(13, solid, WX - 2, axes="x", skip=2)]
    h_mf = [Halo(11, mf.at[0], 1, axes="x"), Halo(12, mf.at[1], rows=1, width=0, axes="y")]

    for fetch in fetches[3:]:
        fetch.wait()
    start(h_vel[0] + h_p[0])

    column_of = lax.broadcasted_iota(jnp.int32, (columns, slots), 0).astype(F32)
    depth_of = lax.broadcasted_iota(jnp.int32, (nz, slots), 0).astype(F32)
    dep[...] = jnp.zeros_like(dep)

    def where_of(b):
        cell = rk[b, 0:1, :]
        column = jnp.floor((cell + 0.5) * (1.0 / nz))
        return column, cell - column * nz

    def deposit(b, carry):
        column, level = where_of(b)
        hot_c = column == column_of
        hot_z = jnp.where(level == depth_of, 1.0, 0.0).astype(BF16)
        volume = rk[b, 1:2, :]
        values = [volume] + [volume * rk[b, 2 + d:3 + d, :] for d in range(3)]
        parts = [split(value) for value in values]
        both = None
        for side in (0, 1):
            left = jnp.concatenate([jnp.where(hot_c, part[side], 0.0).astype(BF16) for part in parts], axis=0)
            term = lax.dot_general(left, hot_z, (((1,), (1,)), ((), ())), preferred_element_type=F32)
            both = term if both is None else both + term
        dep[...] += both
        return carry

    deposit(iy, 0)

    def deposit_from(k, carry):
        incoming(k).wait_recv()
        return deposit(from_mate(k), carry)

    lax.fori_loop(1, n_gy, deposit_from, 0)
    solid[own_x, own_y, :] = dep[pl.ds(0, columns), :].reshape(bx, by, nz)
    for d in range(3):
        mf[d, own_x, own_y, :] = dep[pl.ds((1 + d) * columns, columns), :].reshape(bx, by, nz)
    start(h_solid + h_mf)
    start(h_rest)
    arrive(h_solid + h_mf)
    arrive(h_vel[0])

    row = lax.broadcasted_iota(jnp.int32, (ey, nz), 0)
    depth = lax.broadcasted_iota(jnp.int32, (ey, nz), 1)
    row_in = jnp.where((row >= WY) | (iy > 0), 1.0, 0.0) * jnp.where((row < WY + by) | (iy < n_gy - 1), 1.0, 0.0)

    def voidage(x, carry):
        x_in = ((x >= WX) | (ix > 0)) & ((x < WX + bx) | (ix < n_gx - 1))
        eps[x] = jnp.maximum(1.0 - solid[x], FLOOR) * (row_in * jnp.where(x_in, 1.0, 0.0))
        return carry

    lax.fori_loop(WX - 2, WX + bx + 2, voidage, 0, unroll=4)

    def up_y(v):
        return pltpu.roll(v, ey - 1, 0)

    def down_y(v):
        return pltpu.roll(v, 1, 0)

    def up_z(v):
        return pltpu.roll(v, nz - 1, 1)

    def down_z(v):
        return pltpu.roll(v, 1, 1)

    last_z, first_z = depth == nz - 1, depth == 0

    def weights(x, carry):
        e = eps[x]
        near = [eps[x + 1], eps[x - 1], up_y(e), down_y(e),
                jnp.where(last_z, 0.0, up_z(e)), jnp.where(first_z, 0.0, down_z(e))]
        total = 0.5 * (6.0 * e + (((near[0] + near[1]) + (near[2] + near[3])) + (near[4] + near[5])))
        inside = e > 0.0
        inverse = jnp.where(inside, 0.5 / jnp.where(inside, total, 1.0), 0.0)
        for n in range(6):
            w = (e + near[n]) * inverse
            if n == 4:
                w = jnp.where(last_z, 0.0, w)
            if n == 5:
                w = jnp.where(first_z, 0.0, w)
            coef[n, x] = w
        coef[6, x] = 2.0 * inverse
        recip = 1.0 / jnp.where(inside, e, 1.0)
        rate[x] = (DT * VISC) * total * recip
        pull[x] = (DT * DRAG) * recip
        return carry

    lax.fori_loop(WX - 1, WX + bx + 1, weights, 0, unroll=5)

    def stencil(field, x):
        v = field[x]
        return v, (((coef[0, x] * field[x + 1] + coef[1, x] * field[x - 1])
                    + (coef[2, x] * up_y(v) + coef[3, x] * down_y(v)))
                   + (coef[4, x] * up_z(v) + coef[5, x] * down_z(v)))

    for step in range(STEPS):
        v = (v1, v2)[step]
        pin = (pin1, pin2)[step]
        src = (src1, src2)[step]

        def predict(x, carry):
            s, r, g, e = solid[x], rate[x], pull[x], eps[x]
            for d in range(3):
                old, mean = stencil(v.at[d], x)
                new = old + r * (mean - old) + g * (mf[d, x] - s * old)
                guess[d, x] = new
                flux[d, x] = e * new
            return carry

        lax.fori_loop(WX - 1, WX + bx + 1, predict, 0, unroll=5)

        def balance(x, carry):
            f1, f2 = flux[1, x], flux[2, x]
            out = ((flux[0, x + 1] - flux[0, x - 1]) + (up_y(f1) - down_y(f1))
                   + (jnp.where(last_z, 0.0, up_z(f2)) - jnp.where(first_z, 0.0, down_z(f2))))
            src[x, own_y, :] = (0.5 / DT) * out[WY:WY + by]
            return carry

        lax.fori_loop(WX, WX + bx, balance, 0, unroll=8)
        start(h_src[step])
        if step == 0:
            arrive(h_rest)
            for low in (0, WX + bx + 2):
                lax.fori_loop(low, low + WX - 2, voidage, 0, unroll=3)
            for low in (1, WX + bx + 1):
                lax.fori_loop(low, low + WX - 2, weights, 0, unroll=3)
        arrive(h_p[step])
        arrive(h_src[step])

        def scale(x, carry):
            sp[x] = src[x] * coef[6, x]
            return carry

        lax.fori_loop(1, ex - 1, scale, 0, unroll=8)

        held = pin
        for sweep in range(SWEEPS):
            into = (pa, pb)[sweep % 2]

            def relax(x, carry):
                _, mean = stencil(held, x)
                into[x] = mean - sp[x]
                return carry

            lax.fori_loop(1 + sweep, ex - 1 - sweep, relax, 0, unroll=4)
            held = into

        final = step == STEPS - 1

        def correct(x, carry):
            p = held[x]
            slopes = [held[x + 1] - held[x - 1], up_y(p) - down_y(p),
                      jnp.where(last_z, 0.0, up_z(p)) - jnp.where(first_z, 0.0, down_z(p))]
            for d in range(3):
                new = (guess[d, x] - (0.5 * DT) * slopes[d])[WY:WY + by]
                if final:
                    vel_out[d, x - WX] = new
                else:
                    v2[d, x, own_y, :] = new
            if final:
                p_out[x - WX] = p[WY:WY + by]
            else:
                pin2[x, own_y, :] = p[WY:WY + by]
            return carry

        lax.fori_loop(WX, WX + bx, correct, 0, unroll=4)
        if not final:
            start(h_vel[step + 1])
            start(h_p[step + 1])
            arrive(h_vel[step + 1])

    for f in range(4):
        grid = (vel_out[f] if f < 3 else eps[own_x, own_y, :]).reshape(columns, nz)
        high, low = split(grid.T)
        ft[pl.ds(f * nz, nz), :] = jnp.concatenate([high.astype(BF16), low.astype(BF16)], axis=1)

    def gather(b, carry):
        column, level = where_of(b)
        hot = jnp.where(column == column_of, 1.0, 0.0).astype(BF16)
        hot_z = level == depth_of
        wide = jnp.dot(ft[...], jnp.concatenate([hot, hot], axis=0), preferred_element_type=F32)
        at = [jnp.sum(jnp.where(hot_z, wide[f * nz:(f + 1) * nz], 0.0), axis=0, keepdims=True) for f in range(4)]
        scaled = rk[b, 1:2, :] * DRAG
        for d in range(3):
            dk[b, d:d + 1, :] = scaled * (at[d] - rk[b, 2 + d:3 + d, :]) / at[3]
        return carry

    def giving(k):
        return particles(k, dk.at[to_mate(k)], rd.at[iy], 1)

    def getting(k):
        return particles(k, dk.at[0], rd.at[from_mate(k)], 1)

    def gather_for(k, carry):
        gather(to_mate(n_gy - k), carry)
        giving(n_gy - k).start()
        return carry

    lax.fori_loop(1, n_gy, gather_for, 0)
    gather(iy, 0)
    rd[iy] = dk[iy]
    for h in sent:
        for axis in "xyc":
            h.each(axis, lambda c, _: c.wait_send())
    for k in range(1, n_gy):
        outgoing(k).wait_send()
        getting(k).wait_recv()
        giving(k).wait_send()
    for c in range(n_gy):
        for d in range(3):
            drag_out[d, pl.ds(c, 1), :] = rd[c, d:d + 1, :]


def deliver(*refs):
    pairs = len(refs) // 2
    copies = [pltpu.make_async_copy(refs[n], refs[pairs + n], refs[-1].at[n]) for n in range(pairs)]
    for copy in copies:
        copy.start()
    for copy in copies:
        copy.wait()


def solution(mesh):
    n_gx, n_gy = mesh.shape["gx"], mesh.shape["gy"]

    def per_device(velocity, pressure, part_cell, part_count, grain_velocities, part_vol):
        bx, by, nz = pressure.shape
        slots = part_vol.shape[-1]
        ext = (bx + 2 * WX, by + 2 * WY, nz)
        vmem = pl.BlockSpec(memory_space=pltpu.VMEM)
        anywhere = pl.BlockSpec(memory_space=pl.ANY)

        def field(*lead):
            return pltpu.VMEM(lead + ext, F32)

        def kernel(*refs):
            body(n_gx, n_gy, *refs)

        v, p, drag = pl.pallas_call(
            kernel,
            name="interval",
            out_shape=(
                pltpu.VMEM(velocity.shape, F32),
                pltpu.VMEM(pressure.shape, F32),
                pltpu.VMEM((3, n_gy, slots), F32),
            ),
            in_specs=[pl.BlockSpec(memory_space=pltpu.SMEM)] + [anywhere] * 5,
            out_specs=(vmem,) * 3,
            scratch_shapes=[
                pltpu.VMEM((n_gy, slots), jnp.int32),
                pltpu.VMEM((3, n_gy, slots), F32),
                pltpu.VMEM((n_gy, slots), F32),
                pltpu.SemaphoreType.DMA((7,)),
                field(3), field(3), field(), field(), field(), field(), field(), field(), field(),
                field(), field(3), field(), field(7), field(), field(), field(3), field(3),
                pltpu.VMEM((4 * bx * by, nz), F32),
                pltpu.VMEM((n_gy, ROWS, slots), F32),
                pltpu.VMEM((n_gy, ROWS, slots), F32),
                pltpu.VMEM((n_gy, 3, slots), F32),
                pltpu.VMEM((n_gy, 3, slots), F32),
                pltpu.VMEM((4 * nz, 2 * bx * by), BF16),
                pltpu.VMEM((14, 4, 16, nz), F32),
                pltpu.VMEM((14, 4, 16, nz), F32),
                pltpu.SemaphoreType.DMA((14, 8)),
                pltpu.SemaphoreType.DMA((14, 8)),
                pltpu.SemaphoreType.DMA((2, n_gy)),
                pltpu.SemaphoreType.DMA((2, n_gy)),
            ],
            compiler_params=pltpu.CompilerParams(
                collective_id=0, has_side_effects=True, vmem_limit_bytes=56 * 1024 * 1024
            ),
        )(
            part_count.reshape(n_gy),
            velocity,
            pressure,
            part_cell.reshape(n_gy, slots),
            grain_velocities.reshape(n_gy, 3, slots).transpose(1, 0, 2),
            part_vol.reshape(n_gy, slots),
        )
        v, p, drag = [pltpu.with_memory_space_constraint(a, pltpu.VMEM) for a in (v, p, drag)]
        v, p, drag = pl.pallas_call(
            deliver,
            name="deliver",
            out_shape=tuple(jax.ShapeDtypeStruct(a.shape, F32) for a in (v, p, drag)),
            in_specs=(vmem,) * 3,
            out_specs=(anywhere,) * 3,
            scratch_shapes=[pltpu.SemaphoreType.DMA((3,))],
        )(v, p, drag)
        return v, p, drag.transpose(1, 0, 2).reshape(grain_velocities.shape)

    placed = (
        P(None, "gx", "gy", None),
        P("gx", "gy", None),
        P("gx", "gy", None, None),
        P("gx", "gy", None),
        P("gx", "gy", None, None, None),
        P("gx", "gy", None, None),
    )
    return jax.shard_map(
        per_device,
        mesh=mesh,
        in_specs=placed,
        out_specs=(P(None, "gx", "gy", None), P("gx", "gy", None), P("gx", "gy", None, None, None)),
        check_vma=False,
    )
```

```python
import jax
import jax.numpy as jnp
from jax import lax
from jax.experimental import pallas as pl
from jax.experimental.pallas import tpu as pltpu
from jax.sharding import PartitionSpec as P

STEPS = 2
SWEEPS = 4
DRAG = 2.0
DT = 0.25
VISC = 0.2
FLOOR = 0.4

WX = SWEEPS + 1
WY = 8
ROWS = 5

MESH = pl.DeviceIdType.MESH
CORNERS = ((0, 0), (0, 1), (1, 0), (1, 1))
F32 = jnp.float32
BF16 = jnp.bfloat16


def split(value):
    high = value.astype(BF16).astype(F32)
    return high, value - high


def mate(i, k, n):
    if n & (n - 1):
        return lax.rem(i + k, n)
    bit, flip = 1, 0
    while bit < n:
        flip = flip + bit * ((i // bit + k // bit) % 2)
        bit *= 2
    return flip


def body(n_gx, n_gy, count_ref, vel_hbm, p_hbm, cell_hbm, gv_hbm, vol_hbm,
         vel_out, p_out, drag_out, cell_ref, gv_ref, vol_ref, fetch_sem,
         v1, v2, pin1, pin2, pa, pb, src1, src2, sp, solid, mf, eps, coef, rate, pull,
         guess, flux, dep, pk, rk, dk, rd, ft, pull_of, corner_out, corner_in, field_send, field_recv, part_send, part_recv):
    bx, by, nz = p_hbm.shape
    ex, ey = bx + 2 * WX, by + 2 * WY
    slots = vol_hbm.shape[-1]
    columns = bx * by
    ix, iy = lax.axis_index("gx"), lax.axis_index("gy")
    has = {("x", 0): ix > 0, ("x", 1): ix < n_gx - 1, ("y", 0): iy > 0, ("y", 1): iy < n_gy - 1}
    peer = {("x", 0): (ix - 1, iy), ("x", 1): (ix + 1, iy), ("y", 0): (ix, iy - 1), ("y", 1): (ix, iy + 1)}
    own_x, own_y = pl.ds(WX, bx), pl.ds(WY, by)

    def to_mate(k):
        return mate(iy, k, n_gy)

    def from_mate(k):
        return to_mate(k) if n_gy & (n_gy - 1) == 0 else lax.rem(iy + n_gy - k, n_gy)

    def beyond(corner):
        return ix + (2 * corner[0] - 1), iy + (2 * corner[1] - 1)

    barrier = pltpu.get_barrier_semaphore()
    for k in range(1, n_gy):
        pl.semaphore_signal(barrier, inc=1, device_id=(ix, to_mate(k)), device_id_type=MESH)
    for side in (0, 1):
        @pl.when(has["x", side])
        def _():
            pl.semaphore_signal(barrier, inc=1, device_id=peer["x", side], device_id_type=MESH)
    for corner in CORNERS:
        @pl.when(has["x", corner[0]] & has["y", corner[1]])
        def _():
            pl.semaphore_signal(barrier, inc=1, device_id=beyond(corner), device_id_type=MESH)

    fetches = [(cell_hbm, cell_ref), (vol_hbm, vol_ref), (gv_hbm, gv_ref)]
    fetches += [(vel_hbm.at[d], v1.at[d, own_x, own_y]) for d in range(3)] + [(p_hbm, pin1.at[own_x, own_y])]
    fetches = [pltpu.make_async_copy(source, landing, fetch_sem.at[n]) for n, (source, landing) in enumerate(fetches)]
    for fetch in fetches:
        fetch.start()

    fields = [v1.at[d] for d in range(3)] + [v2.at[d] for d in range(3)] + [mf.at[d] for d in range(3)]
    fields += [pin1, pin2, src1, src2, solid]
    for side in (0, 1):
        @pl.when(jnp.logical_not(has["x", side]))
        def _():
            for field in fields:
                at = 0 if side == 0 else WX + bx
                field[pl.ds(at, WX)] = jnp.zeros((WX, ey, nz), F32)

        @pl.when(jnp.logical_not(has["y", side]))
        def _():
            for field in fields:
                at = 0 if side == 0 else WY + by
                field[:, pl.ds(at, WY), :] = jnp.zeros((ex, WY, nz), F32)

    for fetch in fetches[:3]:
        fetch.wait()
    slot = lax.broadcasted_iota(jnp.int32, (1, slots), 1)
    for c in range(n_gy):
        pk[c, 0:1, :] = cell_ref[pl.ds(c, 1), :].astype(F32)
        pk[c, 1:2, :] = jnp.where(slot < count_ref[c], vol_ref[pl.ds(c, 1), :], 0.0)
        for d in range(3):
            pk[c, 2 + d:3 + d, :] = gv_ref[d, pl.ds(c, 1), :]

    x_peers = jnp.where(ix > 0, 1, 0) + jnp.where(ix < n_gx - 1, 1, 0)
    y_peers = jnp.where(iy > 0, 1, 0) + jnp.where(iy < n_gy - 1, 1, 0)
    pl.semaphore_wait(barrier, n_gy - 1 + x_peers * (1 + y_peers))

    def particles(k, source, landing, bank):
        return pltpu.make_async_remote_copy(
            src_ref=source, dst_ref=landing, send_sem=part_send.at[bank, k], recv_sem=part_recv.at[bank, k],
            device_id=(ix, to_mate(k)), device_id_type=MESH)

    def outgoing(k):
        return particles(k, pk.at[to_mate(k)], rk.at[iy], 0)

    def incoming(k):
        return particles(k, pk.at[0], rk.at[from_mate(k)], 0)

    for k in range(n_gy - 1, 0, -1):
        outgoing(k).start()
    rk[iy] = pk[iy]

    class Halo:
        def __init__(self, slot, ref, width, rows=0, reach=0, axes="xy", skip=0):
            self.slot, self.ref, self.width, self.span, self.axes, self.skip = slot, ref, width, rows, axes, skip
            self.rows = [(i, j) for i in range(reach) for j in range(reach) if i + j + 2 <= reach]

        def copy(self, index, source, landing, to):
            return pltpu.make_async_remote_copy(
                src_ref=source, dst_ref=landing, send_sem=field_send.at[self.slot, index],
                recv_sem=field_recv.at[self.slot, index], device_id=to, device_id_type=MESH)

        def x_copy(self, side):
            w, skip = self.width, self.skip
            at = skip if side == 0 else bx - w - skip
            source = self.ref.at[pl.ds(WX + at, w), own_y]
            landing = self.ref.at[pl.ds(WX + bx + skip if side == 0 else WX - w - skip, w), own_y]
            return self.copy(side, source, landing, peer["x", side])

        def y_copy(self, side):
            h, skip = self.span, self.skip
            source = self.ref.at[own_x, pl.ds(WY + skip if side == 0 else WY + by - h - skip, h)]
            landing = self.ref.at[own_x, pl.ds(WY + by + skip if side == 0 else WY - h - skip, h)]
            return self.copy(2 + side, source, landing, peer["y", side])

        def c_copy(self, corner):
            n = 2 * corner[0] + corner[1]
            size = len(self.rows)
            return self.copy(4 + n, corner_out.at[self.slot, n, pl.ds(0, size)],
                             corner_in.at[self.slot, n, pl.ds(0, size)], beyond(corner))

        def pack(self):
            for corner in CORNERS if self.rows else ():
                for n, (i, j) in enumerate(self.rows):
                    x = WX + (i if corner[0] == 0 else bx - 1 - i)
                    y = WY + (j if corner[1] == 0 else by - 1 - j)
                    corner_out[self.slot, 2 * corner[0] + corner[1], n] = self.ref[x, y:y + 1, :]

        def each(self, axis, act, flip=False):
            if axis == "c":
                for corner in CORNERS if self.rows else ():
                    near = (1 - corner[0], 1 - corner[1]) if flip else corner

                    @pl.when(has["x", near[0]] & has["y", near[1]])
                    def _():
                        act(self.c_copy(corner), corner)
            elif axis in self.axes:
                for side in (0, 1):
                    @pl.when(has[axis, 1 - side if flip else side])
                    def _():
                        act((self.x_copy if axis == "x" else self.y_copy)(side), None)

        def unpack(self, copy, corner):
            copy.wait_recv()
            for n, (i, j) in enumerate(self.rows):
                x = WX + bx + i if corner[0] == 0 else WX - 1 - i
                y = WY + by + j if corner[1] == 0 else WY - 1 - j
                self.ref[x, y:y + 1, :] = corner_in[self.slot, 2 * corner[0] + corner[1], n]

    sent = []

    def start(halos):
        for h in halos:
            h.pack()
        for axis in "cxy":
            for h in halos:
                h.each(axis, lambda c, _: c.start())
        sent.extend(halos)

    def arrive(halos):
        for h in halos:
            h.each("y", lambda c, _: c.wait_recv(), flip=True)
            h.each("x", lambda c, _: c.wait_recv(), flip=True)
        for h in halos:
            h.each("c", h.unpack, flip=True)

    h_vel = [[Halo(0, v1.at[0], 2, 1, 2), Halo(1, v1.at[1], 1, 2, 2), Halo(2, v1.at[2], 1, 1)],
             [Halo(3, v2.at[0], 2, 1, 2), Halo(4, v2.at[1], 1, 2, 2), Halo(5, v2.at[2], 1, 1)]]
    h_p = [[Halo(6, pin1, WX, WX, WX)], [Halo(7, pin2, WX - 1, WX - 1, WX, skip=1)]]
    h_src = [[Halo(8, src1, SWEEPS, SWEEPS, SWEEPS)], [Halo(9, src2, SWEEPS, SWEEPS, SWEEPS)]]
    h_solid = [Halo(10, solid, 2, WX, WX)]
    h_rest = [Halo(13, solid, WX - 2, axes="x", skip=2)]
    h_mf = [Halo(11, mf.at[0], 1, axes="x"), Halo(12, mf.at[1], rows=1, width=0, axes="y")]

    for fetch in fetches[3:]:
        fetch.wait()
    start(h_vel[0] + h_p[0])

    column_of = lax.broadcasted_iota(jnp.int32, (columns, slots), 0).astype(F32)
    depth_of = lax.broadcasted_iota(jnp.int32, (nz, slots), 0).astype(F32)
    dep[...] = jnp.zeros_like(dep)

    def where_of(b):
        cell = rk[b, 0:1, :]
        column = jnp.floor((cell + 0.5) * (1.0 / nz))
        return column, cell - column * nz

    def deposit(b, carry):
        column, level = where_of(b)
        hot_c = column == column_of
        hot_z = jnp.where(level == depth_of, 1.0, 0.0).astype(BF16)
        volume = rk[b, 1:2, :]
        values = [volume] + [volume * rk[b, 2 + d:3 + d, :] for d in range(3)]
        parts = [split(value) for value in values]
        both = None
        for side in (0, 1):
            left = jnp.concatenate([jnp.where(hot_c, part[side], 0.0).astype(BF16) for part in parts], axis=0)
            term = lax.dot_general(left, hot_z, (((1,), (1,)), ((), ())), preferred_element_type=F32)
            both = term if both is None else both + term
        dep[...] += both
        return carry

    deposit(iy, 0)

    def deposit_from(k, carry):
        incoming(k).wait_recv()
        return deposit(from_mate(k), carry)

    lax.fori_loop(1, n_gy, deposit_from, 0)
    solid[own_x, own_y, :] = dep[pl.ds(0, columns), :].reshape(bx, by, nz)
    for d in range(3):
        mf[d, own_x, own_y, :] = dep[pl.ds((1 + d) * columns, columns), :].reshape(bx, by, nz)
    start(h_solid + h_mf)
    start(h_rest)
    arrive(h_solid + h_mf)
    arrive(h_vel[0])

    row = lax.broadcasted_iota(jnp.int32, (ey, nz), 0)
    depth = lax.broadcasted_iota(jnp.int32, (ey, nz), 1)
    row_in = jnp.where((row >= WY) | (iy > 0), 1.0, 0.0) * jnp.where((row < WY + by) | (iy < n_gy - 1), 1.0, 0.0)

    def voidage(x, carry):
        x_in = ((x >= WX) | (ix > 0)) & ((x < WX + bx) | (ix < n_gx - 1))
        eps[x] = jnp.maximum(1.0 - solid[x], FLOOR) * (row_in * jnp.where(x_in, 1.0, 0.0))
        return carry

    lax.fori_loop(WX - 2, WX + bx + 2, voidage, 0, unroll=4)

    def up_y(v):
        return pltpu.roll(v, ey - 1, 0)

    def down_y(v):
        return pltpu.roll(v, 1, 0)

    def up_z(v):
        return pltpu.roll(v, nz - 1, 1)

    def down_z(v):
        return pltpu.roll(v, 1, 1)

    last_z, first_z = depth == nz - 1, depth == 0

    def weights(x, carry):
        e = eps[x]
        near = [eps[x + 1], eps[x - 1], up_y(e), down_y(e),
                jnp.where(last_z, 0.0, up_z(e)), jnp.where(first_z, 0.0, down_z(e))]
        total = 0.5 * (6.0 * e + (((near[0] + near[1]) + (near[2] + near[3])) + (near[4] + near[5])))
        inside = e > 0.0
        inverse = jnp.where(inside, 0.5 / jnp.where(inside, total, 1.0), 0.0)
        for n in range(6):
            w = (e + near[n]) * inverse
            if n == 4:
                w = jnp.where(last_z, 0.0, w)
            if n == 5:
                w = jnp.where(first_z, 0.0, w)
            coef[n, x] = w
        coef[6, x] = 2.0 * inverse
        recip = 1.0 / jnp.where(inside, e, 1.0)
        rate[x] = (DT * VISC) * total * recip
        pull[x] = (DT * DRAG) * recip
        return carry

    lax.fori_loop(WX - 1, WX + bx + 1, weights, 0, unroll=5)

    def stencil(field, x):
        v = field[x]
        return v, (((coef[0, x] * field[x + 1] + coef[1, x] * field[x - 1])
                    + (coef[2, x] * up_y(v) + coef[3, x] * down_y(v)))
                   + (coef[4, x] * up_z(v) + coef[5, x] * down_z(v)))

    def wide(b, tables):
        column, level = where_of(b)
        hot = jnp.where(column == column_of, 1.0, 0.0).astype(BF16)
        found = jnp.dot(tables, jnp.concatenate([hot, hot], axis=0), preferred_element_type=F32)
        hot_z = level == depth_of
        return [jnp.sum(jnp.where(hot_z, found[n:n + nz], 0.0), axis=0, keepdims=True)
                for n in range(0, found.shape[0], nz)]

    def table(grid):
        high, low = split(grid.reshape(columns, nz).T)
        return jnp.concatenate([high.astype(BF16), low.astype(BF16)], axis=1)

    def porosity(b, carry):
        at, = wide(b, ft[pl.ds(3 * nz, nz), :])
        pull_of[b] = rk[b, 1:2, :] * DRAG / at
        return carry

    for step in range(STEPS):
        v = (v1, v2)[step]
        pin = (pin1, pin2)[step]
        src = (src1, src2)[step]

        def predict(x, carry):
            s, r, g, e = solid[x], rate[x], pull[x], eps[x]
            for d in range(3):
                old, mean = stencil(v.at[d], x)
                new = old + r * (mean - old) + g * (mf[d, x] - s * old)
                guess[d, x] = new
                flux[d, x] = e * new
            return carry

        lax.fori_loop(WX - 1, WX + bx + 1, predict, 0, unroll=5)

        def balance(x, carry):
            f1, f2 = flux[1, x], flux[2, x]
            out = ((flux[0, x + 1] - flux[0, x - 1]) + (up_y(f1) - down_y(f1))
                   + (jnp.where(last_z, 0.0, up_z(f2)) - jnp.where(first_z, 0.0, down_z(f2))))
            src[x, own_y, :] = (0.5 / DT) * out[WY:WY + by]
            return carry

        lax.fori_loop(WX, WX + bx, balance, 0, unroll=8)
        start(h_src[step])
        if step == 0:
            arrive(h_rest)
            for low in (0, WX + bx + 2):
                lax.fori_loop(low, low + WX - 2, voidage, 0, unroll=3)
            for low in (1, WX + bx + 1):
                lax.fori_loop(low, low + WX - 2, weights, 0, unroll=3)
        else:
            ft[pl.ds(3 * nz, nz), :] = table(eps[own_x, own_y, :])
            lax.fori_loop(0, n_gy, porosity, 0)
        arrive(h_p[step])
        arrive(h_src[step])

        def scale(x, carry):
            sp[x] = src[x] * coef[6, x]
            return carry

        lax.fori_loop(1, ex - 1, scale, 0, unroll=8)

        held = pin
        for sweep in range(SWEEPS):
            into = (pa, pb)[sweep % 2]

            def relax(x, carry):
                _, mean = stencil(held, x)
                into[x] = mean - sp[x]
                return carry

            lax.fori_loop(1 + sweep, ex - 1 - sweep, relax, 0, unroll=4)
            held = into

        final = step == STEPS - 1

        def correct(x, carry):
            p = held[x]
            slopes = [held[x + 1] - held[x - 1], up_y(p) - down_y(p),
                      jnp.where(last_z, 0.0, up_z(p)) - jnp.where(first_z, 0.0, down_z(p))]
            for d in range(3):
                new = (guess[d, x] - (0.5 * DT) * slopes[d])[WY:WY + by]
                if final:
                    vel_out[d, x - WX] = new
                else:
                    v2[d, x, own_y, :] = new
            if final:
                p_out[x - WX] = p[WY:WY + by]
            else:
                for low, high in ((WY - 1, WY), (WY, WY + by), (WY + by, WY + by + 1)):
                    pin2[x, low:high, :] = p[low:high]
            return carry

        lax.fori_loop(WX, WX + bx, correct, 0, unroll=4)
        if not final:
            for x in (WX - 1, WX + bx):
                pin2[x, own_y, :] = held[x, own_y, :]
            start(h_vel[step + 1])
            start(h_p[step + 1])
            arrive(h_vel[step + 1])

    for d in range(3):
        ft[pl.ds(d * nz, nz), :] = table(vel_out[d])

    def gather(b, carry):
        at = wide(b, ft[pl.ds(0, 3 * nz), :])
        for d in range(3):
            dk[b, d:d + 1, :] = pull_of[b] * (at[d] - rk[b, 2 + d:3 + d, :])
        return carry

    def giving(k):
        return particles(k, dk.at[to_mate(k)], rd.at[iy], 1)

    def getting(k):
        return particles(k, dk.at[0], rd.at[from_mate(k)], 1)

    def gather_for(k, carry):
        gather(to_mate(n_gy - k), carry)
        giving(n_gy - k).start()
        return carry

    lax.fori_loop(1, n_gy, gather_for, 0)
    gather(iy, 0)
    rd[iy] = dk[iy]
    for h in sent:
        for axis in "xyc":
            h.each(axis, lambda c, _: c.wait_send())
    for k in range(1, n_gy):
        outgoing(k).wait_send()
        getting(k).wait_recv()
        giving(k).wait_send()
    for c in range(n_gy):
        for d in range(3):
            drag_out[d, pl.ds(c, 1), :] = rd[c, d:d + 1, :]


def deliver(*refs):
    pairs = len(refs) // 2
    copies = [pltpu.make_async_copy(refs[n], refs[pairs + n], refs[-1].at[n]) for n in range(pairs)]
    for copy in copies:
        copy.start()
    for copy in copies:
        copy.wait()


def solution(mesh):
    n_gx, n_gy = mesh.shape["gx"], mesh.shape["gy"]

    def per_device(velocity, pressure, part_cell, part_count, grain_velocities, part_vol):
        bx, by, nz = pressure.shape
        slots = part_vol.shape[-1]
        ext = (bx + 2 * WX, by + 2 * WY, nz)
        vmem = pl.BlockSpec(memory_space=pltpu.VMEM)
        anywhere = pl.BlockSpec(memory_space=pl.ANY)

        def field(*lead):
            return pltpu.VMEM(lead + ext, F32)

        def kernel(*refs):
            body(n_gx, n_gy, *refs)

        v, p, drag = pl.pallas_call(
            kernel,
            name="interval",
            out_shape=(
                pltpu.VMEM(velocity.shape, F32),
                pltpu.VMEM(pressure.shape, F32),
                pltpu.VMEM((3, n_gy, slots), F32),
            ),
            in_specs=[pl.BlockSpec(memory_space=pltpu.SMEM)] + [anywhere] * 5,
            out_specs=(vmem,) * 3,
            scratch_shapes=[
                pltpu.VMEM((n_gy, slots), jnp.int32),
                pltpu.VMEM((3, n_gy, slots), F32),
                pltpu.VMEM((n_gy, slots), F32),
                pltpu.SemaphoreType.DMA((7,)),
                field(3), field(3), field(), field(), field(), field(), field(), field(), field(),
                field(), field(3), field(), field(7), field(), field(), field(3), field(3),
                pltpu.VMEM((4 * bx * by, nz), F32),
                pltpu.VMEM((n_gy, ROWS, slots), F32),
                pltpu.VMEM((n_gy, ROWS, slots), F32),
                pltpu.VMEM((n_gy, 3, slots), F32),
                pltpu.VMEM((n_gy, 3, slots), F32),
                pltpu.VMEM((4 * nz, 2 * bx * by), BF16),
                pltpu.VMEM((n_gy, 1, slots), F32),
                pltpu.VMEM((14, 4, WX * (WX - 1) // 2, 1, nz), F32),
                pltpu.VMEM((14, 4, WX * (WX - 1) // 2, 1, nz), F32),
                pltpu.SemaphoreType.DMA((14, 8)),
                pltpu.SemaphoreType.DMA((14, 8)),
                pltpu.SemaphoreType.DMA((2, n_gy)),
                pltpu.SemaphoreType.DMA((2, n_gy)),
            ],
            compiler_params=pltpu.CompilerParams(
                collective_id=0, has_side_effects=True, vmem_limit_bytes=56 * 1024 * 1024
            ),
        )(
            part_count.reshape(n_gy),
            velocity,
            pressure,
            part_cell.reshape(n_gy, slots),
            grain_velocities.reshape(n_gy, 3, slots).transpose(1, 0, 2),
            part_vol.reshape(n_gy, slots),
        )
        v, p, drag = [pltpu.with_memory_space_constraint(a, pltpu.VMEM) for a in (v, p, drag)]
        v, p, drag = pl.pallas_call(
            deliver,
            name="deliver",
            out_shape=tuple(jax.ShapeDtypeStruct(a.shape, F32) for a in (v, p, drag)),
            in_specs=(vmem,) * 3,
            out_specs=(anywhere,) * 3,
            scratch_shapes=[pltpu.SemaphoreType.DMA((3,))],
        )(v, p, drag)
        return v, p, drag.transpose(1, 0, 2).reshape(grain_velocities.shape)

    placed = (
        P(None, "gx", "gy", None),
        P("gx", "gy", None),
        P("gx", "gy", None, None),
        P("gx", "gy", None),
        P("gx", "gy", None, None, None),
        P("gx", "gy", None, None),
    )
    return jax.shard_map(
        per_device,
        mesh=mesh,
        in_specs=placed,
        out_specs=(P(None, "gx", "gy", None), P("gx", "gy", None), P("gx", "gy", None, None, None)),
        check_vma=False,
    )
```

```python
import jax
import jax.numpy as jnp
from jax import lax
from jax.experimental import pallas as pl
from jax.experimental.pallas import tpu as pltpu
from jax.sharding import PartitionSpec as P

STEPS = 2
SWEEPS = 4
DRAG = 2.0
DT = 0.25
VISC = 0.2
FLOOR = 0.4

WX = SWEEPS + 1
WY = 8
ROWS = 5

MESH = pl.DeviceIdType.MESH
CORNERS = ((0, 0), (0, 1), (1, 0), (1, 1))
F32 = jnp.float32
BF16 = jnp.bfloat16


def split(value):
    high = value.astype(BF16).astype(F32)
    return high, value - high


def mate(i, k, n):
    if n & (n - 1):
        return lax.rem(i + k, n)
    bit, flip = 1, 0
    while bit < n:
        flip = flip + bit * ((i // bit + k // bit) % 2)
        bit *= 2
    return flip


def body(n_gx, n_gy, count_ref, vel_hbm, p_hbm, cell_hbm, gv_hbm, vol_hbm,
         vel_out, p_out, drag_out, cell_ref, gv_ref, vol_ref, fetch_sem,
         v1, v2, pin1, pin2, pa, pb, src1, src2, sp, solid, mf, eps, coef, rate, pull,
         guess, flux, dep, pk, rk, dk, rd, ft, pull_of, corner_out, corner_in, field_send, field_recv, part_send, part_recv):
    bx, by, nz = p_hbm.shape
    ex, ey = bx + 2 * WX, by + 2 * WY
    slots = vol_hbm.shape[-1]
    columns = bx * by
    ix, iy = lax.axis_index("gx"), lax.axis_index("gy")
    has = {("x", 0): ix > 0, ("x", 1): ix < n_gx - 1, ("y", 0): iy > 0, ("y", 1): iy < n_gy - 1}
    peer = {("x", 0): (ix - 1, iy), ("x", 1): (ix + 1, iy), ("y", 0): (ix, iy - 1), ("y", 1): (ix, iy + 1)}
    own_x, own_y = pl.ds(WX, bx), pl.ds(WY, by)

    def to_mate(k):
        return mate(iy, k, n_gy)

    def from_mate(k):
        return to_mate(k) if n_gy & (n_gy - 1) == 0 else lax.rem(iy + n_gy - k, n_gy)

    def beyond(corner):
        return ix + (2 * corner[0] - 1), iy + (2 * corner[1] - 1)

    barrier = pltpu.get_barrier_semaphore()
    for k in range(1, n_gy):
        pl.semaphore_signal(barrier, inc=1, device_id=(ix, to_mate(k)), device_id_type=MESH)
    for side in (0, 1):
        @pl.when(has["x", side])
        def _():
            pl.semaphore_signal(barrier, inc=1, device_id=peer["x", side], device_id_type=MESH)
    for corner in CORNERS:
        @pl.when(has["x", corner[0]] & has["y", corner[1]])
        def _():
            pl.semaphore_signal(barrier, inc=1, device_id=beyond(corner), device_id_type=MESH)

    fetches = [(cell_hbm, cell_ref), (vol_hbm, vol_ref), (gv_hbm, gv_ref)]
    fetches += [(vel_hbm.at[d], v1.at[d, own_x, own_y]) for d in range(3)] + [(p_hbm, pin1.at[own_x, own_y])]
    fetches = [pltpu.make_async_copy(source, landing, fetch_sem.at[n]) for n, (source, landing) in enumerate(fetches)]
    for fetch in fetches:
        fetch.start()

    fields = [v1.at[d] for d in range(3)] + [v2.at[d] for d in range(3)] + [mf.at[d] for d in range(3)]
    fields += [pin1, pin2, src1, src2, solid]
    for side in (0, 1):
        @pl.when(jnp.logical_not(has["x", side]))
        def _():
            for field in fields:
                at = 0 if side == 0 else WX + bx
                field[pl.ds(at, WX)] = jnp.zeros((WX, ey, nz), F32)

        @pl.when(jnp.logical_not(has["y", side]))
        def _():
            for field in fields:
                at = 0 if side == 0 else WY + by
                field[:, pl.ds(at, WY), :] = jnp.zeros((ex, WY, nz), F32)

    for fetch in fetches[:3]:
        fetch.wait()
    slot = lax.broadcasted_iota(jnp.int32, (1, slots), 1)
    for c in range(n_gy):
        pk[c, 0:1, :] = cell_ref[pl.ds(c, 1), :].astype(F32)
        pk[c, 1:2, :] = jnp.where(slot < count_ref[c], vol_ref[pl.ds(c, 1), :], 0.0)
        for d in range(3):
            pk[c, 2 + d:3 + d, :] = gv_ref[d, pl.ds(c, 1), :]

    x_peers = jnp.where(ix > 0, 1, 0) + jnp.where(ix < n_gx - 1, 1, 0)
    y_peers = jnp.where(iy > 0, 1, 0) + jnp.where(iy < n_gy - 1, 1, 0)
    pl.semaphore_wait(barrier, n_gy - 1 + x_peers * (1 + y_peers))

    def particles(k, source, landing, bank):
        return pltpu.make_async_remote_copy(
            src_ref=source, dst_ref=landing, send_sem=part_send.at[bank, k], recv_sem=part_recv.at[bank, k],
            device_id=(ix, to_mate(k)), device_id_type=MESH)

    def outgoing(k):
        return particles(k, pk.at[to_mate(k)], rk.at[iy], 0)

    def incoming(k):
        return particles(k, pk.at[0], rk.at[from_mate(k)], 0)

    for k in range(n_gy - 1, 0, -1):
        outgoing(k).start()
    rk[iy] = pk[iy]

    class Halo:
        def __init__(self, slot, ref, width, rows=0, reach=0, axes="xy", skip=0, over=0):
            self.slot, self.ref, self.width, self.span, self.axes, self.skip = slot, ref, width, rows, axes, skip
            self.rows = [(i, j) for i in range(reach) for j in range(reach) if over < i + j + 2 <= reach]

        def copy(self, index, source, landing, to):
            return pltpu.make_async_remote_copy(
                src_ref=source, dst_ref=landing, send_sem=field_send.at[self.slot, index],
                recv_sem=field_recv.at[self.slot, index], device_id=to, device_id_type=MESH)

        def x_copy(self, side):
            w, skip = self.width, self.skip
            at = skip if side == 0 else bx - w - skip
            source = self.ref.at[pl.ds(WX + at, w), own_y]
            landing = self.ref.at[pl.ds(WX + bx + skip if side == 0 else WX - w - skip, w), own_y]
            return self.copy(side, source, landing, peer["x", side])

        def y_copy(self, side):
            h, skip = self.span, self.skip
            source = self.ref.at[own_x, pl.ds(WY + skip if side == 0 else WY + by - h - skip, h)]
            landing = self.ref.at[own_x, pl.ds(WY + by + skip if side == 0 else WY - h - skip, h)]
            return self.copy(2 + side, source, landing, peer["y", side])

        def c_copy(self, corner):
            n = 2 * corner[0] + corner[1]
            size = len(self.rows)
            return self.copy(4 + n, corner_out.at[self.slot, n, pl.ds(0, size)],
                             corner_in.at[self.slot, n, pl.ds(0, size)], beyond(corner))

        def pack(self):
            for corner in CORNERS if self.rows else ():
                for n, (i, j) in enumerate(self.rows):
                    x = WX + (i if corner[0] == 0 else bx - 1 - i)
                    y = WY + (j if corner[1] == 0 else by - 1 - j)
                    corner_out[self.slot, 2 * corner[0] + corner[1], n] = self.ref[x, y:y + 1, :]

        def each(self, axis, act, flip=False):
            if axis == "c":
                for corner in CORNERS if self.rows else ():
                    near = (1 - corner[0], 1 - corner[1]) if flip else corner

                    @pl.when(has["x", near[0]] & has["y", near[1]])
                    def _():
                        act(self.c_copy(corner), corner)
            elif axis in self.axes:
                for side in (0, 1):
                    @pl.when(has[axis, 1 - side if flip else side])
                    def _():
                        act((self.x_copy if axis == "x" else self.y_copy)(side), None)

        def unpack(self, copy, corner):
            copy.wait_recv()
            for n, (i, j) in enumerate(self.rows):
                x = WX + bx + i if corner[0] == 0 else WX - 1 - i
                y = WY + by + j if corner[1] == 0 else WY - 1 - j
                self.ref[x, y:y + 1, :] = corner_in[self.slot, 2 * corner[0] + corner[1], n]

    sent = []

    def start(halos):
        for h in halos:
            h.pack()
        for axis in "cxy":
            for h in halos:
                h.each(axis, lambda c, _: c.start())
        sent.extend(halos)

    def arrive(halos, axes="yxc"):
        for axis in axes:
            for h in halos:
                h.each(axis, h.unpack if axis == "c" else lambda c, _: c.wait_recv(), flip=True)

    h_vel = [[Halo(0, v1.at[0], 2, 1, 2), Halo(1, v1.at[1], 1, 2, 2), Halo(2, v1.at[2], 1, 1)],
             [Halo(3, v2.at[0], 2, 1, 2), Halo(4, v2.at[1], 1, 2, 2), Halo(5, v2.at[2], 1, 1)]]
    h_p = [[Halo(6, pin1, WX, WX, WX)], [Halo(7, pin2, WX - 1, WX - 1, WX, skip=1)]]
    near = SWEEPS // 2
    h_src = [[Halo(8, src1, near, SWEEPS, SWEEPS)], [Halo(9, src2, near, SWEEPS, SWEEPS)]]
    h_far = [[Halo(14, src1, SWEEPS - near, axes="x", skip=near)], [Halo(15, src2, SWEEPS - near, axes="x", skip=near)]]
    h_solid = [Halo(10, solid, 2, WX, 2)]
    h_rest = [Halo(13, solid, WX - 2, reach=WX, axes="x", skip=2, over=2)]
    h_mf = [Halo(11, mf.at[0], 1, axes="x"), Halo(12, mf.at[1], rows=1, width=0, axes="y")]

    for fetch in fetches[3:]:
        fetch.wait()
    start(h_vel[0] + h_p[0])

    column_of = lax.broadcasted_iota(jnp.int32, (columns, slots), 0).astype(F32)
    depth_of = lax.broadcasted_iota(jnp.int32, (nz, slots), 0).astype(F32)
    dep[...] = jnp.zeros_like(dep)

    def where_of(b):
        cell = rk[b, 0:1, :]
        column = jnp.floor((cell + 0.5) * (1.0 / nz))
        return column, cell - column * nz

    def deposit(b, carry):
        column, level = where_of(b)
        hot_c = column == column_of
        hot_z = jnp.where(level == depth_of, 1.0, 0.0).astype(BF16)
        volume = rk[b, 1:2, :]
        values = [volume] + [volume * rk[b, 2 + d:3 + d, :] for d in range(3)]
        parts = [split(value) for value in values]
        both = None
        for side in (0, 1):
            left = jnp.concatenate([jnp.where(hot_c, part[side], 0.0).astype(BF16) for part in parts], axis=0)
            term = lax.dot_general(left, hot_z, (((1,), (1,)), ((), ())), preferred_element_type=F32)
            both = term if both is None else both + term
        dep[...] += both
        return carry

    deposit(iy, 0)

    def deposit_from(k, carry):
        incoming(k).wait_recv()
        return deposit(from_mate(k), carry)

    lax.fori_loop(1, n_gy, deposit_from, 0)
    solid[own_x, own_y, :] = dep[pl.ds(0, columns), :].reshape(bx, by, nz)
    for d in range(3):
        mf[d, own_x, own_y, :] = dep[pl.ds((1 + d) * columns, columns), :].reshape(bx, by, nz)
    start(h_solid + h_mf)
    start(h_rest)

    row = lax.broadcasted_iota(jnp.int32, (ey, nz), 0)
    depth = lax.broadcasted_iota(jnp.int32, (ey, nz), 1)
    row_in = jnp.where((row >= WY) | (iy > 0), 1.0, 0.0) * jnp.where((row < WY + by) | (iy < n_gy - 1), 1.0, 0.0)

    def voidage(x, carry):
        x_in = ((x >= WX) | (ix > 0)) & ((x < WX + bx) | (ix < n_gx - 1))
        eps[x] = jnp.maximum(1.0 - solid[x], FLOOR) * (row_in * jnp.where(x_in, 1.0, 0.0))
        return carry

    def sweep_over(act, spans, unroll):
        for first, end in spans:
            if first < end:
                lax.fori_loop(first, end, act, 0, unroll=min(unroll, end - first))

    low, high = WX, WX + bx

    def up_y(v):
        return pltpu.roll(v, ey - 1, 0)

    def down_y(v):
        return pltpu.roll(v, 1, 0)

    def up_z(v):
        return pltpu.roll(v, nz - 1, 1)

    def down_z(v):
        return pltpu.roll(v, 1, 1)

    last_z, first_z = depth == nz - 1, depth == 0

    def weights(x, carry):
        e = eps[x]
        near = [eps[x + 1], eps[x - 1], up_y(e), down_y(e),
                jnp.where(last_z, 0.0, up_z(e)), jnp.where(first_z, 0.0, down_z(e))]
        total = 0.5 * (6.0 * e + (((near[0] + near[1]) + (near[2] + near[3])) + (near[4] + near[5])))
        inside = e > 0.0
        inverse = jnp.where(inside, 0.5 / jnp.where(inside, total, 1.0), 0.0)
        for n in range(6):
            w = (e + near[n]) * inverse
            if n == 4:
                w = jnp.where(last_z, 0.0, w)
            if n == 5:
                w = jnp.where(first_z, 0.0, w)
            coef[n, x] = w
        coef[6, x] = 2.0 * inverse
        recip = 1.0 / jnp.where(inside, e, 1.0)
        rate[x] = (DT * VISC) * total * recip
        pull[x] = (DT * DRAG) * recip
        return carry

    def stencil(field, x):
        v = field[x]
        return v, (((coef[0, x] * field[x + 1] + coef[1, x] * field[x - 1])
                    + (coef[2, x] * up_y(v) + coef[3, x] * down_y(v)))
                   + (coef[4, x] * up_z(v) + coef[5, x] * down_z(v)))

    def wide(b, tables):
        column, level = where_of(b)
        hot = jnp.where(column == column_of, 1.0, 0.0).astype(BF16)
        found = jnp.dot(tables, jnp.concatenate([hot, hot], axis=0), preferred_element_type=F32)
        hot_z = level == depth_of
        return [jnp.sum(jnp.where(hot_z, found[n:n + nz], 0.0), axis=0, keepdims=True)
                for n in range(0, found.shape[0], nz)]

    def table(grid):
        high, low = split(grid.reshape(columns, nz).T)
        return jnp.concatenate([high.astype(BF16), low.astype(BF16)], axis=1)

    def porosity(b, carry):
        at, = wide(b, ft[pl.ds(3 * nz, nz), :])
        pull_of[b] = rk[b, 1:2, :] * DRAG / at
        return carry

    for step in range(STEPS):
        v = (v1, v2)[step]
        pin = (pin1, pin2)[step]
        src = (src1, src2)[step]

        def predict(x, carry):
            s, r, g, e = solid[x], rate[x], pull[x], eps[x]
            for d in range(3):
                old, mean = stencil(v.at[d], x)
                new = old + r * (mean - old) + g * (mf[d, x] - s * old)
                guess[d, x] = new
                flux[d, x] = e * new
            return carry

        def balance(x, carry):
            f1, f2 = flux[1, x], flux[2, x]
            out = ((flux[0, x + 1] - flux[0, x - 1]) + (up_y(f1) - down_y(f1))
                   + (jnp.where(last_z, 0.0, up_z(f2)) - jnp.where(first_z, 0.0, down_z(f2))))
            src[x, own_y, :] = (0.5 / DT) * out[WY:WY + by]
            return carry

        early = h_vel[step] + (h_solid + h_mf if step == 0 else [])
        arrive(early, "y")
        if step == 0:
            sweep_over(voidage, [(low, high)], 4)
            sweep_over(weights, [(low + 1, high - 1)], 3)
        sweep_over(predict, [(low + 1, high - 1)], 3)
        sweep_over(balance, [(low + near, high - near)], 4)
        start(h_far[step])
        arrive(early, "xc")
        if step == 0:
            sweep_over(voidage, [(low - 2, low), (high, high + 2)], 2)
            sweep_over(weights, [(low - 1, low + 1), (high - 1, high + 1)], 2)
        sweep_over(predict, [(low - 1, low + 1), (high - 1, high + 1)], 2)
        sweep_over(balance, [(low, low + near), (high - near, high)], 2)
        start(h_src[step])
        arrive(h_src[step], "y")
        if step == 0:
            arrive(h_rest)
            sweep_over(voidage, [(0, low), (high, ex)], 5)
            sweep_over(weights, [(1, low + 1), (high - 1, ex - 1)], 5)
            arrive(h_p[step])
        else:
            arrive(h_p[step], "y")

        def scale(x, carry):
            sp[x] = src[x] * coef[6, x]
            return carry

        stages = [pin] + [(pa, pb)[sweep % 2] for sweep in range(SWEEPS)]

        def relaxing(sweep):
            held, into = stages[sweep], stages[sweep + 1]

            def relax(x, carry):
                _, mean = stencil(held, x)
                into[x] = mean - sp[x]
                return carry

            return relax

        inset = 0 if step == 0 else 1
        sweep_over(scale, [(low, high)], 8)
        for sweep in range(SWEEPS):
            sweep_over(relaxing(sweep), [(low + sweep + inset, high - sweep - inset)], 4)
        if step:
            ft[pl.ds(3 * nz, nz), :] = table(eps[own_x, own_y, :])
            lax.fori_loop(0, n_gy, porosity, 0)
            arrive(h_p[step], "xc")
        arrive(h_src[step], "xc")
        arrive(h_far[step])
        sweep_over(scale, [(1, low), (high, ex - 1)], 4)
        for sweep in range(SWEEPS):
            sweep_over(relaxing(sweep), [(1 + sweep, low + sweep + inset), (high - sweep - inset, ex - 1 - sweep)], 5)
        held = stages[SWEEPS]

        final = step == STEPS - 1

        def correct(x, carry):
            p = held[x]
            slopes = [held[x + 1] - held[x - 1], up_y(p) - down_y(p),
                      jnp.where(last_z, 0.0, up_z(p)) - jnp.where(first_z, 0.0, down_z(p))]
            for d in range(3):
                new = (guess[d, x] - (0.5 * DT) * slopes[d])[WY:WY + by]
                if final:
                    vel_out[d, x - WX] = new
                else:
                    v2[d, x, own_y, :] = new
            if final:
                p_out[x - WX] = p[WY:WY + by]
            else:
                for low, high in ((WY - 1, WY), (WY, WY + by), (WY + by, WY + by + 1)):
                    pin2[x, low:high, :] = p[low:high]
            return carry

        lax.fori_loop(WX, WX + bx, correct, 0, unroll=4)
        if not final:
            for x in (WX - 1, WX + bx):
                pin2[x, own_y, :] = held[x, own_y, :]
            start(h_vel[step + 1])
            start(h_p[step + 1])

    for d in range(3):
        ft[pl.ds(d * nz, nz), :] = table(vel_out[d])

    def gather(b, carry):
        at = wide(b, ft[pl.ds(0, 3 * nz), :])
        for d in range(3):
            dk[b, d:d + 1, :] = pull_of[b] * (at[d] - rk[b, 2 + d:3 + d, :])
        return carry

    def giving(k):
        return particles(k, dk.at[to_mate(k)], rd.at[iy], 1)

    def getting(k):
        return particles(k, dk.at[0], rd.at[from_mate(k)], 1)

    def gather_for(k, carry):
        gather(to_mate(n_gy - k), carry)
        giving(n_gy - k).start()
        return carry

    lax.fori_loop(1, n_gy, gather_for, 0)
    gather(iy, 0)
    rd[iy] = dk[iy]
    for h in sent:
        for axis in "xyc":
            h.each(axis, lambda c, _: c.wait_send())
    for k in range(1, n_gy):
        outgoing(k).wait_send()
        getting(k).wait_recv()
        giving(k).wait_send()
    for c in range(n_gy):
        for d in range(3):
            drag_out[d, pl.ds(c, 1), :] = rd[c, d:d + 1, :]


def deliver(*refs):
    pairs = len(refs) // 2
    copies = [pltpu.make_async_copy(refs[n], refs[pairs + n], refs[-1].at[n]) for n in range(pairs)]
    for copy in copies:
        copy.start()
    for copy in copies:
        copy.wait()


def solution(mesh):
    n_gx, n_gy = mesh.shape["gx"], mesh.shape["gy"]

    def per_device(velocity, pressure, part_cell, part_count, grain_velocities, part_vol):
        bx, by, nz = pressure.shape
        slots = part_vol.shape[-1]
        ext = (bx + 2 * WX, by + 2 * WY, nz)
        vmem = pl.BlockSpec(memory_space=pltpu.VMEM)
        anywhere = pl.BlockSpec(memory_space=pl.ANY)

        def field(*lead):
            return pltpu.VMEM(lead + ext, F32)

        def kernel(*refs):
            body(n_gx, n_gy, *refs)

        v, p, drag = pl.pallas_call(
            kernel,
            name="interval",
            out_shape=(
                pltpu.VMEM(velocity.shape, F32),
                pltpu.VMEM(pressure.shape, F32),
                pltpu.VMEM((3, n_gy, slots), F32),
            ),
            in_specs=[pl.BlockSpec(memory_space=pltpu.SMEM)] + [anywhere] * 5,
            out_specs=(vmem,) * 3,
            scratch_shapes=[
                pltpu.VMEM((n_gy, slots), jnp.int32),
                pltpu.VMEM((3, n_gy, slots), F32),
                pltpu.VMEM((n_gy, slots), F32),
                pltpu.SemaphoreType.DMA((7,)),
                field(3), field(3), field(), field(), field(), field(), field(), field(), field(),
                field(), field(3), field(), field(7), field(), field(), field(3), field(3),
                pltpu.VMEM((4 * bx * by, nz), F32),
                pltpu.VMEM((n_gy, ROWS, slots), F32),
                pltpu.VMEM((n_gy, ROWS, slots), F32),
                pltpu.VMEM((n_gy, 3, slots), F32),
                pltpu.VMEM((n_gy, 3, slots), F32),
                pltpu.VMEM((4 * nz, 2 * bx * by), BF16),
                pltpu.VMEM((n_gy, 1, slots), F32),
                pltpu.VMEM((16, 4, WX * (WX - 1) // 2, 1, nz), F32),
                pltpu.VMEM((16, 4, WX * (WX - 1) // 2, 1, nz), F32),
                pltpu.SemaphoreType.DMA((16, 8)),
                pltpu.SemaphoreType.DMA((16, 8)),
                pltpu.SemaphoreType.DMA((2, n_gy)),
                pltpu.SemaphoreType.DMA((2, n_gy)),
            ],
            compiler_params=pltpu.CompilerParams(
                collective_id=0, has_side_effects=True, vmem_limit_bytes=56 * 1024 * 1024
            ),
        )(
            part_count.reshape(n_gy),
            velocity,
            pressure,
            part_cell.reshape(n_gy, slots),
            grain_velocities.reshape(n_gy, 3, slots).transpose(1, 0, 2),
            part_vol.reshape(n_gy, slots),
        )
        v, p, drag = [pltpu.with_memory_space_constraint(a, pltpu.VMEM) for a in (v, p, drag)]
        v, p, drag = pl.pallas_call(
            deliver,
            name="deliver",
            out_shape=tuple(jax.ShapeDtypeStruct(a.shape, F32) for a in (v, p, drag)),
            in_specs=(vmem,) * 3,
            out_specs=(anywhere,) * 3,
            scratch_shapes=[pltpu.SemaphoreType.DMA((3,))],
        )(v, p, drag)
        return v, p, drag.transpose(1, 0, 2).reshape(grain_velocities.shape)

    placed = (
        P(None, "gx", "gy", None),
        P("gx", "gy", None),
        P("gx", "gy", None, None),
        P("gx", "gy", None),
        P("gx", "gy", None, None, None),
        P("gx", "gy", None, None),
    )
    return jax.shard_map(
        per_device,
        mesh=mesh,
        in_specs=placed,
        out_specs=(P(None, "gx", "gy", None), P("gx", "gy", None), P("gx", "gy", None, None, None)),
        check_vma=False,
    )
```

```python
import jax
import jax.numpy as jnp
from jax import lax
from jax.experimental import pallas as pl
from jax.experimental.pallas import tpu as pltpu
from jax.sharding import PartitionSpec as P

STEPS = 2
SWEEPS = 4
DRAG = 2.0
DT = 0.25
VISC = 0.2
FLOOR = 0.4

WX = SWEEPS + 1
WY = 8
ROWS = 5

MESH = pl.DeviceIdType.MESH
CORNERS = ((0, 0), (0, 1), (1, 0), (1, 1))
F32 = jnp.float32
BF16 = jnp.bfloat16


def split(value):
    high = value.astype(BF16).astype(F32)
    return high, value - high


def mate(i, k, n):
    if n & (n - 1):
        return lax.rem(i + k, n)
    bit, flip = 1, 0
    while bit < n:
        flip = flip + bit * ((i // bit + k // bit) % 2)
        bit *= 2
    return flip


def body(n_gx, n_gy, count_ref, vel_hbm, p_hbm, cell_hbm, gv_hbm, vol_hbm,
         vel_out, p_out, drag_out, cell_ref, gv_ref, vol_ref, fetch_sem,
         v1, v2, pin1, pin2, pa, pb, src1, src2, sp, solid, mf, eps, coef, rate, pull,
         guess, flux, dep, pk, rk, dk, rd, ft, pull_of, corner_out, corner_in, passed, aside_send, aside_recv,
         field_send, field_recv, part_send, part_recv):
    bx, by, nz = p_hbm.shape
    ex, ey = bx + 2 * WX, by + 2 * WY
    slots = vol_hbm.shape[-1]
    columns = bx * by
    ix, iy = lax.axis_index("gx"), lax.axis_index("gy")
    has = {("x", 0): ix > 0, ("x", 1): ix < n_gx - 1, ("y", 0): iy > 0, ("y", 1): iy < n_gy - 1}
    peer = {("x", 0): (ix - 1, iy), ("x", 1): (ix + 1, iy), ("y", 0): (ix, iy - 1), ("y", 1): (ix, iy + 1)}
    own_x, own_y = pl.ds(WX, bx), pl.ds(WY, by)

    def to_mate(k):
        return mate(iy, k, n_gy)

    def from_mate(k):
        return to_mate(k) if n_gy & (n_gy - 1) == 0 else lax.rem(iy + n_gy - k, n_gy)

    def beyond(corner):
        return ix + (2 * corner[0] - 1), iy + (2 * corner[1] - 1)

    barrier = pltpu.get_barrier_semaphore()
    for k in range(1, n_gy):
        pl.semaphore_signal(barrier, inc=1, device_id=(ix, to_mate(k)), device_id_type=MESH)
    for side in (0, 1):
        @pl.when(has["x", side])
        def _():
            pl.semaphore_signal(barrier, inc=1, device_id=peer["x", side], device_id_type=MESH)
    for corner in CORNERS:
        @pl.when(has["x", corner[0]] & has["y", corner[1]])
        def _():
            pl.semaphore_signal(barrier, inc=1, device_id=beyond(corner), device_id_type=MESH)

    square = n_gx == 4
    origin, middle, target = (2, 1), (0, 3), (1, 2)
    if square:
        for side in (0, 1):
            @pl.when(ix == middle[side])
            def _():
                pl.semaphore_signal(barrier, inc=1, device_id=(origin[side], iy), device_id_type=MESH)

    fetches = [(cell_hbm, cell_ref), (vol_hbm, vol_ref), (gv_hbm, gv_ref)]
    fetches += [(vel_hbm.at[d], v1.at[d, own_x, own_y]) for d in range(3)] + [(p_hbm, pin1.at[own_x, own_y])]
    fetches = [pltpu.make_async_copy(source, landing, fetch_sem.at[n]) for n, (source, landing) in enumerate(fetches)]
    for fetch in fetches:
        fetch.start()

    fields = [v1.at[d] for d in range(3)] + [v2.at[d] for d in range(3)] + [mf.at[d] for d in range(3)]
    fields += [pin1, pin2, src1, src2, solid]
    for side in (0, 1):
        @pl.when(jnp.logical_not(has["x", side]))
        def _():
            for field in fields:
                at = 0 if side == 0 else WX + bx
                field[pl.ds(at, WX)] = jnp.zeros((WX, ey, nz), F32)

        @pl.when(jnp.logical_not(has["y", side]))
        def _():
            for field in fields:
                at = 0 if side == 0 else WY + by
                field[:, pl.ds(at, WY), :] = jnp.zeros((ex, WY, nz), F32)

    for fetch in fetches[:3]:
        fetch.wait()
    slot = lax.broadcasted_iota(jnp.int32, (1, slots), 1)
    for c in range(n_gy):
        pk[c, 0:1, :] = cell_ref[pl.ds(c, 1), :].astype(F32)
        pk[c, 1:2, :] = jnp.where(slot < count_ref[c], vol_ref[pl.ds(c, 1), :], 0.0)
        for d in range(3):
            pk[c, 2 + d:3 + d, :] = gv_ref[d, pl.ds(c, 1), :]

    x_peers = jnp.where(ix > 0, 1, 0) + jnp.where(ix < n_gx - 1, 1, 0)
    y_peers = jnp.where(iy > 0, 1, 0) + jnp.where(iy < n_gy - 1, 1, 0)
    detours = jnp.where((ix == 1) | (ix == 2), 1, 0) if square else 0
    pl.semaphore_wait(barrier, n_gy - 1 + x_peers * (1 + y_peers) + detours)

    def particles(k, source, landing, bank):
        return pltpu.make_async_remote_copy(
            src_ref=source, dst_ref=landing, send_sem=part_send.at[bank, k], recv_sem=part_recv.at[bank, k],
            device_id=(ix, to_mate(k)), device_id_type=MESH)

    def outgoing(k):
        return particles(k, pk.at[to_mate(k)], rk.at[iy], 0)

    def incoming(k):
        return particles(k, pk.at[0], rk.at[from_mate(k)], 0)

    for k in range(n_gy - 1, 0, -1):
        outgoing(k).start()
    rk[iy] = pk[iy]

    class Halo:
        def __init__(self, slot, ref, width, rows=0, reach=0, axes="xy", skip=0, over=0, detour=None):
            self.slot, self.ref, self.width, self.span, self.axes, self.skip = slot, ref, width, rows, axes, skip
            self.detour = detour if square else None
            self.rows = [(i, j) for i in range(reach) for j in range(reach) if over < i + j + 2 <= reach]

        def copy(self, index, source, landing, to):
            return pltpu.make_async_remote_copy(
                src_ref=source, dst_ref=landing, send_sem=field_send.at[self.slot, index],
                recv_sem=field_recv.at[self.slot, index], device_id=to, device_id_type=MESH)

        def x_copy(self, side):
            w, skip = self.width, self.skip
            at = skip if side == 0 else bx - w - skip
            source = self.ref.at[pl.ds(WX + at, w), own_y]
            landing = self.ref.at[pl.ds(WX + bx + skip if side == 0 else WX - w - skip, w), own_y]
            return self.copy(side, source, landing, peer["x", side])

        def aside(self, side):
            held = passed.at[self.detour, pl.ds(0, self.width)]
            at = self.skip if side == 0 else bx - self.width - self.skip
            return pltpu.make_async_remote_copy(
                src_ref=self.ref.at[pl.ds(WX + at, self.width), own_y], dst_ref=held,
                send_sem=field_send.at[self.slot, side], recv_sem=aside_recv.at[self.detour],
                device_id=(middle[side], iy), device_id_type=MESH)

        def onward(self, side):
            landing = WX + bx + self.skip if side == 0 else WX - self.width - self.skip
            return pltpu.make_async_remote_copy(
                src_ref=passed.at[self.detour, pl.ds(0, self.width)],
                dst_ref=self.ref.at[pl.ds(landing, self.width), own_y],
                send_sem=aside_send.at[self.detour], recv_sem=field_recv.at[self.slot, side],
                device_id=(target[side], iy), device_id_type=MESH)

        def send_x(self):
            for side in (0, 1):
                straight = has["x", side]
                if self.detour is not None:
                    straight = straight & (ix != origin[side])

                    @pl.when(ix == origin[side])
                    def _():
                        self.aside(side).start()

                @pl.when(straight)
                def _():
                    self.x_copy(side).start()

        def pass_on(self, act):
            for side in (0, 1) if self.detour is not None else ():
                @pl.when(ix == middle[side])
                def _():
                    act(self, side)

        def y_copy(self, side):
            h, skip = self.span, self.skip
            source = self.ref.at[own_x, pl.ds(WY + skip if side == 0 else WY + by - h - skip, h)]
            landing = self.ref.at[own_x, pl.ds(WY + by + skip if side == 0 else WY - h - skip, h)]
            return self.copy(2 + side, source, landing, peer["y", side])

        def c_copy(self, corner):
            n = 2 * corner[0] + corner[1]
            size = len(self.rows)
            return self.copy(4 + n, corner_out.at[self.slot, n, pl.ds(0, size)],
                             corner_in.at[self.slot, n, pl.ds(0, size)], beyond(corner))

        def pack(self):
            for corner in CORNERS if self.rows else ():
                for n, (i, j) in enumerate(self.rows):
                    x = WX + (i if corner[0] == 0 else bx - 1 - i)
                    y = WY + (j if corner[1] == 0 else by - 1 - j)
                    corner_out[self.slot, 2 * corner[0] + corner[1], n] = self.ref[x, y:y + 1, :]

        def each(self, axis, act, flip=False):
            if axis == "c":
                for corner in CORNERS if self.rows else ():
                    near = (1 - corner[0], 1 - corner[1]) if flip else corner

                    @pl.when(has["x", near[0]] & has["y", near[1]])
                    def _():
                        act(self.c_copy(corner), corner)
            elif axis in self.axes:
                for side in (0, 1):
                    @pl.when(has[axis, 1 - side if flip else side])
                    def _():
                        act((self.x_copy if axis == "x" else self.y_copy)(side), None)

        def unpack(self, copy, corner):
            copy.wait_recv()
            for n, (i, j) in enumerate(self.rows):
                x = WX + bx + i if corner[0] == 0 else WX - 1 - i
                y = WY + by + j if corner[1] == 0 else WY - 1 - j
                self.ref[x, y:y + 1, :] = corner_in[self.slot, 2 * corner[0] + corner[1], n]

    sent = []

    def start(halos):
        for h in halos:
            h.pack()
        for axis in "cxy":
            for h in halos:
                if axis == "x" and "x" in h.axes:
                    h.send_x()
                else:
                    h.each(axis, lambda c, _: c.start())
        sent.extend(halos)

    def arrive(halos, axes="yxc"):
        for axis in axes:
            for h in halos:
                h.each(axis, h.unpack if axis == "c" else lambda c, _: c.wait_recv(), flip=True)

    def forward(h, side):
        h.aside(side).wait_recv()
        h.onward(side).start()

    h_vel = [[Halo(0, v1.at[0], 2, 1, 2), Halo(1, v1.at[1], 1, 2, 2), Halo(2, v1.at[2], 1, 1)],
             [Halo(3, v2.at[0], 2, 1, 2), Halo(4, v2.at[1], 1, 2, 2), Halo(5, v2.at[2], 1, 1)]]
    h_p = [[Halo(6, pin1, WX, WX, WX)], [Halo(7, pin2, WX - 1, WX - 1, WX, skip=1, detour=1)]]
    near = SWEEPS // 2
    h_src = [[Halo(8, src1, near, SWEEPS, SWEEPS)], [Halo(9, src2, near, SWEEPS, SWEEPS)]]
    h_far = [[Halo(14, src1, SWEEPS - near, axes="x", skip=near)], [Halo(15, src2, SWEEPS - near, axes="x", skip=near)]]
    h_solid = [Halo(10, solid, 2, WX, 2)]
    h_rest = [Halo(13, solid, WX - 2, reach=WX, axes="x", skip=2, over=2, detour=0)]
    h_mf = [Halo(11, mf.at[0], 1, axes="x"), Halo(12, mf.at[1], rows=1, width=0, axes="y")]

    for fetch in fetches[3:]:
        fetch.wait()
    start(h_vel[0] + h_p[0])

    column_of = lax.broadcasted_iota(jnp.int32, (columns, slots), 0).astype(F32)
    depth_of = lax.broadcasted_iota(jnp.int32, (nz, slots), 0).astype(F32)
    dep[...] = jnp.zeros_like(dep)

    def where_of(b):
        cell = rk[b, 0:1, :]
        column = jnp.floor((cell + 0.5) * (1.0 / nz))
        return column, cell - column * nz

    def deposit(b, carry):
        column, level = where_of(b)
        hot_c = column == column_of
        hot_z = jnp.where(level == depth_of, 1.0, 0.0).astype(BF16)
        volume = rk[b, 1:2, :]
        values = [volume] + [volume * rk[b, 2 + d:3 + d, :] for d in range(3)]
        parts = [split(value) for value in values]
        both = None
        for side in (0, 1):
            left = jnp.concatenate([jnp.where(hot_c, part[side], 0.0).astype(BF16) for part in parts], axis=0)
            term = lax.dot_general(left, hot_z, (((1,), (1,)), ((), ())), preferred_element_type=F32)
            both = term if both is None else both + term
        dep[...] += both
        return carry

    deposit(iy, 0)

    def deposit_from(k, carry):
        incoming(k).wait_recv()
        return deposit(from_mate(k), carry)

    lax.fori_loop(1, n_gy, deposit_from, 0)
    solid[own_x, own_y, :] = dep[pl.ds(0, columns), :].reshape(bx, by, nz)
    for d in range(3):
        mf[d, own_x, own_y, :] = dep[pl.ds((1 + d) * columns, columns), :].reshape(bx, by, nz)
    start(h_solid + h_mf)
    start(h_rest)

    row = lax.broadcasted_iota(jnp.int32, (ey, nz), 0)
    depth = lax.broadcasted_iota(jnp.int32, (ey, nz), 1)
    row_in = jnp.where((row >= WY) | (iy > 0), 1.0, 0.0) * jnp.where((row < WY + by) | (iy < n_gy - 1), 1.0, 0.0)

    def voidage(x, carry):
        x_in = ((x >= WX) | (ix > 0)) & ((x < WX + bx) | (ix < n_gx - 1))
        eps[x] = jnp.maximum(1.0 - solid[x], FLOOR) * (row_in * jnp.where(x_in, 1.0, 0.0))
        return carry

    def sweep_over(act, spans, unroll):
        for first, end in spans:
            if first < end:
                lax.fori_loop(first, end, act, 0, unroll=min(unroll, end - first))

    low, high = WX, WX + bx

    def up_y(v):
        return pltpu.roll(v, ey - 1, 0)

    def down_y(v):
        return pltpu.roll(v, 1, 0)

    def up_z(v):
        return pltpu.roll(v, nz - 1, 1)

    def down_z(v):
        return pltpu.roll(v, 1, 1)

    last_z, first_z = depth == nz - 1, depth == 0

    def weights(x, carry):
        e = eps[x]
        near = [eps[x + 1], eps[x - 1], up_y(e), down_y(e),
                jnp.where(last_z, 0.0, up_z(e)), jnp.where(first_z, 0.0, down_z(e))]
        total = 0.5 * (6.0 * e + (((near[0] + near[1]) + (near[2] + near[3])) + (near[4] + near[5])))
        inside = e > 0.0
        inverse = jnp.where(inside, 0.5 / jnp.where(inside, total, 1.0), 0.0)
        for n in range(6):
            w = (e + near[n]) * inverse
            if n == 4:
                w = jnp.where(last_z, 0.0, w)
            if n == 5:
                w = jnp.where(first_z, 0.0, w)
            coef[n, x] = w
        coef[6, x] = 2.0 * inverse
        recip = 1.0 / jnp.where(inside, e, 1.0)
        rate[x] = (DT * VISC) * total * recip
        pull[x] = (DT * DRAG) * recip
        return carry

    def stencil(field, x):
        v = field[x]
        return v, (((coef[0, x] * field[x + 1] + coef[1, x] * field[x - 1])
                    + (coef[2, x] * up_y(v) + coef[3, x] * down_y(v)))
                   + (coef[4, x] * up_z(v) + coef[5, x] * down_z(v)))

    def wide(b, tables):
        column, level = where_of(b)
        hot = jnp.where(column == column_of, 1.0, 0.0).astype(BF16)
        found = jnp.dot(tables, jnp.concatenate([hot, hot], axis=0), preferred_element_type=F32)
        hot_z = level == depth_of
        return [jnp.sum(jnp.where(hot_z, found[n:n + nz], 0.0), axis=0, keepdims=True)
                for n in range(0, found.shape[0], nz)]

    def table(grid):
        high, low = split(grid.reshape(columns, nz).T)
        return jnp.concatenate([high.astype(BF16), low.astype(BF16)], axis=1)

    def porosity(b, carry):
        at, = wide(b, ft[pl.ds(3 * nz, nz), :])
        pull_of[b] = rk[b, 1:2, :] * DRAG / at
        return carry

    for step in range(STEPS):
        v = (v1, v2)[step]
        pin = (pin1, pin2)[step]
        src = (src1, src2)[step]

        def predict(x, carry):
            s, r, g, e = solid[x], rate[x], pull[x], eps[x]
            for d in range(3):
                old, mean = stencil(v.at[d], x)
                new = old + r * (mean - old) + g * (mf[d, x] - s * old)
                guess[d, x] = new
                flux[d, x] = e * new
            return carry

        def balance(x, carry):
            f1, f2 = flux[1, x], flux[2, x]
            out = ((flux[0, x + 1] - flux[0, x - 1]) + (up_y(f1) - down_y(f1))
                   + (jnp.where(last_z, 0.0, up_z(f2)) - jnp.where(first_z, 0.0, down_z(f2))))
            src[x, own_y, :] = (0.5 / DT) * out[WY:WY + by]
            return carry

        early = h_vel[step] + (h_solid + h_mf if step == 0 else [])
        arrive(early, "y")
        if step == 0:
            sweep_over(voidage, [(low, high)], 4)
            sweep_over(weights, [(low + 1, high - 1)], 3)
        sweep_over(predict, [(low + 1, high - 1)], 3)
        sweep_over(balance, [(low + near, high - near)], 4)
        start(h_far[step])
        for h in h_p[1] if step else h_rest:
            h.pass_on(forward)
        arrive(early, "xc")
        if step == 0:
            sweep_over(voidage, [(low - 2, low), (high, high + 2)], 2)
            sweep_over(weights, [(low - 1, low + 1), (high - 1, high + 1)], 2)
        sweep_over(predict, [(low - 1, low + 1), (high - 1, high + 1)], 2)
        sweep_over(balance, [(low, low + near), (high - near, high)], 2)
        start(h_src[step])
        arrive(h_src[step], "y")
        if step == 0:
            arrive(h_rest)
            sweep_over(voidage, [(0, low), (high, ex)], 5)
            sweep_over(weights, [(1, low + 1), (high - 1, ex - 1)], 5)
            arrive(h_p[step])
        else:
            arrive(h_p[step], "y")

        def scale(x, carry):
            sp[x] = src[x] * coef[6, x]
            return carry

        stages = [pin] + [(pa, pb)[sweep % 2] for sweep in range(SWEEPS)]

        def relaxing(sweep):
            held, into = stages[sweep], stages[sweep + 1]

            def relax(x, carry):
                _, mean = stencil(held, x)
                into[x] = mean - sp[x]
                return carry

            return relax

        inset = 0 if step == 0 else 1
        sweep_over(scale, [(low, high)], 8)
        for sweep in range(SWEEPS):
            sweep_over(relaxing(sweep), [(low + sweep + inset, high - sweep - inset)], 4)
        if step:
            ft[pl.ds(3 * nz, nz), :] = table(eps[own_x, own_y, :])
            lax.fori_loop(0, n_gy, porosity, 0)
            arrive(h_p[step], "xc")
        arrive(h_src[step], "xc")
        arrive(h_far[step])
        sweep_over(scale, [(1, low), (high, ex - 1)], 4)
        for sweep in range(SWEEPS):
            sweep_over(relaxing(sweep), [(1 + sweep, low + sweep + inset), (high - sweep - inset, ex - 1 - sweep)], 5)
        held = stages[SWEEPS]

        final = step == STEPS - 1

        def correct(x, carry):
            p = held[x]
            slopes = [held[x + 1] - held[x - 1], up_y(p) - down_y(p),
                      jnp.where(last_z, 0.0, up_z(p)) - jnp.where(first_z, 0.0, down_z(p))]
            for d in range(3):
                new = (guess[d, x] - (0.5 * DT) * slopes[d])[WY:WY + by]
                if final:
                    vel_out[d, x - WX] = new
                else:
                    v2[d, x, own_y, :] = new
            if final:
                p_out[x - WX] = p[WY:WY + by]
            else:
                for low, high in ((WY - 1, WY), (WY, WY + by), (WY + by, WY + by + 1)):
                    pin2[x, low:high, :] = p[low:high]
            return carry

        lax.fori_loop(WX, WX + bx, correct, 0, unroll=4)
        if not final:
            for x in (WX - 1, WX + bx):
                pin2[x, own_y, :] = held[x, own_y, :]
            start(h_vel[step + 1])
            start(h_p[step + 1])

    for d in range(3):
        ft[pl.ds(d * nz, nz), :] = table(vel_out[d])

    def gather(b, carry):
        at = wide(b, ft[pl.ds(0, 3 * nz), :])
        for d in range(3):
            dk[b, d:d + 1, :] = pull_of[b] * (at[d] - rk[b, 2 + d:3 + d, :])
        return carry

    def giving(k):
        return particles(k, dk.at[to_mate(k)], rd.at[iy], 1)

    def getting(k):
        return particles(k, dk.at[0], rd.at[from_mate(k)], 1)

    def gather_for(k, carry):
        gather(to_mate(n_gy - k), carry)
        giving(n_gy - k).start()
        return carry

    lax.fori_loop(1, n_gy, gather_for, 0)
    gather(iy, 0)
    rd[iy] = dk[iy]
    for h in sent:
        for axis in "xyc":
            h.each(axis, lambda c, _: c.wait_send())
        h.pass_on(lambda h, side: h.onward(side).wait_send())
    for k in range(1, n_gy):
        outgoing(k).wait_send()
        getting(k).wait_recv()
        giving(k).wait_send()
    for c in range(n_gy):
        for d in range(3):
            drag_out[d, pl.ds(c, 1), :] = rd[c, d:d + 1, :]


def deliver(*refs):
    pairs = len(refs) // 2
    copies = [pltpu.make_async_copy(refs[n], refs[pairs + n], refs[-1].at[n]) for n in range(pairs)]
    for copy in copies:
        copy.start()
    for copy in copies:
        copy.wait()


def solution(mesh):
    n_gx, n_gy = mesh.shape["gx"], mesh.shape["gy"]

    def per_device(velocity, pressure, part_cell, part_count, grain_velocities, part_vol):
        bx, by, nz = pressure.shape
        slots = part_vol.shape[-1]
        ext = (bx + 2 * WX, by + 2 * WY, nz)
        vmem = pl.BlockSpec(memory_space=pltpu.VMEM)
        anywhere = pl.BlockSpec(memory_space=pl.ANY)

        def field(*lead):
            return pltpu.VMEM(lead + ext, F32)

        def kernel(*refs):
            body(n_gx, n_gy, *refs)

        v, p, drag = pl.pallas_call(
            kernel,
            name="interval",
            out_shape=(
                pltpu.VMEM(velocity.shape, F32),
                pltpu.VMEM(pressure.shape, F32),
                pltpu.VMEM((3, n_gy, slots), F32),
            ),
            in_specs=[pl.BlockSpec(memory_space=pltpu.SMEM)] + [anywhere] * 5,
            out_specs=(vmem,) * 3,
            scratch_shapes=[
                pltpu.VMEM((n_gy, slots), jnp.int32),
                pltpu.VMEM((3, n_gy, slots), F32),
                pltpu.VMEM((n_gy, slots), F32),
                pltpu.SemaphoreType.DMA((7,)),
                field(3), field(3), field(), field(), field(), field(), field(), field(), field(),
                field(), field(3), field(), field(7), field(), field(), field(3), field(3),
                pltpu.VMEM((4 * bx * by, nz), F32),
                pltpu.VMEM((n_gy, ROWS, slots), F32),
                pltpu.VMEM((n_gy, ROWS, slots), F32),
                pltpu.VMEM((n_gy, 3, slots), F32),
                pltpu.VMEM((n_gy, 3, slots), F32),
                pltpu.VMEM((4 * nz, 2 * bx * by), BF16),
                pltpu.VMEM((n_gy, 1, slots), F32),
                pltpu.VMEM((16, 4, WX * (WX - 1) // 2, 1, nz), F32),
                pltpu.VMEM((16, 4, WX * (WX - 1) // 2, 1, nz), F32),
                pltpu.VMEM((2, WX, by, nz), F32),
                pltpu.SemaphoreType.DMA((2,)),
                pltpu.SemaphoreType.DMA((2,)),
                pltpu.SemaphoreType.DMA((16, 8)),
                pltpu.SemaphoreType.DMA((16, 8)),
                pltpu.SemaphoreType.DMA((2, n_gy)),
                pltpu.SemaphoreType.DMA((2, n_gy)),
            ],
            compiler_params=pltpu.CompilerParams(
                collective_id=0, has_side_effects=True, vmem_limit_bytes=56 * 1024 * 1024
            ),
        )(
            part_count.reshape(n_gy),
            velocity,
            pressure,
            part_cell.reshape(n_gy, slots),
            grain_velocities.reshape(n_gy, 3, slots).transpose(1, 0, 2),
            part_vol.reshape(n_gy, slots),
        )
        v, p, drag = [pltpu.with_memory_space_constraint(a, pltpu.VMEM) for a in (v, p, drag)]
        v, p, drag = pl.pallas_call(
            deliver,
            name="deliver",
            out_shape=tuple(jax.ShapeDtypeStruct(a.shape, F32) for a in (v, p, drag)),
            in_specs=(vmem,) * 3,
            out_specs=(anywhere,) * 3,
            scratch_shapes=[pltpu.SemaphoreType.DMA((3,))],
        )(v, p, drag)
        return v, p, drag.transpose(1, 0, 2).reshape(grain_velocities.shape)

    placed = (
        P(None, "gx", "gy", None),
        P("gx", "gy", None),
        P("gx", "gy", None, None),
        P("gx", "gy", None),
        P("gx", "gy", None, None, None),
        P("gx", "gy", None, None),
    )
    return jax.shard_map(
        per_device,
        mesh=mesh,
        in_specs=placed,
        out_specs=(P(None, "gx", "gy", None), P("gx", "gy", None), P("gx", "gy", None, None, None)),
        check_vma=False,
    )
```

```python
import jax
import jax.numpy as jnp
from jax import lax
from jax.experimental import pallas as pl
from jax.experimental.pallas import tpu as pltpu
from jax.sharding import PartitionSpec as P

STEPS = 2
SWEEPS = 4
DRAG = 2.0
DT = 0.25
VISC = 0.2
FLOOR = 0.4

WX = SWEEPS + 1
WY = 8
ROWS = 5

MESH = pl.DeviceIdType.MESH
CORNERS = ((0, 0), (0, 1), (1, 0), (1, 1))
F32 = jnp.float32
BF16 = jnp.bfloat16


def split(value):
    high = value.astype(BF16).astype(F32)
    return high, value - high


def mate(i, k, n):
    if n & (n - 1):
        return lax.rem(i + k, n)
    bit, flip = 1, 0
    while bit < n:
        flip = flip + bit * ((i // bit + k // bit) % 2)
        bit *= 2
    return flip


def body(n_gx, n_gy, count_ref, vel_hbm, p_hbm, cell_hbm, gv_hbm, vol_hbm,
         vel_out, p_out, drag_out, cell_ref, gv_ref, vol_ref, fetch_sem,
         v1, v2, pin1, pin2, pa, pb, src1, src2, sp, solid, mf, eps, coef, rate, pull,
         guess, flux, dep, pk, rk, dk, rd, ft, pull_of, corner_out, corner_in, passed, aside_send, aside_recv,
         field_send, field_recv, part_send, part_recv):
    bx, by, nz = p_hbm.shape
    ex, ey = bx + 2 * WX, by + 2 * WY
    slots = vol_hbm.shape[-1]
    columns = bx * by
    ix, iy = lax.axis_index("gx"), lax.axis_index("gy")
    has = {("x", 0): ix > 0, ("x", 1): ix < n_gx - 1, ("y", 0): iy > 0, ("y", 1): iy < n_gy - 1}
    peer = {("x", 0): (ix - 1, iy), ("x", 1): (ix + 1, iy), ("y", 0): (ix, iy - 1), ("y", 1): (ix, iy + 1)}
    own_x, own_y = pl.ds(WX, bx), pl.ds(WY, by)

    def to_mate(k):
        return mate(iy, k, n_gy)

    def from_mate(k):
        return to_mate(k) if n_gy & (n_gy - 1) == 0 else lax.rem(iy + n_gy - k, n_gy)

    def beyond(corner):
        return ix + (2 * corner[0] - 1), iy + (2 * corner[1] - 1)

    barrier = pltpu.get_barrier_semaphore()
    for k in range(1, n_gy):
        pl.semaphore_signal(barrier, inc=1, device_id=(ix, to_mate(k)), device_id_type=MESH)
    for side in (0, 1):
        @pl.when(has["x", side])
        def _():
            pl.semaphore_signal(barrier, inc=1, device_id=peer["x", side], device_id_type=MESH)
    for corner in CORNERS:
        @pl.when(has["x", corner[0]] & has["y", corner[1]])
        def _():
            pl.semaphore_signal(barrier, inc=1, device_id=beyond(corner), device_id_type=MESH)

    square = n_gx == 4
    origin, middle, target = (2, 1), (0, 3), (1, 2)
    if square:
        for side in (0, 1):
            @pl.when(ix == middle[side])
            def _():
                pl.semaphore_signal(barrier, inc=1, device_id=(origin[side], iy), device_id_type=MESH)

    fetches = [(cell_hbm, cell_ref), (vol_hbm, vol_ref), (gv_hbm, gv_ref)]
    fetches += [(vel_hbm.at[d], v1.at[d, own_x, own_y]) for d in range(3)] + [(p_hbm, pin1.at[own_x, own_y])]
    fetches = [pltpu.make_async_copy(source, landing, fetch_sem.at[n]) for n, (source, landing) in enumerate(fetches)]
    for fetch in fetches:
        fetch.start()

    fields = [v1.at[d] for d in range(3)] + [v2.at[d] for d in range(3)] + [mf.at[d] for d in range(3)]
    fields += [pin1, pin2, src1, src2, solid]
    for side in (0, 1):
        @pl.when(jnp.logical_not(has["x", side]))
        def _():
            for field in fields:
                at = 0 if side == 0 else WX + bx
                field[pl.ds(at, WX)] = jnp.zeros((WX, ey, nz), F32)

        @pl.when(jnp.logical_not(has["y", side]))
        def _():
            for field in fields:
                at = 0 if side == 0 else WY + by
                field[:, pl.ds(at, WY), :] = jnp.zeros((ex, WY, nz), F32)

    for fetch in fetches[:3]:
        fetch.wait()
    slot = lax.broadcasted_iota(jnp.int32, (1, slots), 1)
    for c in range(n_gy):
        pk[c, 0:1, :] = cell_ref[pl.ds(c, 1), :].astype(F32)
        pk[c, 1:2, :] = jnp.where(slot < count_ref[c], vol_ref[pl.ds(c, 1), :], 0.0)
        for d in range(3):
            pk[c, 2 + d:3 + d, :] = gv_ref[d, pl.ds(c, 1), :]

    x_peers = jnp.where(ix > 0, 1, 0) + jnp.where(ix < n_gx - 1, 1, 0)
    y_peers = jnp.where(iy > 0, 1, 0) + jnp.where(iy < n_gy - 1, 1, 0)
    detours = jnp.where((ix == 1) | (ix == 2), 1, 0) if square else 0
    pl.semaphore_wait(barrier, n_gy - 1 + x_peers * (1 + y_peers) + detours)

    def particles(k, source, landing, bank):
        return pltpu.make_async_remote_copy(
            src_ref=source, dst_ref=landing, send_sem=part_send.at[bank, k], recv_sem=part_recv.at[bank, k],
            device_id=(ix, to_mate(k)), device_id_type=MESH)

    def outgoing(k):
        return particles(k, pk.at[to_mate(k)], rk.at[iy], 0)

    def incoming(k):
        return particles(k, pk.at[0], rk.at[from_mate(k)], 0)

    for k in range(n_gy - 1, 0, -1):
        outgoing(k).start()
    rk[iy] = pk[iy]

    class Halo:
        def __init__(self, slot, ref, width, rows=0, reach=0, axes="xy", skip=0, over=0, detour=None):
            self.slot, self.ref, self.width, self.span, self.axes, self.skip = slot, ref, width, rows, axes, skip
            self.detour = detour if square else None
            self.rows = [(i, j) for i in range(reach) for j in range(reach) if over < i + j + 2 <= reach]

        def copy(self, index, source, landing, to):
            return pltpu.make_async_remote_copy(
                src_ref=source, dst_ref=landing, send_sem=field_send.at[self.slot, index],
                recv_sem=field_recv.at[self.slot, index], device_id=to, device_id_type=MESH)

        def x_copy(self, side):
            w, skip = self.width, self.skip
            at = skip if side == 0 else bx - w - skip
            source = self.ref.at[pl.ds(WX + at, w), own_y]
            landing = self.ref.at[pl.ds(WX + bx + skip if side == 0 else WX - w - skip, w), own_y]
            return self.copy(side, source, landing, peer["x", side])

        def aside(self, side):
            held = passed.at[self.detour, pl.ds(0, self.width)]
            at = self.skip if side == 0 else bx - self.width - self.skip
            return pltpu.make_async_remote_copy(
                src_ref=self.ref.at[pl.ds(WX + at, self.width), own_y], dst_ref=held,
                send_sem=field_send.at[self.slot, side], recv_sem=aside_recv.at[self.detour],
                device_id=(middle[side], iy), device_id_type=MESH)

        def onward(self, side):
            landing = WX + bx + self.skip if side == 0 else WX - self.width - self.skip
            return pltpu.make_async_remote_copy(
                src_ref=passed.at[self.detour, pl.ds(0, self.width)],
                dst_ref=self.ref.at[pl.ds(landing, self.width), own_y],
                send_sem=aside_send.at[self.detour], recv_sem=field_recv.at[self.slot, side],
                device_id=(target[side], iy), device_id_type=MESH)

        def send_x(self):
            for side in (0, 1):
                straight = has["x", side]
                if self.detour is not None:
                    straight = straight & (ix != origin[side])

                    @pl.when(ix == origin[side])
                    def _():
                        self.aside(side).start()

                @pl.when(straight)
                def _():
                    self.x_copy(side).start()

        def pass_on(self, act):
            for side in (0, 1) if self.detour is not None else ():
                @pl.when(ix == middle[side])
                def _():
                    act(self, side)

        def y_copy(self, side):
            h, skip = self.span, self.skip
            source = self.ref.at[own_x, pl.ds(WY + skip if side == 0 else WY + by - h - skip, h)]
            landing = self.ref.at[own_x, pl.ds(WY + by + skip if side == 0 else WY - h - skip, h)]
            return self.copy(2 + side, source, landing, peer["y", side])

        def c_copy(self, corner):
            n = 2 * corner[0] + corner[1]
            size = len(self.rows)
            return self.copy(4 + n, corner_out.at[self.slot, n, pl.ds(0, size)],
                             corner_in.at[self.slot, n, pl.ds(0, size)], beyond(corner))

        def pack(self):
            for corner in CORNERS if self.rows else ():
                for n, (i, j) in enumerate(self.rows):
                    x = WX + (i if corner[0] == 0 else bx - 1 - i)
                    y = WY + (j if corner[1] == 0 else by - 1 - j)
                    corner_out[self.slot, 2 * corner[0] + corner[1], n] = self.ref[x, y:y + 1, :]

        def each(self, axis, act, flip=False):
            if axis == "c":
                for corner in CORNERS if self.rows else ():
                    near = (1 - corner[0], 1 - corner[1]) if flip else corner

                    @pl.when(has["x", near[0]] & has["y", near[1]])
                    def _():
                        act(self.c_copy(corner), corner)
            elif axis in self.axes:
                for side in (0, 1):
                    @pl.when(has[axis, 1 - side if flip else side])
                    def _():
                        act((self.x_copy if axis == "x" else self.y_copy)(side), None)

        def unpack(self, copy, corner):
            copy.wait_recv()
            for n, (i, j) in enumerate(self.rows):
                x = WX + bx + i if corner[0] == 0 else WX - 1 - i
                y = WY + by + j if corner[1] == 0 else WY - 1 - j
                self.ref[x, y:y + 1, :] = corner_in[self.slot, 2 * corner[0] + corner[1], n]

    sent = []

    def start(halos):
        for h in halos:
            h.pack()
        for axis in "cxy":
            for h in halos:
                if axis == "x" and "x" in h.axes:
                    h.send_x()
                else:
                    h.each(axis, lambda c, _: c.start())
        sent.extend(halos)

    def arrive(halos, axes="yxc"):
        for axis in axes:
            for h in halos:
                h.each(axis, h.unpack if axis == "c" else lambda c, _: c.wait_recv(), flip=True)

    def forward(h, side):
        h.aside(side).wait_recv()
        h.onward(side).start()

    h_vel = [[Halo(0, v1.at[0], 2, 1, 2), Halo(1, v1.at[1], 1, 2, 2), Halo(2, v1.at[2], 1, 1)],
             [Halo(3, v2.at[0], 2, 1, 2), Halo(4, v2.at[1], 1, 2, 2), Halo(5, v2.at[2], 1, 1)]]
    h_p = [[Halo(6, pin1, WX, WX, WX)], [Halo(7, pin2, WX - 1, WX - 1, WX, skip=1, detour=1)]]
    near = SWEEPS // 2
    h_src = [[Halo(8, src1, near, SWEEPS, SWEEPS)], [Halo(9, src2, near, SWEEPS, SWEEPS)]]
    h_far = [[Halo(14, src1, SWEEPS - near, axes="x", skip=near)], [Halo(15, src2, SWEEPS - near, axes="x", skip=near)]]
    h_solid = [Halo(10, solid, 2, WX, 2)]
    h_rest = [Halo(13, solid, WX - 2, reach=WX, axes="x", skip=2, over=2, detour=0)]
    h_mf = [Halo(11, mf.at[0], 1, axes="x"), Halo(12, mf.at[1], rows=1, width=0, axes="y")]

    for fetch in fetches[3:]:
        fetch.wait()
    start(h_vel[0] + h_p[0])

    column_of = lax.broadcasted_iota(jnp.int32, (columns, slots), 0).astype(F32)
    depth_of = lax.broadcasted_iota(jnp.int32, (nz, slots), 0).astype(F32)
    dep[...] = jnp.zeros_like(dep)

    def where_of(b):
        cell = rk[b, 0:1, :]
        column = jnp.floor((cell + 0.5) * (1.0 / nz))
        return column, cell - column * nz

    def deposit(b, carry):
        column, level = where_of(b)
        hot_c = column == column_of
        hot_z = jnp.where(level == depth_of, 1.0, 0.0).astype(BF16)
        volume = rk[b, 1:2, :]
        values = [volume] + [volume * rk[b, 2 + d:3 + d, :] for d in range(3)]
        parts = [split(value) for value in values]
        both = None
        for side in (0, 1):
            left = jnp.concatenate([jnp.where(hot_c, part[side], 0.0).astype(BF16) for part in parts], axis=0)
            term = lax.dot_general(left, hot_z, (((1,), (1,)), ((), ())), preferred_element_type=F32)
            both = term if both is None else both + term
        dep[...] += both
        return carry

    deposit(iy, 0)

    def deposit_from(k, carry):
        incoming(k).wait_recv()
        return deposit(from_mate(k), carry)

    lax.fori_loop(1, n_gy, deposit_from, 0)
    solid[own_x, own_y, :] = dep[pl.ds(0, columns), :].reshape(bx, by, nz)
    for d in range(3):
        mf[d, own_x, own_y, :] = dep[pl.ds((1 + d) * columns, columns), :].reshape(bx, by, nz)
    start(h_solid + h_mf)
    start(h_rest)

    row = lax.broadcasted_iota(jnp.int32, (ey, nz), 0)
    depth = lax.broadcasted_iota(jnp.int32, (ey, nz), 1)
    row_in = jnp.where((row >= WY) | (iy > 0), 1.0, 0.0) * jnp.where((row < WY + by) | (iy < n_gy - 1), 1.0, 0.0)

    def voidage(x, carry):
        x_in = ((x >= WX) | (ix > 0)) & ((x < WX + bx) | (ix < n_gx - 1))
        eps[x] = jnp.maximum(1.0 - solid[x], FLOOR) * (row_in * jnp.where(x_in, 1.0, 0.0))
        return carry

    def sweep_over(act, spans, unroll):
        for first, end in spans:
            if first < end:
                lax.fori_loop(first, end, act, 0, unroll=min(2 * unroll, end - first))

    low, high = WX, WX + bx

    def up_y(v):
        return pltpu.roll(v, ey - 1, 0)

    def down_y(v):
        return pltpu.roll(v, 1, 0)

    def up_z(v):
        return pltpu.roll(v, nz - 1, 1)

    def down_z(v):
        return pltpu.roll(v, 1, 1)

    last_z, first_z = depth == nz - 1, depth == 0

    def weights(x, carry):
        e = eps[x]
        near = [eps[x + 1], eps[x - 1], up_y(e), down_y(e),
                jnp.where(last_z, 0.0, up_z(e)), jnp.where(first_z, 0.0, down_z(e))]
        total = 0.5 * (6.0 * e + (((near[0] + near[1]) + (near[2] + near[3])) + (near[4] + near[5])))
        inside = e > 0.0
        inverse = jnp.where(inside, 0.5 / jnp.where(inside, total, 1.0), 0.0)
        for n in range(6):
            w = (e + near[n]) * inverse
            if n == 4:
                w = jnp.where(last_z, 0.0, w)
            if n == 5:
                w = jnp.where(first_z, 0.0, w)
            coef[n, x] = w
        coef[6, x] = 2.0 * inverse
        recip = 1.0 / jnp.where(inside, e, 1.0)
        rate[x] = (DT * VISC) * total * recip
        pull[x] = (DT * DRAG) * recip
        return carry

    def stencil(field, x):
        v = field[x]
        return v, (((coef[0, x] * field[x + 1] + coef[1, x] * field[x - 1])
                    + (coef[2, x] * up_y(v) + coef[3, x] * down_y(v)))
                   + (coef[4, x] * up_z(v) + coef[5, x] * down_z(v)))

    def wide(b, tables):
        column, level = where_of(b)
        hot = jnp.where(column == column_of, 1.0, 0.0).astype(BF16)
        found = jnp.dot(tables, jnp.concatenate([hot, hot], axis=0), preferred_element_type=F32)
        hot_z = level == depth_of
        return [jnp.sum(jnp.where(hot_z, found[n:n + nz], 0.0), axis=0, keepdims=True)
                for n in range(0, found.shape[0], nz)]

    def table(grid):
        high, low = split(grid.reshape(columns, nz).T)
        return jnp.concatenate([high.astype(BF16), low.astype(BF16)], axis=1)

    def porosity(b, carry):
        at, = wide(b, ft[pl.ds(3 * nz, nz), :])
        pull_of[b] = rk[b, 1:2, :] * DRAG / at
        return carry

    for step in range(STEPS):
        v = (v1, v2)[step]
        pin = (pin1, pin2)[step]
        src = (src1, src2)[step]

        def predict(x, carry):
            s, r, g, e = solid[x], rate[x], pull[x], eps[x]
            for d in range(3):
                old, mean = stencil(v.at[d], x)
                new = old + r * (mean - old) + g * (mf[d, x] - s * old)
                guess[d, x] = new
                flux[d, x] = e * new
            return carry

        def balance(x, carry):
            f1, f2 = flux[1, x], flux[2, x]
            out = ((flux[0, x + 1] - flux[0, x - 1]) + (up_y(f1) - down_y(f1))
                   + (jnp.where(last_z, 0.0, up_z(f2)) - jnp.where(first_z, 0.0, down_z(f2))))
            src[x, own_y, :] = (0.5 / DT) * out[WY:WY + by]
            return carry

        early = h_vel[step] + (h_solid + h_mf if step == 0 else [])
        arrive(early, "y")
        if step == 0:
            sweep_over(voidage, [(low, high)], 4)
            sweep_over(weights, [(low + 1, high - 1)], 3)
        sweep_over(predict, [(low + 1, high - 1)], 3)
        sweep_over(balance, [(low + near, high - near)], 4)
        start(h_far[step])
        for h in h_p[1] if step else h_rest:
            h.pass_on(forward)
        arrive(early, "xc")
        if step == 0:
            sweep_over(voidage, [(low - 2, low), (high, high + 2)], 2)
            sweep_over(weights, [(low - 1, low + 1), (high - 1, high + 1)], 2)
        sweep_over(predict, [(low - 1, low + 1), (high - 1, high + 1)], 2)
        sweep_over(balance, [(low, low + near), (high - near, high)], 2)
        start(h_src[step])
        arrive(h_src[step], "y")
        if step == 0:
            arrive(h_rest)
            sweep_over(voidage, [(0, low), (high, ex)], 5)
            sweep_over(weights, [(1, low + 1), (high - 1, ex - 1)], 5)
            arrive(h_p[step])
        else:
            arrive(h_p[step], "y")

        def scale(x, carry):
            sp[x] = src[x] * coef[6, x]
            return carry

        stages = [pin] + [(pa, pb)[sweep % 2] for sweep in range(SWEEPS)]

        def relaxing(sweep):
            held, into = stages[sweep], stages[sweep + 1]

            def relax(x, carry):
                _, mean = stencil(held, x)
                into[x] = mean - sp[x]
                return carry

            return relax

        inset = 0 if step == 0 else 1
        sweep_over(scale, [(low, high)], 8)
        for sweep in range(SWEEPS):
            sweep_over(relaxing(sweep), [(low + sweep + inset, high - sweep - inset)], 4)
        if step:
            ft[pl.ds(3 * nz, nz), :] = table(eps[own_x, own_y, :])
            lax.fori_loop(0, n_gy, porosity, 0)
            arrive(h_p[step], "xc")
        arrive(h_src[step], "xc")
        arrive(h_far[step])
        sweep_over(scale, [(1, low), (high, ex - 1)], 4)
        for sweep in range(SWEEPS):
            sweep_over(relaxing(sweep), [(1 + sweep, low + sweep + inset), (high - sweep - inset, ex - 1 - sweep)], 5)
        held = stages[SWEEPS]

        final = step == STEPS - 1

        def correct(x, carry):
            p = held[x]
            slopes = [held[x + 1] - held[x - 1], up_y(p) - down_y(p),
                      jnp.where(last_z, 0.0, up_z(p)) - jnp.where(first_z, 0.0, down_z(p))]
            for d in range(3):
                new = (guess[d, x] - (0.5 * DT) * slopes[d])[WY:WY + by]
                if final:
                    vel_out[d, x - WX] = new
                else:
                    v2[d, x, own_y, :] = new
            if final:
                p_out[x - WX] = p[WY:WY + by]
            else:
                for low, high in ((WY - 1, WY), (WY, WY + by), (WY + by, WY + by + 1)):
                    pin2[x, low:high, :] = p[low:high]
            return carry

        lax.fori_loop(WX, WX + bx, correct, 0, unroll=8)
        if not final:
            for x in (WX - 1, WX + bx):
                pin2[x, own_y, :] = held[x, own_y, :]
            start(h_vel[step + 1])
            start(h_p[step + 1])

    for d in range(3):
        ft[pl.ds(d * nz, nz), :] = table(vel_out[d])

    def gather(b, carry):
        at = wide(b, ft[pl.ds(0, 3 * nz), :])
        for d in range(3):
            dk[b, d:d + 1, :] = pull_of[b] * (at[d] - rk[b, 2 + d:3 + d, :])
        return carry

    def giving(k):
        return particles(k, dk.at[to_mate(k)], rd.at[iy], 1)

    def getting(k):
        return particles(k, dk.at[0], rd.at[from_mate(k)], 1)

    def gather_for(k, carry):
        gather(to_mate(n_gy - k), carry)
        giving(n_gy - k).start()
        return carry

    lax.fori_loop(1, n_gy, gather_for, 0)
    gather(iy, 0)
    rd[iy] = dk[iy]
    for h in sent:
        for axis in "xyc":
            h.each(axis, lambda c, _: c.wait_send())
        h.pass_on(lambda h, side: h.onward(side).wait_send())
    for k in range(1, n_gy):
        outgoing(k).wait_send()
        getting(k).wait_recv()
        giving(k).wait_send()
    for c in range(n_gy):
        for d in range(3):
            drag_out[d, pl.ds(c, 1), :] = rd[c, d:d + 1, :]


def deliver(*refs):
    pairs = len(refs) // 2
    copies = [pltpu.make_async_copy(refs[n], refs[pairs + n], refs[-1].at[n]) for n in range(pairs)]
    for copy in copies:
        copy.start()
    for copy in copies:
        copy.wait()


def solution(mesh):
    n_gx, n_gy = mesh.shape["gx"], mesh.shape["gy"]

    def per_device(velocity, pressure, part_cell, part_count, grain_velocities, part_vol):
        bx, by, nz = pressure.shape
        slots = part_vol.shape[-1]
        ext = (bx + 2 * WX, by + 2 * WY, nz)
        vmem = pl.BlockSpec(memory_space=pltpu.VMEM)
        anywhere = pl.BlockSpec(memory_space=pl.ANY)

        def field(*lead):
            return pltpu.VMEM(lead + ext, F32)

        def kernel(*refs):
            body(n_gx, n_gy, *refs)

        v, p, drag = pl.pallas_call(
            kernel,
            name="interval",
            out_shape=(
                pltpu.VMEM(velocity.shape, F32),
                pltpu.VMEM(pressure.shape, F32),
                pltpu.VMEM((3, n_gy, slots), F32),
            ),
            in_specs=[pl.BlockSpec(memory_space=pltpu.SMEM)] + [anywhere] * 5,
            out_specs=(vmem,) * 3,
            scratch_shapes=[
                pltpu.VMEM((n_gy, slots), jnp.int32),
                pltpu.VMEM((3, n_gy, slots), F32),
                pltpu.VMEM((n_gy, slots), F32),
                pltpu.SemaphoreType.DMA((7,)),
                field(3), field(3), field(), field(), field(), field(), field(), field(), field(),
                field(), field(3), field(), field(7), field(), field(), field(3), field(3),
                pltpu.VMEM((4 * bx * by, nz), F32),
                pltpu.VMEM((n_gy, ROWS, slots), F32),
                pltpu.VMEM((n_gy, ROWS, slots), F32),
                pltpu.VMEM((n_gy, 3, slots), F32),
                pltpu.VMEM((n_gy, 3, slots), F32),
                pltpu.VMEM((4 * nz, 2 * bx * by), BF16),
                pltpu.VMEM((n_gy, 1, slots), F32),
                pltpu.VMEM((16, 4, WX * (WX - 1) // 2, 1, nz), F32),
                pltpu.VMEM((16, 4, WX * (WX - 1) // 2, 1, nz), F32),
                pltpu.VMEM((2, WX, by, nz), F32),
                pltpu.SemaphoreType.DMA((2,)),
                pltpu.SemaphoreType.DMA((2,)),
                pltpu.SemaphoreType.DMA((16, 8)),
                pltpu.SemaphoreType.DMA((16, 8)),
                pltpu.SemaphoreType.DMA((2, n_gy)),
                pltpu.SemaphoreType.DMA((2, n_gy)),
            ],
            compiler_params=pltpu.CompilerParams(
                collective_id=0, has_side_effects=True, vmem_limit_bytes=56 * 1024 * 1024
            ),
        )(
            part_count.reshape(n_gy),
            velocity,
            pressure,
            part_cell.reshape(n_gy, slots),
            grain_velocities.reshape(n_gy, 3, slots).transpose(1, 0, 2),
            part_vol.reshape(n_gy, slots),
        )
        v, p, drag = [pltpu.with_memory_space_constraint(a, pltpu.VMEM) for a in (v, p, drag)]
        v, p, drag = pl.pallas_call(
            deliver,
            name="deliver",
            out_shape=tuple(jax.ShapeDtypeStruct(a.shape, F32) for a in (v, p, drag)),
            in_specs=(vmem,) * 3,
            out_specs=(anywhere,) * 3,
            scratch_shapes=[pltpu.SemaphoreType.DMA((3,))],
        )(v, p, drag)
        return v, p, drag.transpose(1, 0, 2).reshape(grain_velocities.shape)

    placed = (
        P(None, "gx", "gy", None),
        P("gx", "gy", None),
        P("gx", "gy", None, None),
        P("gx", "gy", None),
        P("gx", "gy", None, None, None),
        P("gx", "gy", None, None),
    )
    return jax.shard_map(
        per_device,
        mesh=mesh,
        in_specs=placed,
        out_specs=(P(None, "gx", "gy", None), P("gx", "gy", None), P("gx", "gy", None, None, None)),
        check_vma=False,
    )
```

```python
import jax
import jax.numpy as jnp
from jax import lax
from jax.experimental import pallas as pl
from jax.experimental.pallas import tpu as pltpu
from jax.sharding import PartitionSpec as P

STEPS = 2
SWEEPS = 4
DRAG = 2.0
DT = 0.25
VISC = 0.2
FLOOR = 0.4

WX = SWEEPS + 1
WY = 8
ROWS = 5

MESH = pl.DeviceIdType.MESH
CORNERS = ((0, 0), (0, 1), (1, 0), (1, 1))
F32 = jnp.float32
BF16 = jnp.bfloat16


def split(value):
    high = value.astype(BF16).astype(F32)
    return high, value - high


def mate(i, k, n):
    if n & (n - 1):
        return lax.rem(i + k, n)
    bit, flip = 1, 0
    while bit < n:
        flip = flip + bit * ((i // bit + k // bit) % 2)
        bit *= 2
    return flip


def body(n_gx, n_gy, count_ref, vel_hbm, p_hbm, cell_hbm, gv_hbm, vol_hbm,
         vel_out, p_out, drag_out, cell_ref, gv_ref, vol_ref, fetch_sem,
         v1, v2, pin1, pin2, pa, pb, src1, src2, sp, solid, mf, eps, coef, rate, pull,
         guess, flux, dep, pk, rk, dk, rd, ft, pull_of, corner_out, corner_in, passed, aside_send, aside_recv,
         field_send, field_recv, part_send, part_recv):
    bx, by, nz = p_hbm.shape
    ex, ey = bx + 2 * WX, by + 2 * WY
    slots = vol_hbm.shape[-1]
    columns = bx * by
    ix, iy = lax.axis_index("gx"), lax.axis_index("gy")
    has = {("x", 0): ix > 0, ("x", 1): ix < n_gx - 1, ("y", 0): iy > 0, ("y", 1): iy < n_gy - 1}
    peer = {("x", 0): (ix - 1, iy), ("x", 1): (ix + 1, iy), ("y", 0): (ix, iy - 1), ("y", 1): (ix, iy + 1)}
    own_x, own_y = pl.ds(WX, bx), pl.ds(WY, by)

    def to_mate(k):
        return mate(iy, k, n_gy)

    def from_mate(k):
        return to_mate(k) if n_gy & (n_gy - 1) == 0 else lax.rem(iy + n_gy - k, n_gy)

    def beyond(corner):
        return ix + (2 * corner[0] - 1), iy + (2 * corner[1] - 1)

    fetches = [(cell_hbm, cell_ref), (vol_hbm, vol_ref), (gv_hbm, gv_ref)]
    fetches += [(vel_hbm.at[d], v1.at[d, own_x, own_y]) for d in range(3)] + [(p_hbm, pin1.at[own_x, own_y])]
    fetches = [pltpu.make_async_copy(source, landing, fetch_sem.at[n]) for n, (source, landing) in enumerate(fetches)]
    for fetch in fetches:
        fetch.start()

    barrier = pltpu.get_barrier_semaphore()
    for k in range(1, n_gy):
        pl.semaphore_signal(barrier, inc=1, device_id=(ix, to_mate(k)), device_id_type=MESH)
    for side in (0, 1):
        @pl.when(has["x", side])
        def _():
            pl.semaphore_signal(barrier, inc=1, device_id=peer["x", side], device_id_type=MESH)
    for corner in CORNERS:
        @pl.when(has["x", corner[0]] & has["y", corner[1]])
        def _():
            pl.semaphore_signal(barrier, inc=1, device_id=beyond(corner), device_id_type=MESH)

    square = n_gx == 4
    origin, middle, target = (2, 1), (0, 3), (1, 2)
    if square:
        for side in (0, 1):
            @pl.when(ix == middle[side])
            def _():
                pl.semaphore_signal(barrier, inc=1, device_id=(origin[side], iy), device_id_type=MESH)


    fields = [v1.at[d] for d in range(3)] + [v2.at[d] for d in range(3)] + [mf.at[d] for d in range(3)]
    fields += [pin1, pin2, src1, src2, solid]
    for side in (0, 1):
        @pl.when(jnp.logical_not(has["x", side]))
        def _():
            for field in fields:
                at = 0 if side == 0 else WX + bx
                field[pl.ds(at, WX)] = jnp.zeros((WX, ey, nz), F32)

        @pl.when(jnp.logical_not(has["y", side]))
        def _():
            for field in fields:
                at = 0 if side == 0 else WY + by
                field[:, pl.ds(at, WY), :] = jnp.zeros((ex, WY, nz), F32)

    for fetch in fetches[:3]:
        fetch.wait()
    slot = lax.broadcasted_iota(jnp.int32, (1, slots), 1)
    for c in range(n_gy):
        pk[c, 0:1, :] = cell_ref[pl.ds(c, 1), :].astype(F32)
        pk[c, 1:2, :] = jnp.where(slot < count_ref[c], vol_ref[pl.ds(c, 1), :], 0.0)
        for d in range(3):
            pk[c, 2 + d:3 + d, :] = gv_ref[d, pl.ds(c, 1), :]

    x_peers = jnp.where(ix > 0, 1, 0) + jnp.where(ix < n_gx - 1, 1, 0)
    y_peers = jnp.where(iy > 0, 1, 0) + jnp.where(iy < n_gy - 1, 1, 0)
    detours = jnp.where((ix == 1) | (ix == 2), 1, 0) if square else 0
    pl.semaphore_wait(barrier, n_gy - 1 + x_peers * (1 + y_peers) + detours)

    def particles(k, source, landing, bank):
        return pltpu.make_async_remote_copy(
            src_ref=source, dst_ref=landing, send_sem=part_send.at[bank, k], recv_sem=part_recv.at[bank, k],
            device_id=(ix, to_mate(k)), device_id_type=MESH)

    def outgoing(k):
        return particles(k, pk.at[to_mate(k)], rk.at[iy], 0)

    def incoming(k):
        return particles(k, pk.at[0], rk.at[from_mate(k)], 0)

    for k in range(n_gy - 1, 0, -1):
        outgoing(k).start()
    rk[iy] = pk[iy]

    class Halo:
        def __init__(self, slot, ref, width, rows=0, reach=0, axes="xy", skip=0, over=0, detour=None):
            self.slot, self.ref, self.width, self.span, self.axes, self.skip = slot, ref, width, rows, axes, skip
            self.detour = detour if square else None
            self.rows = [(i, j) for i in range(reach) for j in range(reach) if over < i + j + 2 <= reach]

        def copy(self, index, source, landing, to):
            return pltpu.make_async_remote_copy(
                src_ref=source, dst_ref=landing, send_sem=field_send.at[self.slot, index],
                recv_sem=field_recv.at[self.slot, index], device_id=to, device_id_type=MESH)

        def x_copy(self, side):
            w, skip = self.width, self.skip
            at = skip if side == 0 else bx - w - skip
            source = self.ref.at[pl.ds(WX + at, w), own_y]
            landing = self.ref.at[pl.ds(WX + bx + skip if side == 0 else WX - w - skip, w), own_y]
            return self.copy(side, source, landing, peer["x", side])

        def aside(self, side):
            held = passed.at[self.detour, pl.ds(0, self.width)]
            at = self.skip if side == 0 else bx - self.width - self.skip
            return pltpu.make_async_remote_copy(
                src_ref=self.ref.at[pl.ds(WX + at, self.width), own_y], dst_ref=held,
                send_sem=field_send.at[self.slot, side], recv_sem=aside_recv.at[self.detour],
                device_id=(middle[side], iy), device_id_type=MESH)

        def onward(self, side):
            landing = WX + bx + self.skip if side == 0 else WX - self.width - self.skip
            return pltpu.make_async_remote_copy(
                src_ref=passed.at[self.detour, pl.ds(0, self.width)],
                dst_ref=self.ref.at[pl.ds(landing, self.width), own_y],
                send_sem=aside_send.at[self.detour], recv_sem=field_recv.at[self.slot, side],
                device_id=(target[side], iy), device_id_type=MESH)

        def send_x(self):
            for side in (0, 1):
                straight = has["x", side]
                if self.detour is not None:
                    straight = straight & (ix != origin[side])

                    @pl.when(ix == origin[side])
                    def _():
                        self.aside(side).start()

                @pl.when(straight)
                def _():
                    self.x_copy(side).start()

        def pass_on(self, act):
            for side in (0, 1) if self.detour is not None else ():
                @pl.when(ix == middle[side])
                def _():
                    act(self, side)

        def y_copy(self, side):
            h, skip = self.span, self.skip
            source = self.ref.at[own_x, pl.ds(WY + skip if side == 0 else WY + by - h - skip, h)]
            landing = self.ref.at[own_x, pl.ds(WY + by + skip if side == 0 else WY - h - skip, h)]
            return self.copy(2 + side, source, landing, peer["y", side])

        def c_copy(self, corner):
            n = 2 * corner[0] + corner[1]
            size = len(self.rows)
            return self.copy(4 + n, corner_out.at[self.slot, n, pl.ds(0, size)],
                             corner_in.at[self.slot, n, pl.ds(0, size)], beyond(corner))

        def pack(self):
            for corner in CORNERS if self.rows else ():
                for n, (i, j) in enumerate(self.rows):
                    x = WX + (i if corner[0] == 0 else bx - 1 - i)
                    y = WY + (j if corner[1] == 0 else by - 1 - j)
                    corner_out[self.slot, 2 * corner[0] + corner[1], n] = self.ref[x, y:y + 1, :]

        def each(self, axis, act, flip=False):
            if axis == "c":
                for corner in CORNERS if self.rows else ():
                    near = (1 - corner[0], 1 - corner[1]) if flip else corner

                    @pl.when(has["x", near[0]] & has["y", near[1]])
                    def _():
                        act(self.c_copy(corner), corner)
            elif axis in self.axes:
                for side in (0, 1):
                    @pl.when(has[axis, 1 - side if flip else side])
                    def _():
                        act((self.x_copy if axis == "x" else self.y_copy)(side), None)

        def unpack(self, copy, corner):
            copy.wait_recv()
            for n, (i, j) in enumerate(self.rows):
                x = WX + bx + i if corner[0] == 0 else WX - 1 - i
                y = WY + by + j if corner[1] == 0 else WY - 1 - j
                self.ref[x, y:y + 1, :] = corner_in[self.slot, 2 * corner[0] + corner[1], n]

    sent = []

    def start(halos):
        for h in halos:
            h.pack()
        for axis in "cxy":
            for h in halos:
                if axis == "x" and "x" in h.axes:
                    h.send_x()
                else:
                    h.each(axis, lambda c, _: c.start())
        sent.extend(halos)

    def arrive(halos, axes="yxc"):
        for axis in axes:
            for h in halos:
                h.each(axis, h.unpack if axis == "c" else lambda c, _: c.wait_recv(), flip=True)

    def forward(h, side):
        h.aside(side).wait_recv()
        h.onward(side).start()

    h_vel = [[Halo(0, v1.at[0], 2, 1, 2), Halo(1, v1.at[1], 1, 2, 2), Halo(2, v1.at[2], 1, 1)],
             [Halo(3, v2.at[0], 2, 1, 2), Halo(4, v2.at[1], 1, 2, 2), Halo(5, v2.at[2], 1, 1)]]
    h_p = [[Halo(6, pin1, WX, WX, WX)], [Halo(7, pin2, WX - 1, WX - 1, WX, skip=1, detour=1)]]
    near = SWEEPS // 2
    h_src = [[Halo(8, src1, near, SWEEPS, SWEEPS)], [Halo(9, src2, near, SWEEPS, SWEEPS)]]
    h_far = [[Halo(14, src1, SWEEPS - near, axes="x", skip=near)], [Halo(15, src2, SWEEPS - near, axes="x", skip=near)]]
    h_solid = [Halo(10, solid, 2, WX, 2)]
    h_rest = [Halo(13, solid, WX - 2, reach=WX, axes="x", skip=2, over=2, detour=0)]
    h_mf = [Halo(11, mf.at[0], 1, axes="x"), Halo(12, mf.at[1], rows=1, width=0, axes="y")]

    for fetch in fetches[3:]:
        fetch.wait()
    start(h_vel[0] + h_p[0])

    column_of = lax.broadcasted_iota(jnp.int32, (columns, slots), 0).astype(F32)
    depth_of = lax.broadcasted_iota(jnp.int32, (nz, slots), 0).astype(F32)
    dep[...] = jnp.zeros_like(dep)

    def where_of(b):
        cell = rk[b, 0:1, :]
        column = jnp.floor((cell + 0.5) * (1.0 / nz))
        return column, cell - column * nz

    def deposit(b, carry):
        column, level = where_of(b)
        hot_c = column == column_of
        hot_z = jnp.where(level == depth_of, 1.0, 0.0).astype(BF16)
        volume = rk[b, 1:2, :]
        values = [volume] + [volume * rk[b, 2 + d:3 + d, :] for d in range(3)]
        parts = [split(value) for value in values]
        left = jnp.concatenate(
            [jnp.concatenate([jnp.where(hot_c, part[side], 0.0).astype(BF16) for side in (0, 1)], axis=1) for part in parts], axis=0)
        dep[...] += lax.dot_general(left, jnp.concatenate([hot_z, hot_z], axis=1), (((1,), (1,)), ((), ())),
                                    preferred_element_type=F32)
        return carry

    deposit(iy, 0)

    def deposit_from(k, carry):
        incoming(k).wait_recv()
        return deposit(from_mate(k), carry)

    lax.fori_loop(1, n_gy, deposit_from, 0)
    solid[own_x, own_y, :] = dep[pl.ds(0, columns), :].reshape(bx, by, nz)
    for d in range(3):
        mf[d, own_x, own_y, :] = dep[pl.ds((1 + d) * columns, columns), :].reshape(bx, by, nz)
    start(h_solid + h_mf)
    start(h_rest)

    row = lax.broadcasted_iota(jnp.int32, (ey, nz), 0)
    depth = lax.broadcasted_iota(jnp.int32, (ey, nz), 1)
    row_in = jnp.where((row >= WY) | (iy > 0), 1.0, 0.0) * jnp.where((row < WY + by) | (iy < n_gy - 1), 1.0, 0.0)

    def voidage(x, carry):
        x_in = ((x >= WX) | (ix > 0)) & ((x < WX + bx) | (ix < n_gx - 1))
        eps[x] = jnp.maximum(1.0 - solid[x], FLOOR) * (row_in * jnp.where(x_in, 1.0, 0.0))
        return carry

    def sweep_over(act, spans, unroll):
        for first, end in spans:
            if first < end:
                lax.fori_loop(first, end, act, 0, unroll=min(2 * unroll, end - first))

    low, high = WX, WX + bx

    def up_y(v):
        return pltpu.roll(v, ey - 1, 0)

    def down_y(v):
        return pltpu.roll(v, 1, 0)

    def up_z(v):
        return pltpu.roll(v, nz - 1, 1)

    def down_z(v):
        return pltpu.roll(v, 1, 1)

    last_z, first_z = depth == nz - 1, depth == 0

    def weights(x, carry):
        e = eps[x]
        near = [eps[x + 1], eps[x - 1], up_y(e), down_y(e),
                jnp.where(last_z, 0.0, up_z(e)), jnp.where(first_z, 0.0, down_z(e))]
        total = 0.5 * (6.0 * e + (((near[0] + near[1]) + (near[2] + near[3])) + (near[4] + near[5])))
        inside = e > 0.0
        inverse = jnp.where(inside, 0.5 / jnp.where(inside, total, 1.0), 0.0)
        for n in range(6):
            w = (e + near[n]) * inverse
            if n == 4:
                w = jnp.where(last_z, 0.0, w)
            if n == 5:
                w = jnp.where(first_z, 0.0, w)
            coef[n, x] = w
        coef[6, x] = 2.0 * inverse
        recip = 1.0 / jnp.where(inside, e, 1.0)
        rate[x] = (DT * VISC) * total * recip
        pull[x] = (DT * DRAG) * recip
        return carry

    def stencil(field, x):
        v = field[x]
        return v, (((coef[0, x] * field[x + 1] + coef[1, x] * field[x - 1])
                    + (coef[2, x] * up_y(v) + coef[3, x] * down_y(v)))
                   + (coef[4, x] * up_z(v) + coef[5, x] * down_z(v)))

    def wide(b, tables):
        column, level = where_of(b)
        hot = jnp.where(column == column_of, 1.0, 0.0).astype(BF16)
        found = jnp.dot(tables, jnp.concatenate([hot, hot], axis=0), preferred_element_type=F32)
        hot_z = level == depth_of
        return [jnp.sum(jnp.where(hot_z, found[n:n + nz], 0.0), axis=0, keepdims=True)
                for n in range(0, found.shape[0], nz)]

    def table(grid):
        high, low = split(grid.reshape(columns, nz).T)
        return jnp.concatenate([high.astype(BF16), low.astype(BF16)], axis=1)

    def porosity(b, carry):
        at, = wide(b, ft[pl.ds(3 * nz, nz), :])
        pull_of[b] = rk[b, 1:2, :] * DRAG / at
        return carry

    for step in range(STEPS):
        v = (v1, v2)[step]
        pin = (pin1, pin2)[step]
        src = (src1, src2)[step]

        def predict(x, carry):
            s, r, g, e = solid[x], rate[x], pull[x], eps[x]
            for d in range(3):
                old, mean = stencil(v.at[d], x)
                new = old + r * (mean - old) + g * (mf[d, x] - s * old)
                guess[d, x] = new
                flux[d, x] = e * new
            return carry

        def balance(x, carry):
            f1, f2 = flux[1, x], flux[2, x]
            out = ((flux[0, x + 1] - flux[0, x - 1]) + (up_y(f1) - down_y(f1))
                   + (jnp.where(last_z, 0.0, up_z(f2)) - jnp.where(first_z, 0.0, down_z(f2))))
            src[x, own_y, :] = (0.5 / DT) * out[WY:WY + by]
            return carry

        early = h_vel[step] + (h_solid + h_mf if step == 0 else [])
        if step:
            ft[pl.ds(3 * nz, nz), :] = table(eps[own_x, own_y, :])
            lax.fori_loop(0, n_gy, porosity, 0)
        arrive(early, "y")
        if step == 0:
            sweep_over(voidage, [(low, high)], 4)
            sweep_over(weights, [(low + 1, high - 1)], 3)
        sweep_over(predict, [(low + 1, high - 1)], 3)
        sweep_over(balance, [(low + near, high - near)], 4)
        start(h_far[step])
        for h in h_p[1] if step else h_rest:
            h.pass_on(forward)
        arrive(early, "xc")
        if step == 0:
            sweep_over(voidage, [(low - 2, low), (high, high + 2)], 2)
            sweep_over(weights, [(low - 1, low + 1), (high - 1, high + 1)], 2)
        sweep_over(predict, [(low - 1, low + 1), (high - 1, high + 1)], 2)
        sweep_over(balance, [(low, low + near), (high - near, high)], 2)
        start(h_src[step])
        arrive(h_src[step], "y")
        if step == 0:
            arrive(h_rest)
            sweep_over(voidage, [(0, low), (high, ex)], 5)
            sweep_over(weights, [(1, low + 1), (high - 1, ex - 1)], 5)
            arrive(h_p[step])
        else:
            arrive(h_p[step], "y")

        def scale(x, carry):
            sp[x] = src[x] * coef[6, x]
            return carry

        stages = [pin] + [(pa, pb)[sweep % 2] for sweep in range(SWEEPS)]

        def relaxing(sweep):
            held, into = stages[sweep], stages[sweep + 1]

            def relax(x, carry):
                _, mean = stencil(held, x)
                into[x] = mean - sp[x]
                return carry

            return relax

        inset = 0 if step == 0 else 1
        sweep_over(scale, [(low, high)], 8)
        for sweep in range(SWEEPS):
            sweep_over(relaxing(sweep), [(low + sweep + inset, high - sweep - inset)], 4)
        if step:
            arrive(h_p[step], "xc")
        arrive(h_src[step], "xc")
        arrive(h_far[step])
        sweep_over(scale, [(1, low), (high, ex - 1)], 4)
        for sweep in range(SWEEPS):
            sweep_over(relaxing(sweep), [(1 + sweep, low + sweep + inset), (high - sweep - inset, ex - 1 - sweep)], 5)
        held = stages[SWEEPS]

        final = step == STEPS - 1

        def correct(x, carry):
            p = held[x]
            slopes = [held[x + 1] - held[x - 1], up_y(p) - down_y(p),
                      jnp.where(last_z, 0.0, up_z(p)) - jnp.where(first_z, 0.0, down_z(p))]
            for d in range(3):
                new = (guess[d, x] - (0.5 * DT) * slopes[d])[WY:WY + by]
                if final:
                    vel_out[d, x - WX] = new
                else:
                    v2[d, x, own_y, :] = new
            if final:
                p_out[x - WX] = p[WY:WY + by]
            else:
                for low, high in ((WY - 1, WY), (WY, WY + by), (WY + by, WY + by + 1)):
                    pin2[x, low:high, :] = p[low:high]
            return carry

        lax.fori_loop(WX, WX + bx, correct, 0, unroll=8)
        if not final:
            for x in (WX - 1, WX + bx):
                pin2[x, own_y, :] = held[x, own_y, :]
            start(h_vel[step + 1])
            start(h_p[step + 1])

    for d in range(3):
        ft[pl.ds(d * nz, nz), :] = table(vel_out[d])

    def gather(b, carry):
        at = wide(b, ft[pl.ds(0, 3 * nz), :])
        for d in range(3):
            dk[b, d:d + 1, :] = pull_of[b] * (at[d] - rk[b, 2 + d:3 + d, :])
        return carry

    def giving(k):
        return particles(k, dk.at[to_mate(k)], rd.at[iy], 1)

    def getting(k):
        return particles(k, dk.at[0], rd.at[from_mate(k)], 1)

    def gather_for(k, carry):
        gather(to_mate(n_gy - k), carry)
        giving(n_gy - k).start()
        return carry

    lax.fori_loop(1, n_gy, gather_for, 0)
    gather(iy, 0)
    rd[iy] = dk[iy]
    for h in sent:
        for axis in "xyc":
            h.each(axis, lambda c, _: c.wait_send())
        h.pass_on(lambda h, side: h.onward(side).wait_send())
    for k in range(1, n_gy):
        outgoing(k).wait_send()
        getting(k).wait_recv()
        giving(k).wait_send()
    for c in range(n_gy):
        for d in range(3):
            drag_out[d, pl.ds(c, 1), :] = rd[c, d:d + 1, :]


def deliver(*refs):
    pairs = len(refs) // 2
    copies = [pltpu.make_async_copy(refs[n], refs[pairs + n], refs[-1].at[n]) for n in range(pairs)]
    for copy in copies:
        copy.start()
    for copy in copies:
        copy.wait()


def solution(mesh):
    n_gx, n_gy = mesh.shape["gx"], mesh.shape["gy"]

    def per_device(velocity, pressure, part_cell, part_count, grain_velocities, part_vol):
        bx, by, nz = pressure.shape
        slots = part_vol.shape[-1]
        ext = (bx + 2 * WX, by + 2 * WY, nz)
        vmem = pl.BlockSpec(memory_space=pltpu.VMEM)
        anywhere = pl.BlockSpec(memory_space=pl.ANY)

        def field(*lead):
            return pltpu.VMEM(lead + ext, F32)

        def kernel(*refs):
            body(n_gx, n_gy, *refs)

        v, p, drag = pl.pallas_call(
            kernel,
            name="interval",
            out_shape=(
                pltpu.VMEM(velocity.shape, F32),
                pltpu.VMEM(pressure.shape, F32),
                pltpu.VMEM((3, n_gy, slots), F32),
            ),
            in_specs=[pl.BlockSpec(memory_space=pltpu.SMEM)] + [anywhere] * 5,
            out_specs=(vmem,) * 3,
            scratch_shapes=[
                pltpu.VMEM((n_gy, slots), jnp.int32),
                pltpu.VMEM((3, n_gy, slots), F32),
                pltpu.VMEM((n_gy, slots), F32),
                pltpu.SemaphoreType.DMA((7,)),
                field(3), field(3), field(), field(), field(), field(), field(), field(), field(),
                field(), field(3), field(), field(7), field(), field(), field(3), field(3),
                pltpu.VMEM((4 * bx * by, nz), F32),
                pltpu.VMEM((n_gy, ROWS, slots), F32),
                pltpu.VMEM((n_gy, ROWS, slots), F32),
                pltpu.VMEM((n_gy, 3, slots), F32),
                pltpu.VMEM((n_gy, 3, slots), F32),
                pltpu.VMEM((4 * nz, 2 * bx * by), BF16),
                pltpu.VMEM((n_gy, 1, slots), F32),
                pltpu.VMEM((16, 4, WX * (WX - 1) // 2, 1, nz), F32),
                pltpu.VMEM((16, 4, WX * (WX - 1) // 2, 1, nz), F32),
                pltpu.VMEM((2, WX, by, nz), F32),
                pltpu.SemaphoreType.DMA((2,)),
                pltpu.SemaphoreType.DMA((2,)),
                pltpu.SemaphoreType.DMA((16, 8)),
                pltpu.SemaphoreType.DMA((16, 8)),
                pltpu.SemaphoreType.DMA((2, n_gy)),
                pltpu.SemaphoreType.DMA((2, n_gy)),
            ],
            compiler_params=pltpu.CompilerParams(
                collective_id=0, has_side_effects=True, vmem_limit_bytes=56 * 1024 * 1024
            ),
        )(
            part_count.reshape(n_gy),
            velocity,
            pressure,
            part_cell.reshape(n_gy, slots),
            grain_velocities.reshape(n_gy, 3, slots).transpose(1, 0, 2),
            part_vol.reshape(n_gy, slots),
        )
        v, p, drag = [pltpu.with_memory_space_constraint(a, pltpu.VMEM) for a in (v, p, drag)]
        v, p, drag = pl.pallas_call(
            deliver,
            name="deliver",
            out_shape=tuple(jax.ShapeDtypeStruct(a.shape, F32) for a in (v, p, drag)),
            in_specs=(vmem,) * 3,
            out_specs=(anywhere,) * 3,
            scratch_shapes=[pltpu.SemaphoreType.DMA((3,))],
        )(v, p, drag)
        return v, p, drag.transpose(1, 0, 2).reshape(grain_velocities.shape)

    placed = (
        P(None, "gx", "gy", None),
        P("gx", "gy", None),
        P("gx", "gy", None, None),
        P("gx", "gy", None),
        P("gx", "gy", None, None, None),
        P("gx", "gy", None, None),
    )
    return jax.shard_map(
        per_device,
        mesh=mesh,
        in_specs=placed,
        out_specs=(P(None, "gx", "gy", None), P("gx", "gy", None), P("gx", "gy", None, None, None)),
        check_vma=False,
    )
```

```python
import jax
import jax.numpy as jnp
from jax import lax
from jax.experimental import pallas as pl
from jax.experimental.pallas import tpu as pltpu
from jax.sharding import PartitionSpec as P

STEPS = 2
SWEEPS = 4
DRAG = 2.0
DT = 0.25
VISC = 0.2
FLOOR = 0.4

WX = SWEEPS + 1
WY = 8
ROWS = 5

MESH = pl.DeviceIdType.MESH
CORNERS = ((0, 0), (0, 1), (1, 0), (1, 1))
F32 = jnp.float32
BF16 = jnp.bfloat16


def split(value):
    high = value.astype(BF16).astype(F32)
    return high, value - high


def mate(i, k, n):
    if n & (n - 1):
        return lax.rem(i + k, n)
    bit, flip = 1, 0
    while bit < n:
        flip = flip + bit * ((i // bit + k // bit) % 2)
        bit *= 2
    return flip


def body(n_gx, n_gy, count_ref, vel_hbm, p_hbm, cell_hbm, gv_hbm, vol_hbm,
         vel_out, p_out, drag_out, cell_ref, gv_ref, vol_ref, fetch_sem,
         v1, v2, pin1, pin2, pa, pb, src1, src2, sp, solid, mf, eps, coef, rate, pull,
         guess, flux, dep, pk, rk, dk, rd, ft, pull_of, corner_out, corner_in, passed, aside_send, aside_recv,
         field_send, field_recv, part_send, part_recv):
    bx, by, nz = p_hbm.shape
    ex, ey = bx + 2 * WX, by + 2 * WY
    slots = vol_hbm.shape[-1]
    columns = bx * by
    ix, iy = lax.axis_index("gx"), lax.axis_index("gy")
    has = {("x", 0): ix > 0, ("x", 1): ix < n_gx - 1, ("y", 0): iy > 0, ("y", 1): iy < n_gy - 1}
    peer = {("x", 0): (ix - 1, iy), ("x", 1): (ix + 1, iy), ("y", 0): (ix, iy - 1), ("y", 1): (ix, iy + 1)}
    own_x, own_y = pl.ds(WX, bx), pl.ds(WY, by)

    def to_mate(k):
        return mate(iy, k, n_gy)

    def from_mate(k):
        return to_mate(k) if n_gy & (n_gy - 1) == 0 else lax.rem(iy + n_gy - k, n_gy)

    def beyond(corner):
        return ix + (2 * corner[0] - 1), iy + (2 * corner[1] - 1)

    fetches = [(cell_hbm, cell_ref), (vol_hbm, vol_ref), (gv_hbm, gv_ref)]
    fetches += [(vel_hbm.at[d], v1.at[d, own_x, own_y]) for d in range(3)] + [(p_hbm, pin1.at[own_x, own_y])]
    fetches = [pltpu.make_async_copy(source, landing, fetch_sem.at[n]) for n, (source, landing) in enumerate(fetches)]
    for fetch in fetches:
        fetch.start()

    barrier = pltpu.get_barrier_semaphore()
    for k in range(1, n_gy):
        pl.semaphore_signal(barrier, inc=1, device_id=(ix, to_mate(k)), device_id_type=MESH)
    for side in (0, 1):
        @pl.when(has["x", side])
        def _():
            pl.semaphore_signal(barrier, inc=1, device_id=peer["x", side], device_id_type=MESH)
    for corner in CORNERS:
        @pl.when(has["x", corner[0]] & has["y", corner[1]])
        def _():
            pl.semaphore_signal(barrier, inc=1, device_id=beyond(corner), device_id_type=MESH)

    square = n_gx == 4
    origin, middle, target = (2, 1), (0, 3), (1, 2)
    if square:
        for side in (0, 1):
            @pl.when(ix == middle[side])
            def _():
                pl.semaphore_signal(barrier, inc=1, device_id=(origin[side], iy), device_id_type=MESH)


    fields = [v1.at[d] for d in range(3)] + [v2.at[d] for d in range(3)] + [mf.at[d] for d in range(3)]
    fields += [pin1, pin2, src1, src2, solid]
    for side in (0, 1):
        @pl.when(jnp.logical_not(has["x", side]))
        def _():
            for field in fields:
                at = 0 if side == 0 else WX + bx
                field[pl.ds(at, WX)] = jnp.zeros((WX, ey, nz), F32)

        @pl.when(jnp.logical_not(has["y", side]))
        def _():
            for field in fields:
                at = 0 if side == 0 else WY + by
                field[:, pl.ds(at, WY), :] = jnp.zeros((ex, WY, nz), F32)

    for fetch in fetches[:3]:
        fetch.wait()
    slot = lax.broadcasted_iota(jnp.int32, (1, slots), 1)
    for c in range(n_gy):
        pk[c, 0:1, :] = cell_ref[pl.ds(c, 1), :].astype(F32)
        pk[c, 1:2, :] = jnp.where(slot < count_ref[c], vol_ref[pl.ds(c, 1), :], 0.0)
        for d in range(3):
            pk[c, 2 + d:3 + d, :] = gv_ref[d, pl.ds(c, 1), :]

    x_peers = jnp.where(ix > 0, 1, 0) + jnp.where(ix < n_gx - 1, 1, 0)
    y_peers = jnp.where(iy > 0, 1, 0) + jnp.where(iy < n_gy - 1, 1, 0)
    detours = jnp.where((ix == 1) | (ix == 2), 1, 0) if square else 0
    pl.semaphore_wait(barrier, n_gy - 1 + x_peers * (1 + y_peers) + detours)

    def particles(k, source, landing, bank):
        return pltpu.make_async_remote_copy(
            src_ref=source, dst_ref=landing, send_sem=part_send.at[bank, k], recv_sem=part_recv.at[bank, k],
            device_id=(ix, to_mate(k)), device_id_type=MESH)

    def outgoing(k):
        return particles(k, pk.at[to_mate(k)], rk.at[iy], 0)

    def incoming(k):
        return particles(k, pk.at[0], rk.at[from_mate(k)], 0)

    for k in range(n_gy - 1, 0, -1):
        outgoing(k).start()
    rk[iy] = pk[iy]

    class Halo:
        def __init__(self, slot, ref, width, rows=0, reach=0, axes="xy", skip=0, over=0, detour=None):
            self.slot, self.ref, self.width, self.span, self.axes, self.skip = slot, ref, width, rows, axes, skip
            self.detour = detour if square else None
            self.rows = [(i, j) for i in range(reach) for j in range(reach) if over < i + j + 2 <= reach]

        def copy(self, index, source, landing, to):
            return pltpu.make_async_remote_copy(
                src_ref=source, dst_ref=landing, send_sem=field_send.at[self.slot, index],
                recv_sem=field_recv.at[self.slot, index], device_id=to, device_id_type=MESH)

        def x_copy(self, side):
            w, skip = self.width, self.skip
            at = skip if side == 0 else bx - w - skip
            source = self.ref.at[pl.ds(WX + at, w), own_y]
            landing = self.ref.at[pl.ds(WX + bx + skip if side == 0 else WX - w - skip, w), own_y]
            return self.copy(side, source, landing, peer["x", side])

        def aside(self, side):
            held = passed.at[self.detour, pl.ds(0, self.width)]
            at = self.skip if side == 0 else bx - self.width - self.skip
            return pltpu.make_async_remote_copy(
                src_ref=self.ref.at[pl.ds(WX + at, self.width), own_y], dst_ref=held,
                send_sem=field_send.at[self.slot, side], recv_sem=aside_recv.at[self.detour],
                device_id=(middle[side], iy), device_id_type=MESH)

        def onward(self, side):
            landing = WX + bx + self.skip if side == 0 else WX - self.width - self.skip
            return pltpu.make_async_remote_copy(
                src_ref=passed.at[self.detour, pl.ds(0, self.width)],
                dst_ref=self.ref.at[pl.ds(landing, self.width), own_y],
                send_sem=aside_send.at[self.detour], recv_sem=field_recv.at[self.slot, side],
                device_id=(target[side], iy), device_id_type=MESH)

        def send_x(self):
            for side in (0, 1):
                straight = has["x", side]
                if self.detour is not None:
                    straight = straight & (ix != origin[side])

                    @pl.when(ix == origin[side])
                    def _():
                        self.aside(side).start()

                @pl.when(straight)
                def _():
                    self.x_copy(side).start()

        def pass_on(self, act):
            for side in (0, 1) if self.detour is not None else ():
                @pl.when(ix == middle[side])
                def _():
                    act(self, side)

        def y_copy(self, side):
            h, skip = self.span, self.skip
            source = self.ref.at[own_x, pl.ds(WY + skip if side == 0 else WY + by - h - skip, h)]
            landing = self.ref.at[own_x, pl.ds(WY + by + skip if side == 0 else WY - h - skip, h)]
            return self.copy(2 + side, source, landing, peer["y", side])

        def c_copy(self, corner):
            n = 2 * corner[0] + corner[1]
            size = len(self.rows)
            return self.copy(4 + n, corner_out.at[self.slot, n, pl.ds(0, size)],
                             corner_in.at[self.slot, n, pl.ds(0, size)], beyond(corner))

        def pack(self):
            for corner in CORNERS if self.rows else ():
                for n, (i, j) in enumerate(self.rows):
                    x = WX + (i if corner[0] == 0 else bx - 1 - i)
                    y = WY + (j if corner[1] == 0 else by - 1 - j)
                    corner_out[self.slot, 2 * corner[0] + corner[1], n] = self.ref[x, y:y + 1, :]

        def each(self, axis, act, flip=False):
            if axis == "c":
                for corner in CORNERS if self.rows else ():
                    near = (1 - corner[0], 1 - corner[1]) if flip else corner

                    @pl.when(has["x", near[0]] & has["y", near[1]])
                    def _():
                        act(self.c_copy(corner), corner)
            elif axis in self.axes:
                for side in (0, 1):
                    @pl.when(has[axis, 1 - side if flip else side])
                    def _():
                        act((self.x_copy if axis == "x" else self.y_copy)(side), None)

        def unpack(self, copy, corner):
            copy.wait_recv()
            for n, (i, j) in enumerate(self.rows):
                x = WX + bx + i if corner[0] == 0 else WX - 1 - i
                y = WY + by + j if corner[1] == 0 else WY - 1 - j
                self.ref[x, y:y + 1, :] = corner_in[self.slot, 2 * corner[0] + corner[1], n]

    sent = []

    def send(halos, axis):
        for h in halos:
            if axis == "x" and "x" in h.axes:
                h.send_x()
            else:
                h.each(axis, lambda c, _: c.start())

    def start(halos):
        for h in halos:
            h.pack()
        for axis in "cxy":
            send(halos, axis)
        sent.extend(halos)

    def arrive(halos, axes="yxc"):
        for axis in axes:
            for h in halos:
                h.each(axis, h.unpack if axis == "c" else lambda c, _: c.wait_recv(), flip=True)

    def forward(h, side):
        h.aside(side).wait_recv()
        h.onward(side).start()

    h_vel = [[Halo(0, v1.at[0], 2, 1, 2), Halo(1, v1.at[1], 1, 2, 2), Halo(2, v1.at[2], 1, 1)],
             [Halo(3, v2.at[0], 2, 1, 2), Halo(4, v2.at[1], 1, 2, 2), Halo(5, v2.at[2], 1, 1)]]
    h_p = [[Halo(6, pin1, WX, WX, WX)], [Halo(7, pin2, WX - 1, WX - 1, WX, skip=1, detour=0)]]
    near = SWEEPS // 2
    h_src = [[Halo(8, src1, near, SWEEPS, SWEEPS)], [Halo(9, src2, near, SWEEPS, SWEEPS)]]
    h_far = [[Halo(14, src1, SWEEPS - near, axes="x", skip=near)], [Halo(15, src2, SWEEPS - near, axes="x", skip=near)]]
    h_solid = [Halo(10, solid, 2, WX, 2)]
    h_rest = [Halo(13, solid, WX - 2, reach=WX, axes="x", skip=2, over=2)]
    h_mf = [Halo(11, mf.at[0], 1, axes="x"), Halo(12, mf.at[1], rows=1, width=0, axes="y")]

    for fetch in fetches[3:]:
        fetch.wait()
    start(h_vel[0] + h_p[0])

    column_of = lax.broadcasted_iota(jnp.int32, (columns, slots), 0).astype(F32)
    depth_of = lax.broadcasted_iota(jnp.int32, (nz, slots), 0).astype(F32)
    dep[...] = jnp.zeros_like(dep)

    def where_of(b):
        cell = rk[b, 0:1, :]
        column = jnp.floor((cell + 0.5) * (1.0 / nz))
        return column, cell - column * nz

    def deposit(b, carry):
        column, level = where_of(b)
        hot_c = column == column_of
        hot_z = jnp.where(level == depth_of, 1.0, 0.0).astype(BF16)
        volume = rk[b, 1:2, :]
        values = [volume] + [volume * rk[b, 2 + d:3 + d, :] for d in range(3)]
        parts = [split(value) for value in values]
        left = jnp.concatenate(
            [jnp.concatenate([jnp.where(hot_c, part[side], 0.0).astype(BF16) for side in (0, 1)], axis=1) for part in parts], axis=0)
        dep[...] += lax.dot_general(left, jnp.concatenate([hot_z, hot_z], axis=1), (((1,), (1,)), ((), ())),
                                    preferred_element_type=F32)
        return carry

    deposit(iy, 0)

    def deposit_from(k, carry):
        incoming(k).wait_recv()
        return deposit(from_mate(k), carry)

    lax.fori_loop(1, n_gy, deposit_from, 0)
    solid[own_x, own_y, :] = dep[pl.ds(0, columns), :].reshape(bx, by, nz)
    for d in range(3):
        mf[d, own_x, own_y, :] = dep[pl.ds((1 + d) * columns, columns), :].reshape(bx, by, nz)
    start(h_solid + h_mf)
    start(h_rest)

    row = lax.broadcasted_iota(jnp.int32, (ey, nz), 0)
    depth = lax.broadcasted_iota(jnp.int32, (ey, nz), 1)
    row_in = jnp.where((row >= WY) | (iy > 0), 1.0, 0.0) * jnp.where((row < WY + by) | (iy < n_gy - 1), 1.0, 0.0)

    def voidage(x, carry):
        x_in = ((x >= WX) | (ix > 0)) & ((x < WX + bx) | (ix < n_gx - 1))
        eps[x] = jnp.maximum(1.0 - solid[x], FLOOR) * (row_in * jnp.where(x_in, 1.0, 0.0))
        return carry

    def sweep_over(act, spans, unroll):
        for first, end in spans:
            if first < end:
                lax.fori_loop(first, end, act, 0, unroll=min(2 * unroll, end - first))

    low, high = WX, WX + bx

    def up_y(v):
        return pltpu.roll(v, ey - 1, 0)

    def down_y(v):
        return pltpu.roll(v, 1, 0)

    def up_z(v):
        return pltpu.roll(v, nz - 1, 1)

    def down_z(v):
        return pltpu.roll(v, 1, 1)

    last_z, first_z = depth == nz - 1, depth == 0

    def weights(x, carry):
        e = eps[x]
        near = [eps[x + 1], eps[x - 1], up_y(e), down_y(e),
                jnp.where(last_z, 0.0, up_z(e)), jnp.where(first_z, 0.0, down_z(e))]
        total = 0.5 * (6.0 * e + (((near[0] + near[1]) + (near[2] + near[3])) + (near[4] + near[5])))
        inside = e > 0.0
        inverse = jnp.where(inside, 0.5 / jnp.where(inside, total, 1.0), 0.0)
        for n in range(6):
            w = (e + near[n]) * inverse
            if n == 4:
                w = jnp.where(last_z, 0.0, w)
            if n == 5:
                w = jnp.where(first_z, 0.0, w)
            coef[n, x] = w
        coef[6, x] = 2.0 * inverse
        recip = 1.0 / jnp.where(inside, e, 1.0)
        rate[x] = (DT * VISC) * total * recip
        pull[x] = (DT * DRAG) * recip
        return carry

    def stencil(field, x):
        v = field[x]
        return v, (((coef[0, x] * field[x + 1] + coef[1, x] * field[x - 1])
                    + (coef[2, x] * up_y(v) + coef[3, x] * down_y(v)))
                   + (coef[4, x] * up_z(v) + coef[5, x] * down_z(v)))

    def wide(b, tables):
        column, level = where_of(b)
        hot = jnp.where(column == column_of, 1.0, 0.0).astype(BF16)
        found = jnp.dot(tables, jnp.concatenate([hot, hot], axis=0), preferred_element_type=F32)
        hot_z = level == depth_of
        return [jnp.sum(jnp.where(hot_z, found[n:n + nz], 0.0), axis=0, keepdims=True)
                for n in range(0, found.shape[0], nz)]

    def table(grid):
        high, low = split(grid.reshape(columns, nz).T)
        return jnp.concatenate([high.astype(BF16), low.astype(BF16)], axis=1)

    def porosity(b, carry):
        at, = wide(b, ft[pl.ds(3 * nz, nz), :])
        pull_of[b] = rk[b, 1:2, :] * DRAG / at
        return carry

    for step in range(STEPS):
        v = (v1, v2)[step]
        pin = (pin1, pin2)[step]
        src = (src1, src2)[step]

        def predicting(parts):
            def predict(x, carry):
                s, r, g, e = solid[x], rate[x], pull[x], eps[x]
                for d in range(parts):
                    old, mean = stencil(v.at[d], x)
                    new = old + r * (mean - old) + g * (mf[d, x] - s * old)
                    if parts == 3:
                        guess[d, x] = new
                    flux[d, x] = e * new
                return carry

            return predict

        def balance(x, carry):
            f1, f2 = flux[1, x], flux[2, x]
            out = ((flux[0, x + 1] - flux[0, x - 1]) + (up_y(f1) - down_y(f1))
                   + (jnp.where(last_z, 0.0, up_z(f2)) - jnp.where(first_z, 0.0, down_z(f2))))
            src[x, own_y, :] = (0.5 / DT) * out[WY:WY + by]
            return carry

        early = h_vel[step] + (h_solid + h_mf if step == 0 else [])
        if step:
            ft[pl.ds(3 * nz, nz), :] = table(eps[own_x, own_y, :])
            lax.fori_loop(0, n_gy, porosity, 0)
        arrive(early, "y")
        if step == 0:
            sweep_over(voidage, [(low, high)], 4)
            sweep_over(weights, [(low + 1, high - 1)], 3)
        sweep_over(predicting(3), [(low + 1, high - 1)], 3)
        sweep_over(balance, [(low + near, high - near)], 4)
        start(h_far[step])
        for h in h_p[1] if step else ():
            h.pass_on(forward)
        arrive(early, "xc")
        if step == 0:
            sweep_over(voidage, [(low - 2, low), (high, high + 2)], 2)
            sweep_over(weights, [(low - 1, low + 1), (high - 1, high + 1)], 2)
        sweep_over(predicting(1), [(low - 1, low), (high, high + 1)], 1)
        sweep_over(predicting(3), [(low, low + 1), (high - 1, high)], 1)
        sweep_over(balance, [(low, low + near), (high - near, high)], 2)
        start(h_src[step])
        arrive(h_src[step], "y")
        if step == 0:
            arrive(h_rest)
            sweep_over(voidage, [(0, low), (high, ex)], 5)
            sweep_over(weights, [(1, low + 1), (high - 1, ex - 1)], 5)
            arrive(h_p[step])
        else:
            arrive(h_p[step], "y")

        def scale(x, carry):
            sp[x] = src[x] * coef[6, x]
            return carry

        stages = [pin] + [(pa, pb)[sweep % 2] for sweep in range(SWEEPS)]

        def relaxing(sweep):
            held, into = stages[sweep], stages[sweep + 1]

            def relax(x, carry):
                _, mean = stencil(held, x)
                into[x] = mean - sp[x]
                return carry

            return relax

        inset = 0 if step == 0 else 1
        sweep_over(scale, [(low, high)], 8)
        for sweep in range(SWEEPS):
            sweep_over(relaxing(sweep), [(low + sweep + inset, high - sweep - inset)], 4)
        if step:
            arrive(h_p[step], "xc")
        arrive(h_src[step], "xc")
        arrive(h_far[step])
        sweep_over(scale, [(1, low), (high, ex - 1)], 4)
        for sweep in range(SWEEPS):
            sweep_over(relaxing(sweep), [(1 + sweep, low + sweep + inset), (high - sweep - inset, ex - 1 - sweep)], 5)
        held = stages[SWEEPS]

        final = step == STEPS - 1

        def correct(x, carry):
            p = held[x]
            slopes = [held[x + 1] - held[x - 1], up_y(p) - down_y(p),
                      jnp.where(last_z, 0.0, up_z(p)) - jnp.where(first_z, 0.0, down_z(p))]
            for d in range(3):
                new = (guess[d, x] - (0.5 * DT) * slopes[d])[WY:WY + by]
                if final:
                    vel_out[d, x - WX] = new
                else:
                    v2[d, x, own_y, :] = new
            if final:
                p_out[x - WX] = p[WY:WY + by]
            else:
                for low, high in ((WY - 1, WY), (WY, WY + by), (WY + by, WY + by + 1)):
                    pin2[x, low:high, :] = p[low:high]
            return carry

        if final:
            sweep_over(correct, [(low, high)], bx)
        else:
            sweep_over(correct, [(low, low + 2), (high - 2, high)], 2)
            for h in h_vel[step + 1]:
                h.pack()
            for axis in "cx":
                send(h_vel[step + 1], axis)
            sweep_over(correct, [(low + 2, high - 2)], bx)
            send(h_vel[step + 1], "y")
            sent.extend(h_vel[step + 1])
            for x in (WX - 1, WX + bx):
                pin2[x, own_y, :] = held[x, own_y, :]
            start(h_p[step + 1])

    for d in range(3):
        ft[pl.ds(d * nz, nz), :] = table(vel_out[d])

    def gather(b, carry):
        at = wide(b, ft[pl.ds(0, 3 * nz), :])
        for d in range(3):
            dk[b, d:d + 1, :] = pull_of[b] * (at[d] - rk[b, 2 + d:3 + d, :])
        return carry

    def giving(k):
        return particles(k, dk.at[to_mate(k)], rd.at[iy], 1)

    def getting(k):
        return particles(k, dk.at[0], rd.at[from_mate(k)], 1)

    def gather_for(k, carry):
        gather(to_mate(n_gy - k), carry)
        giving(n_gy - k).start()
        return carry

    lax.fori_loop(1, n_gy, gather_for, 0)
    gather(iy, 0)
    rd[iy] = dk[iy]
    for h in sent:
        for axis in "xyc":
            h.each(axis, lambda c, _: c.wait_send())
        h.pass_on(lambda h, side: h.onward(side).wait_send())
    for k in range(1, n_gy):
        outgoing(k).wait_send()
        getting(k).wait_recv()
        giving(k).wait_send()
    for c in range(n_gy):
        for d in range(3):
            drag_out[d, pl.ds(c, 1), :] = rd[c, d:d + 1, :]


def deliver(*refs):
    pairs = len(refs) // 2
    copies = [pltpu.make_async_copy(refs[n], refs[pairs + n], refs[-1].at[n]) for n in range(pairs)]
    for copy in copies:
        copy.start()
    for copy in copies:
        copy.wait()


def solution(mesh):
    n_gx, n_gy = mesh.shape["gx"], mesh.shape["gy"]

    def per_device(velocity, pressure, part_cell, part_count, grain_velocities, part_vol):
        bx, by, nz = pressure.shape
        slots = part_vol.shape[-1]
        ext = (bx + 2 * WX, by + 2 * WY, nz)
        vmem = pl.BlockSpec(memory_space=pltpu.VMEM)
        anywhere = pl.BlockSpec(memory_space=pl.ANY)

        def field(*lead):
            return pltpu.VMEM(lead + ext, F32)

        def kernel(*refs):
            body(n_gx, n_gy, *refs)

        v, p, drag = pl.pallas_call(
            kernel,
            name="interval",
            out_shape=(
                pltpu.VMEM(velocity.shape, F32),
                pltpu.VMEM(pressure.shape, F32),
                pltpu.VMEM((3, n_gy, slots), F32),
            ),
            in_specs=[pl.BlockSpec(memory_space=pltpu.SMEM)] + [anywhere] * 5,
            out_specs=(vmem,) * 3,
            scratch_shapes=[
                pltpu.VMEM((n_gy, slots), jnp.int32),
                pltpu.VMEM((3, n_gy, slots), F32),
                pltpu.VMEM((n_gy, slots), F32),
                pltpu.SemaphoreType.DMA((7,)),
                field(3), field(3), field(), field(), field(), field(), field(), field(), field(),
                field(), field(3), field(), field(7), field(), field(), field(3), field(3),
                pltpu.VMEM((4 * bx * by, nz), F32),
                pltpu.VMEM((n_gy, ROWS, slots), F32),
                pltpu.VMEM((n_gy, ROWS, slots), F32),
                pltpu.VMEM((n_gy, 3, slots), F32),
                pltpu.VMEM((n_gy, 3, slots), F32),
                pltpu.VMEM((4 * nz, 2 * bx * by), BF16),
                pltpu.VMEM((n_gy, 1, slots), F32),
                pltpu.VMEM((16, 4, WX * (WX - 1) // 2, 1, nz), F32),
                pltpu.VMEM((16, 4, WX * (WX - 1) // 2, 1, nz), F32),
                pltpu.VMEM((1, WX, by, nz), F32),
                pltpu.SemaphoreType.DMA((2,)),
                pltpu.SemaphoreType.DMA((2,)),
                pltpu.SemaphoreType.DMA((16, 8)),
                pltpu.SemaphoreType.DMA((16, 8)),
                pltpu.SemaphoreType.DMA((2, n_gy)),
                pltpu.SemaphoreType.DMA((2, n_gy)),
            ],
            compiler_params=pltpu.CompilerParams(
                collective_id=0, has_side_effects=True, vmem_limit_bytes=56 * 1024 * 1024
            ),
        )(
            part_count.reshape(n_gy),
            velocity,
            pressure,
            part_cell.reshape(n_gy, slots),
            grain_velocities.reshape(n_gy, 3, slots).transpose(1, 0, 2),
            part_vol.reshape(n_gy, slots),
        )
        v, p, drag = [pltpu.with_memory_space_constraint(a, pltpu.VMEM) for a in (v, p, drag)]
        v, p, drag = pl.pallas_call(
            deliver,
            name="deliver",
            out_shape=tuple(jax.ShapeDtypeStruct(a.shape, F32) for a in (v, p, drag)),
            in_specs=(vmem,) * 3,
            out_specs=(anywhere,) * 3,
            scratch_shapes=[pltpu.SemaphoreType.DMA((3,))],
        )(v, p, drag)
        return v, p, drag.transpose(1, 0, 2).reshape(grain_velocities.shape)

    placed = (
        P(None, "gx", "gy", None),
        P("gx", "gy", None),
        P("gx", "gy", None, None),
        P("gx", "gy", None),
        P("gx", "gy", None, None, None),
        P("gx", "gy", None, None),
    )
    return jax.shard_map(
        per_device,
        mesh=mesh,
        in_specs=placed,
        out_specs=(P(None, "gx", "gy", None), P("gx", "gy", None), P("gx", "gy", None, None, None)),
        check_vma=False,
    )
```

```python
import jax
import jax.numpy as jnp
from jax import lax
from jax.experimental import pallas as pl
from jax.experimental.pallas import tpu as pltpu
from jax.sharding import PartitionSpec as P

STEPS = 2
SWEEPS = 4
DRAG = 2.0
DT = 0.25
VISC = 0.2
FLOOR = 0.4

WX = SWEEPS + 1
WY = 8
ROWS = 5

MESH = pl.DeviceIdType.MESH
CORNERS = ((0, 0), (0, 1), (1, 0), (1, 1))
F32 = jnp.float32
BF16 = jnp.bfloat16


def split(value):
    high = value.astype(BF16).astype(F32)
    return high, value - high


def mate(i, k, n):
    if n & (n - 1):
        return lax.rem(i + k, n)
    bit, flip = 1, 0
    while bit < n:
        flip = flip + bit * ((i // bit + k // bit) % 2)
        bit *= 2
    return flip


def body(n_gx, n_gy, count_ref, vel_hbm, p_hbm, cell_hbm, gv_hbm, vol_hbm,
         vel_out, p_out, drag_out, cell_ref, gv_ref, vol_ref, fetch_sem,
         v1, v2, pin1, pin2, pa, pb, src1, src2, sp, solid, mf, eps, coef, rate, pull,
         guess, flux, dep, pk, rk, dk, rd, ft, pull_of, corner_out, corner_in, passed, aside_send, aside_recv,
         field_send, field_recv, part_send, part_recv):
    bx, by, nz = p_hbm.shape
    ex, ey = bx + 2 * WX, by + 2 * WY
    slots = vol_hbm.shape[-1]
    columns = bx * by
    ix, iy = lax.axis_index("gx"), lax.axis_index("gy")
    has = {("x", 0): ix > 0, ("x", 1): ix < n_gx - 1, ("y", 0): iy > 0, ("y", 1): iy < n_gy - 1}
    peer = {("x", 0): (ix - 1, iy), ("x", 1): (ix + 1, iy), ("y", 0): (ix, iy - 1), ("y", 1): (ix, iy + 1)}
    own_x, own_y = pl.ds(WX, bx), pl.ds(WY, by)

    def to_mate(k):
        return mate(iy, k, n_gy)

    def from_mate(k):
        return to_mate(k) if n_gy & (n_gy - 1) == 0 else lax.rem(iy + n_gy - k, n_gy)

    def beyond(corner):
        return ix + (2 * corner[0] - 1), iy + (2 * corner[1] - 1)

    fetches = [(cell_hbm, cell_ref), (vol_hbm, vol_ref), (gv_hbm, gv_ref)]
    fetches += [(vel_hbm.at[d], v1.at[d, own_x, own_y]) for d in range(3)] + [(p_hbm, pin1.at[own_x, own_y])]
    fetches = [pltpu.make_async_copy(source, landing, fetch_sem.at[n]) for n, (source, landing) in enumerate(fetches)]
    for fetch in fetches:
        fetch.start()

    barrier = pltpu.get_barrier_semaphore()
    for k in range(1, n_gy):
        pl.semaphore_signal(barrier, inc=1, device_id=(ix, to_mate(k)), device_id_type=MESH)
    for side in (0, 1):
        @pl.when(has["x", side])
        def _():
            pl.semaphore_signal(barrier, inc=1, device_id=peer["x", side], device_id_type=MESH)
    for corner in CORNERS:
        @pl.when(has["x", corner[0]] & has["y", corner[1]])
        def _():
            pl.semaphore_signal(barrier, inc=1, device_id=beyond(corner), device_id_type=MESH)

    square = n_gx == 4
    origin, middle, target = (2, 1), (0, 3), (1, 2)
    if square:
        for side in (0, 1):
            @pl.when(ix == middle[side])
            def _():
                pl.semaphore_signal(barrier, inc=1, device_id=(origin[side], iy), device_id_type=MESH)


    fields = [v1.at[d] for d in range(3)] + [v2.at[d] for d in range(3)] + [mf.at[d] for d in range(3)]
    fields += [pin1, pin2, src1, src2, solid]
    for side in (0, 1):
        @pl.when(jnp.logical_not(has["x", side]))
        def _():
            for field in fields:
                at = 0 if side == 0 else WX + bx
                field[pl.ds(at, WX)] = jnp.zeros((WX, ey, nz), F32)

        @pl.when(jnp.logical_not(has["y", side]))
        def _():
            for field in fields:
                at = 0 if side == 0 else WY + by
                field[:, pl.ds(at, WY), :] = jnp.zeros((ex, WY, nz), F32)

    for fetch in fetches[:3]:
        fetch.wait()
    slot = lax.broadcasted_iota(jnp.int32, (1, slots), 1)
    for c in range(n_gy):
        pk[c, 0:1, :] = cell_ref[pl.ds(c, 1), :].astype(F32)
        pk[c, 1:2, :] = jnp.where(slot < count_ref[c], vol_ref[pl.ds(c, 1), :], 0.0)
        for d in range(3):
            pk[c, 2 + d:3 + d, :] = gv_ref[d, pl.ds(c, 1), :]

    x_peers = jnp.where(ix > 0, 1, 0) + jnp.where(ix < n_gx - 1, 1, 0)
    y_peers = jnp.where(iy > 0, 1, 0) + jnp.where(iy < n_gy - 1, 1, 0)
    detours = jnp.where((ix == 1) | (ix == 2), 1, 0) if square else 0
    pl.semaphore_wait(barrier, n_gy - 1 + x_peers * (1 + y_peers) + detours)

    def particles(k, source, landing, bank):
        return pltpu.make_async_remote_copy(
            src_ref=source, dst_ref=landing, send_sem=part_send.at[bank, k], recv_sem=part_recv.at[bank, k],
            device_id=(ix, to_mate(k)), device_id_type=MESH)

    def outgoing(k):
        return particles(k, pk.at[to_mate(k)], rk.at[iy], 0)

    def incoming(k):
        return particles(k, pk.at[0], rk.at[from_mate(k)], 0)

    for k in range(n_gy - 1, 0, -1):
        outgoing(k).start()
    rk[iy] = pk[iy]

    class Halo:
        def __init__(self, slot, ref, width, rows=0, reach=0, axes="xy", skip=0, over=0, detour=None):
            self.slot, self.ref, self.width, self.span, self.axes, self.skip = slot, ref, width, rows, axes, skip
            self.detour = detour if square else None
            self.rows = [(i, j) for i in range(reach) for j in range(reach) if over < i + j + 2 <= reach]

        def copy(self, index, source, landing, to):
            return pltpu.make_async_remote_copy(
                src_ref=source, dst_ref=landing, send_sem=field_send.at[self.slot, index],
                recv_sem=field_recv.at[self.slot, index], device_id=to, device_id_type=MESH)

        def x_copy(self, side):
            w, skip = self.width, self.skip
            at = skip if side == 0 else bx - w - skip
            source = self.ref.at[pl.ds(WX + at, w), own_y]
            landing = self.ref.at[pl.ds(WX + bx + skip if side == 0 else WX - w - skip, w), own_y]
            return self.copy(side, source, landing, peer["x", side])

        def aside(self, side):
            held = passed.at[self.detour, pl.ds(0, self.width)]
            at = self.skip if side == 0 else bx - self.width - self.skip
            return pltpu.make_async_remote_copy(
                src_ref=self.ref.at[pl.ds(WX + at, self.width), own_y], dst_ref=held,
                send_sem=field_send.at[self.slot, side], recv_sem=aside_recv.at[self.detour],
                device_id=(middle[side], iy), device_id_type=MESH)

        def onward(self, side):
            landing = WX + bx + self.skip if side == 0 else WX - self.width - self.skip
            return pltpu.make_async_remote_copy(
                src_ref=passed.at[self.detour, pl.ds(0, self.width)],
                dst_ref=self.ref.at[pl.ds(landing, self.width), own_y],
                send_sem=aside_send.at[self.detour], recv_sem=field_recv.at[self.slot, side],
                device_id=(target[side], iy), device_id_type=MESH)

        def send_x(self):
            for side in (0, 1):
                straight = has["x", side]
                if self.detour is not None:
                    straight = straight & (ix != origin[side])

                    @pl.when(ix == origin[side])
                    def _():
                        self.aside(side).start()

                @pl.when(straight)
                def _():
                    self.x_copy(side).start()

        def pass_on(self, act):
            for side in (0, 1) if self.detour is not None else ():
                @pl.when(ix == middle[side])
                def _():
                    act(self, side)

        def y_copy(self, side):
            h, skip = self.span, self.skip
            source = self.ref.at[own_x, pl.ds(WY + skip if side == 0 else WY + by - h - skip, h)]
            landing = self.ref.at[own_x, pl.ds(WY + by + skip if side == 0 else WY - h - skip, h)]
            return self.copy(2 + side, source, landing, peer["y", side])

        def c_copy(self, corner):
            n = 2 * corner[0] + corner[1]
            size = len(self.rows)
            return self.copy(4 + n, corner_out.at[self.slot, n, pl.ds(0, size)],
                             corner_in.at[self.slot, n, pl.ds(0, size)], beyond(corner))

        def pack(self):
            for corner in CORNERS if self.rows else ():
                for n, (i, j) in enumerate(self.rows):
                    x = WX + (i if corner[0] == 0 else bx - 1 - i)
                    y = WY + (j if corner[1] == 0 else by - 1 - j)
                    corner_out[self.slot, 2 * corner[0] + corner[1], n] = self.ref[x, y:y + 1, :]

        def each(self, axis, act, flip=False):
            if axis == "c":
                for corner in CORNERS if self.rows else ():
                    near = (1 - corner[0], 1 - corner[1]) if flip else corner

                    @pl.when(has["x", near[0]] & has["y", near[1]])
                    def _():
                        act(self.c_copy(corner), corner)
            elif axis in self.axes:
                for side in (0, 1):
                    @pl.when(has[axis, 1 - side if flip else side])
                    def _():
                        act((self.x_copy if axis == "x" else self.y_copy)(side), None)

        def unpack(self, copy, corner):
            copy.wait_recv()
            for n, (i, j) in enumerate(self.rows):
                x = WX + bx + i if corner[0] == 0 else WX - 1 - i
                y = WY + by + j if corner[1] == 0 else WY - 1 - j
                self.ref[x, y:y + 1, :] = corner_in[self.slot, 2 * corner[0] + corner[1], n]

    sent = []

    def send(halos, axis):
        for h in halos:
            if axis == "x" and "x" in h.axes:
                h.send_x()
            else:
                h.each(axis, lambda c, _: c.start())

    def start(halos):
        for h in halos:
            h.pack()
        for axis in "cxy":
            send(halos, axis)
        sent.extend(halos)

    def arrive(halos, axes="yxc"):
        for axis in axes:
            for h in halos:
                h.each(axis, h.unpack if axis == "c" else lambda c, _: c.wait_recv(), flip=True)

    def forward(h, side):
        h.aside(side).wait_recv()
        h.onward(side).start()

    h_vel = [[Halo(0, v1.at[0], 2, 1, 2), Halo(1, v1.at[1], 1, 2, 2), Halo(2, v1.at[2], 1, 1)],
             [Halo(3, v2.at[0], 2, 1, 2), Halo(4, v2.at[1], 1, 2, 2), Halo(5, v2.at[2], 1, 1)]]
    h_p = [[Halo(6, pin1, WX, WX, WX)], [Halo(7, pin2, WX - 1, WX - 1, WX, skip=1, detour=0)]]
    near = SWEEPS // 2
    h_src = [[Halo(8, src1, near, SWEEPS, SWEEPS)], [Halo(9, src2, near, SWEEPS, SWEEPS)]]
    h_far = [[Halo(14, src1, SWEEPS - near, axes="x", skip=near)], [Halo(15, src2, SWEEPS - near, axes="x", skip=near)]]
    h_solid = [Halo(10, solid, 2, WX, 2)]
    h_rest = [Halo(13, solid, WX - 2, reach=WX, axes="x", skip=2, over=2)]
    h_mf = [Halo(11, mf.at[0], 1, axes="x"), Halo(12, mf.at[1], rows=1, width=0, axes="y")]

    for fetch in fetches[3:]:
        fetch.wait()
    start(h_vel[0] + h_p[0])

    column_of = lax.broadcasted_iota(jnp.int32, (columns, slots), 0).astype(F32)
    depth_of = lax.broadcasted_iota(jnp.int32, (nz, slots), 0).astype(F32)
    dep[...] = jnp.zeros_like(dep)

    def where_of(b):
        cell = rk[b, 0:1, :]
        column = jnp.floor((cell + 0.5) * (1.0 / nz))
        return column, cell - column * nz

    def deposit(b, carry):
        column, level = where_of(b)
        hot_c = column == column_of
        hot_z = jnp.where(level == depth_of, 1.0, 0.0).astype(BF16)
        volume = rk[b, 1:2, :]
        values = [volume] + [volume * rk[b, 2 + d:3 + d, :] for d in range(3)]
        parts = [split(value) for value in values]
        left = jnp.concatenate(
            [jnp.concatenate([jnp.where(hot_c, part[side], 0.0).astype(BF16) for side in (0, 1)], axis=1) for part in parts], axis=0)
        dep[...] += lax.dot_general(left, jnp.concatenate([hot_z, hot_z], axis=1), (((1,), (1,)), ((), ())),
                                    preferred_element_type=F32)
        return carry

    deposit(iy, 0)

    def deposit_from(k, carry):
        incoming(k).wait_recv()
        return deposit(from_mate(k), carry)

    lax.fori_loop(1, n_gy, deposit_from, 0)
    solid[own_x, own_y, :] = dep[pl.ds(0, columns), :].reshape(bx, by, nz)
    for d in range(3):
        mf[d, own_x, own_y, :] = dep[pl.ds((1 + d) * columns, columns), :].reshape(bx, by, nz)
    start(h_solid + h_mf)
    start(h_rest)

    row = lax.broadcasted_iota(jnp.int32, (ey, nz), 0)
    depth = lax.broadcasted_iota(jnp.int32, (ey, nz), 1)
    row_in = jnp.where((row >= WY) | (iy > 0), 1.0, 0.0) * jnp.where((row < WY + by) | (iy < n_gy - 1), 1.0, 0.0)

    def voidage(x, carry):
        x_in = ((x >= WX) | (ix > 0)) & ((x < WX + bx) | (ix < n_gx - 1))
        eps[x] = jnp.maximum(1.0 - solid[x], FLOOR) * (row_in * jnp.where(x_in, 1.0, 0.0))
        return carry

    def sweep_over(act, spans, unroll):
        for first, end in spans:
            if first < end:
                lax.fori_loop(first, end, act, 0, unroll=min(2 * unroll, end - first))

    low, high = WX, WX + bx

    def up_y(v):
        return pltpu.roll(v, ey - 1, 0)

    def down_y(v):
        return pltpu.roll(v, 1, 0)

    def up_z(v):
        return pltpu.roll(v, nz - 1, 1)

    def down_z(v):
        return pltpu.roll(v, 1, 1)

    last_z, first_z = depth == nz - 1, depth == 0

    def weights(x, carry):
        e = eps[x]
        near = [eps[x + 1], eps[x - 1], up_y(e), down_y(e),
                jnp.where(last_z, 0.0, up_z(e)), jnp.where(first_z, 0.0, down_z(e))]
        total = 0.5 * (6.0 * e + (((near[0] + near[1]) + (near[2] + near[3])) + (near[4] + near[5])))
        inside = e > 0.0
        inverse = jnp.where(inside, 0.5 / jnp.where(inside, total, 1.0), 0.0)
        for n in range(6):
            w = (e + near[n]) * inverse
            if n == 4:
                w = jnp.where(last_z, 0.0, w)
            if n == 5:
                w = jnp.where(first_z, 0.0, w)
            coef[n, x] = w
        coef[6, x] = 2.0 * inverse
        recip = 1.0 / jnp.where(inside, e, 1.0)
        rate[x] = (DT * VISC) * total * recip
        pull[x] = (DT * DRAG) * recip
        return carry

    def stencil(field, x):
        v = field[x]
        return v, (((coef[0, x] * field[x + 1] + coef[1, x] * field[x - 1])
                    + (coef[2, x] * up_y(v) + coef[3, x] * down_y(v)))
                   + (coef[4, x] * up_z(v) + coef[5, x] * down_z(v)))

    def wide(b, tables):
        column, level = where_of(b)
        hot = jnp.where(column == column_of, 1.0, 0.0).astype(BF16)
        found = jnp.dot(tables, jnp.concatenate([hot, hot], axis=0), preferred_element_type=F32)
        hot_z = level == depth_of
        return [jnp.sum(jnp.where(hot_z, found[n:n + nz], 0.0), axis=0, keepdims=True)
                for n in range(0, found.shape[0], nz)]

    def table(grid):
        high, low = split(grid.reshape(columns, nz).T)
        return jnp.concatenate([high.astype(BF16), low.astype(BF16)], axis=1)

    def porosity(b, carry):
        at, = wide(b, ft[pl.ds(3 * nz, nz), :])
        pull_of[b] = rk[b, 1:2, :] * DRAG / at
        return carry

    for step in range(STEPS):
        v = (v1, v2)[step]
        pin = (pin1, pin2)[step]
        src = (src1, src2)[step]

        def predicting(parts):
            def predict(x, carry):
                s, r, g, e = solid[x], rate[x], pull[x], eps[x]
                for d in range(parts):
                    old, mean = stencil(v.at[d], x)
                    new = old + r * (mean - old) + g * (mf[d, x] - s * old)
                    if parts == 3:
                        guess[d, x] = new
                    flux[d, x] = e * new
                return carry

            return predict

        def balance(x, carry):
            f1, f2 = flux[1, x], flux[2, x]
            out = ((flux[0, x + 1] - flux[0, x - 1]) + (up_y(f1) - down_y(f1))
                   + (jnp.where(last_z, 0.0, up_z(f2)) - jnp.where(first_z, 0.0, down_z(f2))))
            src[x, own_y, :] = (0.5 / DT) * out[WY:WY + by]
            return carry

        early = h_vel[step] + (h_solid + h_mf if step == 0 else [])
        if step:
            ft[pl.ds(3 * nz, nz), :] = table(eps[own_x, own_y, :])
            lax.fori_loop(0, n_gy, porosity, 0)
        arrive(early, "y")
        if step == 0:
            sweep_over(voidage, [(low, high)], 4)
            sweep_over(weights, [(low + 1, high - 1)], 3)
        sweep_over(predicting(3), [(low + 1, high - 1)], 3)
        sweep_over(balance, [(low + near, high - near)], 4)
        start(h_far[step])
        for h in h_p[1] if step else ():
            h.pass_on(forward)
        arrive(early, "xc")
        if step == 0:
            sweep_over(voidage, [(low - 2, low), (high, high + 2)], 2)
            sweep_over(weights, [(low - 1, low + 1), (high - 1, high + 1)], 2)
        sweep_over(predicting(1), [(low - 1, low), (high, high + 1)], 1)
        sweep_over(predicting(3), [(low, low + 1), (high - 1, high)], 1)
        sweep_over(balance, [(low, low + near), (high - near, high)], 2)
        start(h_src[step])
        arrive(h_src[step], "y")
        if step == 0:
            arrive(h_rest)
            sweep_over(voidage, [(0, low), (high, ex)], 5)
            sweep_over(weights, [(1, low + 1), (high - 1, ex - 1)], 5)
            arrive(h_p[step])
        else:
            arrive(h_p[step], "y")

        def scale(x, carry):
            sp[x] = src[x] * coef[6, x]
            return carry

        stages = [pin] + [(pa, pb)[sweep % 2] for sweep in range(SWEEPS)]

        def relaxing(sweep):
            held, into = stages[sweep], stages[sweep + 1]

            def relax(x, carry):
                _, mean = stencil(held, x)
                into[x] = mean - sp[x]
                return carry

            return relax

        inset = 0 if step == 0 else 1
        sweep_over(scale, [(low, high)], 8)
        for sweep in range(SWEEPS):
            sweep_over(relaxing(sweep), [(low + sweep + inset, high - sweep - inset)], 4)
        if step:
            arrive(h_p[step], "xc")
        arrive(h_src[step], "xc")
        arrive(h_far[step])
        sweep_over(scale, [(1, low), (high, ex - 1)], 4)
        for sweep in range(SWEEPS):
            sweep_over(relaxing(sweep), [(1 + sweep, low + sweep + inset), (high - sweep - inset, ex - 1 - sweep)], 5)
        held = stages[SWEEPS]

        final = step == STEPS - 1

        def correct(x, carry):
            p = held[x]
            slopes = [held[x + 1] - held[x - 1], up_y(p) - down_y(p),
                      jnp.where(last_z, 0.0, up_z(p)) - jnp.where(first_z, 0.0, down_z(p))]
            for d in range(3):
                new = (guess[d, x] - (0.5 * DT) * slopes[d])[WY:WY + by]
                if final:
                    vel_out[d, x - WX] = new
                else:
                    v2[d, x, own_y, :] = new
            if final:
                p_out[x - WX] = p[WY:WY + by]
            else:
                for low, high in ((WY - 1, WY), (WY, WY + by), (WY + by, WY + by + 1)):
                    pin2[x, low:high, :] = p[low:high]
            return carry

        if final:
            sweep_over(correct, [(low, high)], bx)
        else:
            sweep_over(correct, [(low, low + 2), (high - 2, high)], 2)
            for h in h_vel[step + 1]:
                h.pack()
            for axis in "cx":
                send(h_vel[step + 1], axis)
            sweep_over(correct, [(low + 2, high - 2)], bx)
            send(h_vel[step + 1], "y")
            sent.extend(h_vel[step + 1])
            for x in (WX - 1, WX + bx):
                pin2[x, own_y, :] = held[x, own_y, :]
            start(h_p[step + 1])

    for d in range(3):
        ft[pl.ds(d * nz, nz), :] = table(vel_out[d])

    def gather(b, carry):
        at = wide(b, ft[pl.ds(0, 3 * nz), :])
        for d in range(3):
            dk[b, d:d + 1, :] = pull_of[b] * (at[d] - rk[b, 2 + d:3 + d, :])
        return carry

    def giving(k):
        return particles(k, dk.at[to_mate(k)], rd.at[iy], 1)

    def getting(k):
        return particles(k, dk.at[0], rd.at[from_mate(k)], 1)

    def gather_for(k, carry):
        gather(to_mate(n_gy - k), carry)
        giving(n_gy - k).start()
        return carry

    lax.fori_loop(1, n_gy, gather_for, 0, unroll=min(7, n_gy - 1))
    gather(iy, 0)
    rd[iy] = dk[iy]
    for h in sent:
        for axis in "xyc":
            h.each(axis, lambda c, _: c.wait_send())
        h.pass_on(lambda h, side: h.onward(side).wait_send())
    for k in range(1, n_gy):
        outgoing(k).wait_send()
        getting(k).wait_recv()
        giving(k).wait_send()
    for c in range(n_gy):
        for d in range(3):
            drag_out[d, pl.ds(c, 1), :] = rd[c, d:d + 1, :]


def deliver(*refs):
    pairs = len(refs) // 2
    copies = [pltpu.make_async_copy(refs[n], refs[pairs + n], refs[-1].at[n]) for n in range(pairs)]
    for copy in copies:
        copy.start()
    for copy in copies:
        copy.wait()


def solution(mesh):
    n_gx, n_gy = mesh.shape["gx"], mesh.shape["gy"]

    def per_device(velocity, pressure, part_cell, part_count, grain_velocities, part_vol):
        bx, by, nz = pressure.shape
        slots = part_vol.shape[-1]
        ext = (bx + 2 * WX, by + 2 * WY, nz)
        vmem = pl.BlockSpec(memory_space=pltpu.VMEM)
        anywhere = pl.BlockSpec(memory_space=pl.ANY)

        def field(*lead):
            return pltpu.VMEM(lead + ext, F32)

        def kernel(*refs):
            body(n_gx, n_gy, *refs)

        v, p, drag = pl.pallas_call(
            kernel,
            name="interval",
            out_shape=(
                pltpu.VMEM(velocity.shape, F32),
                pltpu.VMEM(pressure.shape, F32),
                pltpu.VMEM((3, n_gy, slots), F32),
            ),
            in_specs=[pl.BlockSpec(memory_space=pltpu.SMEM)] + [anywhere] * 5,
            out_specs=(vmem,) * 3,
            scratch_shapes=[
                pltpu.VMEM((n_gy, slots), jnp.int32),
                pltpu.VMEM((3, n_gy, slots), F32),
                pltpu.VMEM((n_gy, slots), F32),
                pltpu.SemaphoreType.DMA((7,)),
                field(3), field(3), field(), field(), field(), field(), field(), field(), field(),
                field(), field(3), field(), field(7), field(), field(), field(3), field(3),
                pltpu.VMEM((4 * bx * by, nz), F32),
                pltpu.VMEM((n_gy, ROWS, slots), F32),
                pltpu.VMEM((n_gy, ROWS, slots), F32),
                pltpu.VMEM((n_gy, 3, slots), F32),
                pltpu.VMEM((n_gy, 3, slots), F32),
                pltpu.VMEM((4 * nz, 2 * bx * by), BF16),
                pltpu.VMEM((n_gy, 1, slots), F32),
                pltpu.VMEM((16, 4, WX * (WX - 1) // 2, 1, nz), F32),
                pltpu.VMEM((16, 4, WX * (WX - 1) // 2, 1, nz), F32),
                pltpu.VMEM((1, WX, by, nz), F32),
                pltpu.SemaphoreType.DMA((2,)),
                pltpu.SemaphoreType.DMA((2,)),
                pltpu.SemaphoreType.DMA((16, 8)),
                pltpu.SemaphoreType.DMA((16, 8)),
                pltpu.SemaphoreType.DMA((2, n_gy)),
                pltpu.SemaphoreType.DMA((2, n_gy)),
            ],
            compiler_params=pltpu.CompilerParams(
                collective_id=0, has_side_effects=True, vmem_limit_bytes=56 * 1024 * 1024
            ),
        )(
            part_count.reshape(n_gy),
            velocity,
            pressure,
            part_cell.reshape(n_gy, slots),
            grain_velocities.reshape(n_gy, 3, slots).transpose(1, 0, 2),
            part_vol.reshape(n_gy, slots),
        )
        v, p, drag = [pltpu.with_memory_space_constraint(a, pltpu.VMEM) for a in (v, p, drag)]
        v, p, drag = pl.pallas_call(
            deliver,
            name="deliver",
            out_shape=tuple(jax.ShapeDtypeStruct(a.shape, F32) for a in (v, p, drag)),
            in_specs=(vmem,) * 3,
            out_specs=(anywhere,) * 3,
            scratch_shapes=[pltpu.SemaphoreType.DMA((3,))],
        )(v, p, drag)
        return v, p, drag.transpose(1, 0, 2).reshape(grain_velocities.shape)

    placed = (
        P(None, "gx", "gy", None),
        P("gx", "gy", None),
        P("gx", "gy", None, None),
        P("gx", "gy", None),
        P("gx", "gy", None, None, None),
        P("gx", "gy", None, None),
    )
    return jax.shard_map(
        per_device,
        mesh=mesh,
        in_specs=placed,
        out_specs=(P(None, "gx", "gy", None), P("gx", "gy", None), P("gx", "gy", None, None, None)),
        check_vma=False,
    )
```
